32 devices in a mesh: liq: 4 (over y, x), ill: 2 (over core), dur: 4 (over z).
Axes of the slice: x: 2, y: 2, z: 4, core: 2. Of those that a mesh axis runs over, the one named last changes fastest.
Arguments:
- marginal_value: float32 [32, 8, 4, 512], P(None, 'dur', 'ill', 'liq'), may hold values from 0.5 to 2
- transition: float32 [32, 32], replicated, may hold values from 0 to 1, as said below
- discount_shock: float32 [32], replicated, may hold values from 0.5 to 2
- illiquid_drift: float32 [4], P('ill'), may hold values from 0.2 to 0.8
- durable_keep: float32 [8], P('dur'), may hold values from 0.3 to 0.9
- bracket_index: int32 [32, 8, 4, 512], P(None, 'dur', 'ill', 'liq'), may hold values from 0 to 510
- bracket_weight: float32 [32, 8, 4, 512], P(None, 'dur', 'ill', 'liq'), may hold values from 0 to 1
- steady_consumption: float32 [32, 8, 4, 512], P(None, 'dur', 'ill', 'liq'), may hold values from 0.8 to 1.6
- lottery_weight: float32 [32, 8, 4, 512], P(None, 'dur', 'ill', 'liq'), may hold values from 0 to 1
- liquid_target: int32 [32, 8, 4, 512], P(None, 'dur', 'ill', 'liq'), may hold values from 0 to 510
- illiquid_target: int32 [32, 8, 4], P(None, 'dur', 'ill'), may hold values from 0 to 3
- population: float32 [32, 8, 4, 512], P(None, 'dur', 'ill', 'liq'), may hold values from 0.5 to 2
Outputs:
- consumption: float32 [32, 8, 4, 512], P(None, 'dur', 'ill', 'liq')
- population_next: float32 [32, 8, 4, 512], P(None, 'dur', 'ill', 'liq')
The draws below stay inside these ranges and needn't reach their ends.
Inputs may be any that keep to these rules, and one draw needn't show every extreme that they name: `bracket_index`: global liquid index; the upper bracket point is index + 1. `liquid_target`: global liquid index; the upper target is index + 1. `illiquid_target`: global illiquid index. `transition`: entries positive, every row sums to one.
All inputs are finite; a program needn't handle non-finite values.
Results may differ from the reference program's by a relative error of at most 0.000065.
Values sent between devices are 32-bit elements; how exact they have to be, the bound alone decides.
A program may use at most 64 MiB of HBM per device.

```python
import math
import jax
import jax.numpy as jnp
from jax import lax

Z = 32
NB = 512
NA = 4
ND = 8


def draw_transition(key, part):
    key_spread, key_diagonal = jax.random.split(key)
    spread = jax.random.uniform(key_spread, (Z, Z), jnp.float32, 0.2, 1.0)
    diagonal = jax.random.uniform(key_diagonal, (Z,), jnp.float32, 20.0, 30.0)
    raw_matrix = spread + jnp.diag(diagonal)
    return raw_matrix / jnp.sum(raw_matrix, axis=1, keepdims=True)


def place_ends(array, stream_key, low, top_value):
    extent = array.shape
    index_at = [jax.random.randint(jax.random.fold_in(stream_key, axis), (), 0, extent[axis]) for axis in range(len(extent))]
    array = array.at[tuple(index_at)].set(low)
    longest = extent.index(max(extent))
    index_at[longest] = (index_at[longest] + 1) % extent[longest]
    return array.at[tuple(index_at)].set(top_value)


def block_levels(stream_key, dims, pieces, least, high):
    level, own = 1.0, jax.random.fold_in(stream_key, 6)
    for position, shards_of in pieces:
        heights = jnp.exp(jax.random.uniform(jax.random.fold_in(own, position), (shards_of,), jnp.float32, least / len(pieces), high / len(pieces)))
        level = level * jnp.repeat(heights, dims[position] // shards_of).reshape([-1 if axis == position else 1 for axis in range(len(dims))])
    return level


def setup_inputs(seed: int = 0) -> dict:
    key_list = jax.random.split(jax.random.key(seed), 13)
    return {
        "marginal_value": jnp.clip(jnp.exp(math.log(2.0) - 1.3862944 * jax.random.uniform(key_list[0], (Z, ND, NA, NB), jnp.float32) ** block_levels(key_list[0], (Z, ND, NA, NB), ((1, 4), (2, 2), (3, 4)), -0.2, 0.2)), 0.5, 2.0),
        "transition": draw_transition(jax.random.fold_in(key_list[12], 71), 0),
        "discount_shock": jnp.clip(jnp.exp(jax.random.uniform(key_list[2], (Z,), jnp.float32, math.log(0.5), math.log(2.0))), 0.5, 2.0),
        "illiquid_drift": jnp.clip(0.2 + 0.6 * jax.random.uniform(key_list[3], (NA,), jnp.float32) ** block_levels(key_list[3], (NA,), ((0, 2),), -0.2, 0.2), 0.2, 0.8),
        "durable_keep": jnp.clip(0.3 + 0.59999996 * jax.random.uniform(key_list[4], (ND,), jnp.float32) ** block_levels(key_list[4], (ND,), ((0, 4),), -0.2, 0.2), 0.3, 0.9),
        "bracket_index": place_ends(jax.random.randint(key_list[5], (Z, ND, NA, NB), 0, NB - 1), jax.random.fold_in(key_list[5], 1), 0, (NB - 1) - 1).astype(jnp.int32),
        "bracket_weight": jnp.clip(1.0 * jax.random.uniform(key_list[6], (Z, ND, NA, NB), jnp.float32) ** block_levels(key_list[6], (Z, ND, NA, NB), ((1, 4), (2, 2), (3, 4)), -0.2, 0.2), 0.0, 1.0),
        "steady_consumption": jnp.clip(0.8 + 0.8 * jax.random.uniform(key_list[7], (Z, ND, NA, NB), jnp.float32) ** block_levels(key_list[7], (Z, ND, NA, NB), ((1, 4), (2, 2), (3, 4)), -0.2, 0.2), 0.8, 1.6),
        "lottery_weight": jnp.clip(1.0 * jax.random.uniform(key_list[8], (Z, ND, NA, NB), jnp.float32) ** block_levels(key_list[8], (Z, ND, NA, NB), ((1, 4), (2, 2), (3, 4)), -0.2, 0.2), 0.0, 1.0),
        "liquid_target": place_ends(jax.random.randint(key_list[9], (Z, ND, NA, NB), 0, NB - 1), jax.random.fold_in(key_list[9], 1), 0, (NB - 1) - 1).astype(jnp.int32),
        "illiquid_target": place_ends(jax.random.randint(key_list[10], (Z, ND, NA), 0, NA), jax.random.fold_in(key_list[10], 1), 0, NA - 1).astype(jnp.int32),
        "population": jnp.clip(jnp.exp(math.log(2.0) - 1.3862944 * jax.random.uniform(key_list[11], (Z, ND, NA, NB), jnp.float32) ** block_levels(key_list[11], (Z, ND, NA, NB), ((1, 4), (2, 2), (3, 4)), -0.2, 0.2)), 0.5, 2.0),
    }


DISCOUNT = 0.96
GROSS_RATE = 1.01
SLOPE_GAIN = 0.5
HIGHEST_PREC = lax.Precision.HIGHEST

def expect_upper(values, transition, drift_rate):
    expected = jnp.einsum('zy,ydab->zdab', transition, values, precision=HIGHEST_PREC)
    upper_plane = jnp.concatenate([expected[:, :, 1:, :], expected[:, :, -1:, :]], axis=2)
    drift_full = drift_rate[None, None, :, None]
    return drift_full * expected + (1.0 - drift_full) * upper_plane

def backward_step(values, transition, drift_rate, shock_scale, bracket_index, bracket_weight):
    drifted = expect_upper(values, transition, drift_rate)
    endogenous = lax.rsqrt(DISCOUNT * GROSS_RATE * shock_scale[:, None, None, None] * drifted)
    lower_value = jnp.take_along_axis(endogenous, bracket_index, axis=3)
    upper_value = jnp.take_along_axis(endogenous, bracket_index + 1, axis=3)
    return bracket_weight * lower_value + (1.0 - bracket_weight) * upper_value

def reference(marginal_value, transition, discount_shock, illiquid_drift, durable_keep, bracket_index, bracket_weight, steady_consumption, lottery_weight, liquid_target, illiquid_target, population):
    policy_one = backward_step(marginal_value, transition, illiquid_drift, discount_shock, bracket_index, bracket_weight)
    value_two = GROSS_RATE / (policy_one * policy_one)
    consumption = backward_step(value_two, transition, illiquid_drift, jnp.ones_like(discount_shock), bracket_index, bracket_weight)
    share = jnp.clip(lottery_weight + SLOPE_GAIN * (policy_one - steady_consumption), 0.0, 1.0)
    incomes, durables, ill_count, liq_count = population.shape
    inc_idx = lax.broadcasted_iota(jnp.int32, population.shape, 0)
    dur_idx = lax.broadcasted_iota(jnp.int32, population.shape, 1)
    ill_dest = jnp.broadcast_to(illiquid_target[:, :, :, None], population.shape).astype(jnp.int32)
    base_index = ((inc_idx * durables + dur_idx) * ill_count + ill_dest) * liq_count
    flat_mass = jnp.zeros((incomes * durables * ill_count * liq_count,), jnp.float32)
    flat_mass = flat_mass.at[(base_index + liquid_target).reshape(-1)].add((population * share).reshape(-1))
    flat_mass = flat_mass.at[(base_index + liquid_target + 1).reshape(-1)].add((population * (1.0 - share)).reshape(-1))
    lottery_mass = flat_mass.reshape(population.shape)
    dur_plane = lax.broadcasted_iota(jnp.int32, (durables,), 0)
    stay_share = jnp.where(dur_plane == 0, 1.0, durable_keep)[None, :, None, None]
    depart = (1.0 - stay_share) * lottery_mass
    settled = stay_share * lottery_mass + jnp.concatenate([depart[:, 1:], jnp.zeros_like(depart[:, :1])], axis=1)
    population_next = jnp.einsum('zy,zdab->ydab', transition, settled, precision=HIGHEST_PREC)
    return (consumption, population_next)
```

```python
import contextlib
import functools

import jax
import jax.numpy as jnp
from jax import lax
from jax.experimental import pallas as pl
from jax.experimental.pallas import tpu as pltpu
from jax.sharding import PartitionSpec as P

DISCOUNT = 0.96
GROSS_RATE = 1.01
SLOPE_GAIN = 0.5
HIGHEST_PREC = lax.Precision.HIGHEST
MESH_ID = pl.DeviceIdType.MESH
NT = (((1,), (1,)), ((), ()))
TILE = 8


def scope(name):
    return contextlib.nullcontext()


def split_by(x, n):
    if n & (n - 1) == 0:
        return x >> (n.bit_length() - 1), x & (n - 1)
    return lax.div(x, jnp.int32(n)), lax.rem(x, jnp.int32(n))


def dot(a, b):
    return jnp.dot(a, b, precision=HIGHEST_PREC, preferred_element_type=jnp.float32)


def iota(shape, axis):
    return lax.broadcasted_iota(jnp.int32, shape, axis)


def as_float(flag):
    return jnp.where(flag, jnp.float32(1.0), jnp.float32(0.0))


def peer_of(me, step, n):
    if n & (n - 1):
        return lax.rem(me + step, n)
    out = me
    for bit in range(n.bit_length() - 1):
        if step >> bit & 1:
            out = out + (1 - 2 * lax.rem(lax.div(me, jnp.int32(1 << bit)), jnp.int32(2))) * (1 << bit)
    return out


def kernel(
    dims,
    value_hbm, transition_hbm, shock_hbm, drift_hbm, keep_hbm, index_hbm, weight_hbm,
    steady_hbm, lottery_hbm, target_hbm, ill_target_hbm, population_hbm,
    consumption_ref, next_ref,
    value_ref, transition_ref, shock_ref, index_ref, weight_ref, steady_ref, lottery_ref, target_ref,
    population_ref, drift_ref, keep_ref, ill_target_ref, load_sem,
    first_mat, first_up, second_mat, second_up, next_mat, next_in,
    near_value, value_two, pencil, mass_low, mass_high, target_hi, target_lo,
    placed_rows, terms, terms_in, owner_sum, owner_in, settled, depart, depart_in,
    value_send, value_recv, pencil_send, pencil_recv, terms_send, terms_recv,
    owner_send, owner_recv, depart_send, depart_recv,
):
    incomes, durables, ill_rows, liq_rows, liq_n, ill_n, dur_n = dims
    group = durables * ill_rows
    rows = incomes * group
    half_rows = rows // 2
    plane_rows = incomes * ill_rows
    liq_me, ill_me, dur_me = (lax.axis_index(name) for name in ("liq", "ill", "dur"))
    far_first = range(liq_n - 1, 0, -1)

    barrier = pltpu.get_barrier_semaphore()
    for step in far_first:
        pl.semaphore_signal(barrier, inc=1, device_id={"liq": peer_of(liq_me, step, liq_n)}, device_id_type=MESH_ID)
    for step in range(1, ill_n):
        pl.semaphore_signal(barrier, inc=1, device_id={"ill": peer_of(ill_me, step, ill_n)}, device_id_type=MESH_ID)

    @pl.when(dur_me > 0)
    def _():
        pl.semaphore_signal(barrier, inc=1, device_id={"dur": dur_me - 1}, device_id_type=MESH_ID)

    @pl.when(dur_me < dur_n - 1)
    def _():
        pl.semaphore_signal(barrier, inc=1, device_id={"dur": dur_me + 1}, device_id_type=MESH_ID)

    loads = [
        pltpu.make_async_copy(source, held, load_sem.at[slot])
        for slot, (source, held) in enumerate((
            (transition_hbm, transition_ref), (shock_hbm, shock_ref), (drift_hbm, drift_ref), (value_hbm, value_ref),
            (keep_hbm, keep_ref), (ill_target_hbm, ill_target_ref),
            (index_hbm, index_ref), (weight_hbm, weight_ref), (target_hbm, target_ref),
            (lottery_hbm, lottery_ref), (steady_hbm, steady_ref), (population_hbm, population_ref),
        ))
    ]
    for load in loads:
        load.start()
    for load in loads[:3]:
        load.wait()

    transition = transition_ref[...]
    row_z, row_rest = split_by(iota((rows, rows), 0), group)
    col_z, col_rest = split_by(iota((rows, rows), 1), group)
    row_d, row_a = split_by(row_rest, ill_rows)
    col_d, col_a = split_by(col_rest, ill_rows)
    spread = as_float(split_by(iota((rows, incomes), 0), group)[0] == iota((rows, incomes), 1))
    spread_t = as_float(iota((incomes, rows), 0) == split_by(iota((incomes, rows), 1), group)[0])
    drift = jnp.zeros((rows, rows), jnp.float32)
    for a in range(ill_rows):
        drift = jnp.where(row_a == a, drift_ref[a], drift)
    is_last = as_float(ill_me == ill_n - 1)
    same_d = row_d == col_d
    top_row = row_a == ill_rows - 1
    local = jnp.where(col_a == row_a, drift, 0.0)
    local = local + jnp.where(col_a == row_a + 1, 1.0 - drift, 0.0)
    local = local + jnp.where(top_row & (col_a == ill_rows - 1), is_last * (1.0 - drift), 0.0)
    local = jnp.where(same_d, local, 0.0)
    upper = jnp.where(same_d & top_row & (col_a == 0), (1.0 - is_last) * (1.0 - drift), 0.0)
    constant = jnp.float32(DISCOUNT * GROSS_RATE)
    eye = iota((incomes, incomes), 0) == iota((incomes, incomes), 1)
    scaled = dot(jnp.where(eye, constant * shock_ref[...], 0.0), transition)
    wide = dot(dot(spread, scaled), spread_t)
    first_mat[...] = wide * local
    first_up[...] = wide * upper

    dur_peers = jnp.minimum(dur_me, 1) + jnp.minimum(dur_n - 1 - dur_me, 1)
    pl.semaphore_wait(barrier, liq_n - 1 + ill_n - 1 + dur_peers)

    ill_below = lax.rem(ill_me + ill_n - 1, ill_n)

    def value_copy(k, source):
        return pltpu.make_async_remote_copy(
            src_ref=source, dst_ref=near_value.at[k], send_sem=value_send.at[k],
            recv_sem=value_recv.at[k], device_id={"ill": ill_below}, device_id_type=MESH_ID,
        )

    def pencil_copy(k, half, step):
        slot = (k * 2 + half) * liq_n + step
        part = pencil.at[k * liq_n + liq_me, pl.ds(half * half_rows, half_rows)]
        return pltpu.make_async_remote_copy(
            src_ref=part, dst_ref=part, send_sem=pencil_send.at[slot], recv_sem=pencil_recv.at[slot],
            device_id={"liq": peer_of(liq_me, step, liq_n)}, device_id_type=MESH_ID,
        )

    def pencil_relay(half):
        near, far = (1, 2) if half == 0 else (2, 1)
        slot = (2 + half) * liq_n
        part = pencil.at[liq_n + peer_of(liq_me, near, liq_n), pl.ds(half * half_rows, half_rows)]
        return pltpu.make_async_remote_copy(
            src_ref=part, dst_ref=part, send_sem=pencil_send.at[slot], recv_sem=pencil_recv.at[slot],
            device_id={"liq": peer_of(liq_me, far, liq_n)}, device_id_type=MESH_ID,
        )

    relayed = liq_n == 4
    if relayed:
        early, late = [(0, 1), (1, 2)], [(1, 1), (0, 2)]
    else:
        early, late = [(0, step) for step in far_first], [(1, step) for step in far_first]

    def terms_copy(d, step):
        peer = peer_of(ill_me, step, ill_n)
        slot = d * (ill_n - 1) + step - 1
        return pltpu.make_async_remote_copy(
            src_ref=terms.at[pl.ds((d * ill_n + peer) * (liq_n * plane_rows), liq_n * plane_rows)],
            dst_ref=terms_in.at[slot], send_sem=terms_send.at[slot], recv_sem=terms_recv.at[slot],
            device_id={"ill": peer}, device_id_type=MESH_ID,
        )

    def owner_copy(d, step):
        peer = peer_of(liq_me, step, liq_n)
        slot = d * (liq_n - 1) + step - 1
        return pltpu.make_async_remote_copy(
            src_ref=owner_sum.at[d * liq_n + peer], dst_ref=owner_in.at[slot],
            send_sem=owner_send.at[slot], recv_sem=owner_recv.at[slot],
            device_id={"liq": peer}, device_id_type=MESH_ID,
        )

    loads[3].wait()
    value_copy(0, value_ref).start()
    drifted = dot(first_mat[...], value_ref[...])
    value_copy(0, value_ref).wait_recv()
    drifted = drifted + dot(first_up[...], near_value[0])
    pencil[liq_me] = lax.rsqrt(drifted)
    for half in range(2):
        for step in far_first:
            pencil_copy(0, half, step).start()

    wide = constant * dot(dot(spread, transition), spread_t)
    second_mat[...] = wide * local
    second_up[...] = wide * upper

    for load in loads[4:]:
        load.wait()

    first_d = as_float(dur_me == 0)
    stay = [keep_ref[d] for d in range(durables)]
    stay[0] = first_d + (1.0 - first_d) * stay[0]
    back_d, back_rest = split_by(iota((rows, rows), 1), plane_rows)
    back_a = split_by(back_rest, ill_rows)[1]
    stays = jnp.zeros((rows, rows), jnp.float32)
    for d in range(durables):
        stays = jnp.where(back_d == d, stay[d], stays)
    mix = jnp.where(back_d == row_d, stays, 0.0) + jnp.where(back_d == row_d + 1, 1.0 - stays, 0.0)
    mix = jnp.where(back_a == row_a, mix, 0.0)
    back_z = split_by(split_by(iota((incomes, rows), 1), plane_rows)[1], ill_rows)[0]
    turned = lax.dot_general(spread, transition, NT, precision=HIGHEST_PREC, preferred_element_type=jnp.float32)
    wide = dot(turned, as_float(iota((incomes, rows), 0) == back_z))
    next_mat[...] = wide * mix
    in_z, in_a = split_by(iota((incomes, plane_rows), 1), ill_rows)
    wide = dot(turned, as_float(iota((incomes, plane_rows), 0) == in_z))
    in_row = split_by(iota((rows, plane_rows), 0), group)[1]
    in_row_d, in_row_a = split_by(in_row, ill_rows)
    in_col_a = split_by(iota((rows, plane_rows), 1), ill_rows)[1]
    next_in[...] = jnp.where((in_row_d == durables - 1) & (in_row_a == in_col_a), wide, 0.0)

    def block_of(position):
        block = jnp.zeros(position.shape, jnp.int32)
        for h in range(1, liq_n):
            block = block + jnp.where(position >= h * liq_rows, 1, 0)
        return block, position - block * liq_rows

    target_hi[...], lo = block_of(target_ref[...])
    target_lo[...] = lo.astype(jnp.float32)

    def interpolate(k, tile):
        span = pl.ds(tile * TILE, TILE)
        index = index_ref[span, :]
        low_block, low_lane = block_of(index)
        high_block, high_lane = block_of(index + 1)
        low = high = None
        for h in range(liq_n):
            block = pencil[k * liq_n + h, span, :]
            low_h = jnp.take_along_axis(block, low_lane, axis=1, mode="promise_in_bounds")
            high_h = jnp.take_along_axis(block, high_lane, axis=1, mode="promise_in_bounds")
            low = low_h if h == 0 else jnp.where(low_block == h, low_h, low)
            high = high_h if h == 0 else jnp.where(high_block == h, high_h, high)
        weight = weight_ref[span, :]
        return weight * low + (1.0 - weight) * high

    tiles = rows // TILE
    halves = (range(tiles // 2), range(tiles // 2, tiles))

    def first_policy(half):
        for step in far_first:
            pencil_copy(0, half, step).wait_recv()
        for tile in halves[half]:
            span = pl.ds(tile * TILE, TILE)
            chosen = interpolate(0, tile)
            value_two[span, :] = GROSS_RATE / (chosen * chosen)
            share = jnp.clip(lottery_ref[span, :] + SLOPE_GAIN * (chosen - steady_ref[span, :]), 0.0, 1.0)
            mass = population_ref[span, :]
            mass_low[span, :] = mass * share
            mass_high[span, :] = mass * (1.0 - share)

    lanes = 2 * liq_n
    sub = iota((lanes, liq_rows), 0)
    lane_at = iota((TILE, liq_rows), 1)
    sub_block = jnp.where(sub < liq_n, sub, sub - liq_n)
    lane_row = iota((liq_rows, liq_rows), 0).astype(jnp.float32).astype(jnp.bfloat16)
    one = jnp.ones((liq_rows, liq_rows), jnp.bfloat16)
    nil = jnp.zeros((liq_rows, liq_rows), jnp.bfloat16)
    per_tile = TILE // group

    def scatter_tile(d, tile):
        span = pl.ds(pl.multiple_of(tile * TILE, TILE), TILE)
        low_t, high_t, hi_t, lo_t = mass_low[span, :], mass_high[span, :], target_hi[span, :], target_lo[span, :]
        for zz in range(per_tile):
            z = tile * per_tile + zz
            totals = []
            for a in range(ill_rows):
                k = zz * group + d * ill_rows + a
                both = jnp.where(sub < liq_n, low_t[k : k + 1, :], high_t[k : k + 1, :])
                both = jnp.where(hi_t[k : k + 1, :] == sub_block, both, 0.0)
                rounded = both.astype(jnp.bfloat16).astype(jnp.float32)
                parts = jnp.concatenate([both, both - rounded], axis=0).astype(jnp.bfloat16)
                place = jnp.broadcast_to(lo_t[k : k + 1, :], (2 * TILE, liq_rows)).astype(jnp.bfloat16)
                place = jnp.concatenate([place] * (liq_rows // (2 * TILE)), axis=0)
                hot = jnp.where(lane_row == place, one, nil)
                placed = lax.dot_general(parts, hot, NT, preferred_element_type=jnp.float32)
                placed = placed[:lanes] + placed[lanes:]
                totals.append(placed)
            for dest in range(ill_n * ill_rows):
                out = None
                for a in range(ill_rows):
                    here = as_float(ill_target_ref[d * ill_rows + a, z] == dest) * totals[a]
                    out = here if out is None else out + here
                base = dest // ill_rows * lanes * plane_rows + z * ill_rows + dest % ill_rows
                placed_rows[pl.ds(base, lanes, stride=plane_rows), :] = out

    unroll = tiles // 2

    def scatter(d, half):
        def step(pair, carry):
            for turn in range(unroll):
                scatter_tile(d, halves[half].start + unroll * pair + turn)
            return carry

        lax.fori_loop(0, tiles // 2 // unroll, step, 0)

    def send_terms(d):
        for owner in range(ill_n):
            for piece in range(plane_rows // TILE):
                carried = None
                for h in range(liq_n):
                    low_at = (owner * lanes + h) * plane_rows + piece * TILE
                    low = placed_rows[pl.ds(low_at, TILE), :]
                    moved = pltpu.roll(placed_rows[pl.ds(low_at + liq_n * plane_rows, TILE), :], 1, 1)
                    edge = jnp.where(lane_at > 0, moved, 0.0 if carried is None else carried)
                    carried = moved
                    out_at = ((d * ill_n + owner) * liq_n + h) * plane_rows + piece * TILE
                    terms[pl.ds(out_at, TILE), :] = low + edge
        for step in range(1, ill_n):
            terms_copy(d, step).start()

    def send_owners(d):
        for step in range(1, ill_n):
            terms_copy(d, step).wait_recv()
        for h in range(liq_n):
            start = pl.multiple_of(((d * ill_n + ill_me) * liq_n + h) * plane_rows, TILE)
            total = terms[pl.ds(start, plane_rows), :]
            for step in range(1, ill_n):
                total = total + terms_in[d * (ill_n - 1) + step - 1, pl.ds(h * plane_rows, plane_rows), :]
            owner_sum[d * liq_n + h] = total
        for step in far_first:
            owner_copy(d, step).start()

    def collect(d):
        for step in far_first:
            owner_copy(d, step).wait_recv()
        total = owner_sum[d * liq_n + liq_me]
        for step in range(1, liq_n):
            total = total + owner_in[d * (liq_n - 1) + step - 1]
        settled[pl.ds(d * plane_rows, plane_rows), :] = total
        return total

    def second_policy():
        if relayed:
            for half in range(2):
                pencil_relay(half).wait_recv()
        else:
            for half, step in early:
                pencil_copy(1, half, step).wait_recv()
        for half, step in late:
            pencil_copy(1, half, step).wait_recv()
        for tile in range(tiles):
            consumption_ref[pl.ds(tile * TILE, TILE), :] = interpolate(1, tile)

    first_policy(0)
    scatter(0, 0)
    first_policy(1)
    value_copy(1, value_two).start()
    scatter(0, 1)
    send_terms(0)
    value_copy(1, value_two).wait_recv()
    drifted = dot(second_mat[...], value_two[...]) + dot(second_up[...], near_value[1])
    pencil[liq_n + liq_me] = lax.rsqrt(drifted)
    for half, step in early:
        pencil_copy(1, half, step).start()
    for d in range(1, durables):
        scatter(d, 0)
        if d == 1:
            send_owners(0)
            for half, step in late:
                pencil_copy(1, half, step).start()
        scatter(d, 1)
        send_terms(d)
    for d in range(1, durables):
        send_owners(d)
    if relayed:
        for half, step in early:
            pencil_copy(1, half, step).wait_recv()
        for half in range(2):
            pencil_relay(half).start()

    depart_copy = pltpu.make_async_remote_copy(
        src_ref=depart, dst_ref=depart_in, send_sem=depart_send.at[0], recv_sem=depart_recv.at[0],
        device_id={"dur": jnp.maximum(dur_me - 1, 0)}, device_id_type=MESH_ID,
    )

    depart[...] = (1.0 - stay[0]) * collect(0)

    @pl.when(dur_me > 0)
    def _():
        depart_copy.start()

    for d in range(1, durables):
        collect(d)
    next_ref[...] = dot(next_mat[...], settled[...])
    second_policy()

    @pl.when(dur_me < dur_n - 1)
    def _():
        depart_copy.wait_recv()
        next_ref[...] += dot(next_in[...], depart_in[...])

    value_copy(0, value_ref).wait_send()
    value_copy(1, value_two).wait_send()
    for step in range(1, liq_n):
        for half in range(2):
            pencil_copy(0, half, step).wait_send()
        for d in range(durables):
            owner_copy(d, step).wait_send()
    for half, step in early + late:
        pencil_copy(1, half, step).wait_send()
    if relayed:
        for half in range(2):
            pencil_relay(half).wait_send()
    for step in range(1, ill_n):
        for d in range(durables):
            terms_copy(d, step).wait_send()

    @pl.when(dur_me > 0)
    def _():
        depart_copy.wait_send()


def halves_of(x):
    high = x.astype(jnp.bfloat16)
    return high, (x - high.astype(jnp.float32)).astype(jnp.bfloat16)


def stack_data(x):
    high, low = halves_of(x)
    return jnp.concatenate([high, low, high], axis=0)


def transposed_kernel(
    dims,
    value_hbm, transition_hbm, shock_hbm, drift_hbm, keep_hbm, index_hbm, weight_hbm,
    steady_hbm, lottery_hbm, target_hbm, ill_target_hbm, population_hbm,
    consumption_ref, next_ref,
    value_ref, transition_ref, shock_ref, index_ref, weight_ref, steady_ref, lottery_ref, target_ref,
    population_ref, ill_target_ref, drift_ref, keep_ref, load_sem,
    near_out, near_in, late_out, late_in, side_out, side_in,
    pencil_one, value_two, values_in, pencil_two, placed, mass_out, depart_out, mass_in,
    near_send, near_recv, late_send, late_recv, side_send, side_recv,
    value_send, value_recv, plane_send, plane_recv, mass_send, mass_recv, depart_send, depart_recv, ready_sem,
):
    incomes, durables, ill_rows, liq_rows, liq_n, ill_n, dur_n = dims
    group = durables * ill_rows
    ill_all = ill_n * ill_rows
    part = incomes // liq_n
    per_dest = 3 * ill_rows
    grid_tiles = ill_rows * liq_n
    planes = (ill_rows + 1) * liq_n
    constant = jnp.float32(DISCOUNT * GROSS_RATE)
    f32 = jnp.float32
    liq_me, ill_me, dur_me = (lax.axis_index(name) for name in ("liq", "ill", "dur"))
    peers = [(step, flip) for step in range(liq_n - 1, -1, -1) for flip in range(ill_n) if step or flip]

    def at(step, flip):
        return {"liq": peer_of(liq_me, step, liq_n), "ill": peer_of(ill_me, flip, ill_n)}

    def slot_of(step, flip):
        return flip * liq_n + step

    barrier = pltpu.get_barrier_semaphore()
    for step, flip in peers:
        pl.semaphore_signal(barrier, inc=1, device_id=at(step, flip), device_id_type=MESH_ID)

    @pl.when(dur_me > 0)
    def _():
        pl.semaphore_signal(barrier, inc=1, device_id={"dur": dur_me - 1}, device_id_type=MESH_ID)

    @pl.when(dur_me < dur_n - 1)
    def _():
        pl.semaphore_signal(barrier, inc=1, device_id={"dur": dur_me + 1}, device_id_type=MESH_ID)

    loads = [
        pltpu.make_async_copy(source, held, load_sem.at[slot])
        for slot, (source, held) in enumerate((
            (transition_hbm, transition_ref), (shock_hbm, shock_ref), (value_hbm, value_ref),
            (index_hbm, index_ref), (weight_hbm, weight_ref), (drift_hbm, drift_ref), (ill_target_hbm, ill_target_ref),
            (target_hbm, target_ref), (lottery_hbm, lottery_ref), (steady_hbm, steady_ref),
            (population_hbm, population_ref), (keep_hbm, keep_ref),
        ))
    ]
    for load in loads:
        load.start()

    def rows_at(d, a, z_part):
        return pl.ds(z_part * part * group + d * ill_rows + a, part, stride=group)

    def whole_rows(d, a):
        return pl.ds(d * ill_rows + a, incomes, stride=group)

    kinds = [(d, a) for d in range(durables) for a in range(ill_rows)]
    for load in loads[:2]:
        load.wait()
    transition = transition_ref[...]
    eye = iota((incomes, incomes), 0) == iota((incomes, incomes), 1)
    scaled = dot(jnp.where(eye, constant * shock_ref[...], 0.0), transition)

    def stack_left(x):
        high, low = halves_of(x)
        return jnp.concatenate([high, high, low], axis=1)

    def times(left, x):
        return jnp.dot(left, stack_data(x), preferred_element_type=f32)

    left_one = stack_left(scaled)
    left_two = stack_left(constant * transition)
    loads[2].wait()
    wide = jnp.concatenate([value_ref[whole_rows(d, a), :] for d, a in kinds], axis=1)
    wide = times(left_one, wide)
    for load in loads[3:5]:
        load.wait()
    for k, (d, a) in enumerate(kinds):
        for q in range(liq_n):
            base = (d * liq_n + q) * per_dest
            near_out[base + a] = wide[q * part : (q + 1) * part, k * liq_rows : (k + 1) * liq_rows]
            near_out[base + ill_rows + a] = index_ref[rows_at(d, a, q), :].astype(f32)
            near_out[base + 2 * ill_rows + a] = weight_ref[rows_at(d, a, q), :]

    for load in loads[5:7]:
        load.wait()
    column = iota((part, incomes), 1)
    wanted = column == liq_me * part + iota((part, incomes), 0)
    picked = jnp.concatenate(
        [
            jnp.where(wanted, jnp.broadcast_to(ill_target_ref[k : k + 1, :], (part, incomes)), 0)
            for k in range(group)
        ],
        axis=0,
    )
    spread = jnp.dot(
        picked.astype(f32).astype(jnp.bfloat16), jnp.ones((incomes, liq_rows), jnp.bfloat16), preferred_element_type=f32
    )
    row = iota((TILE, liq_rows), 0)
    drifts = jnp.zeros((TILE, liq_rows), f32)
    for a in range(ill_rows):
        drifts = jnp.where(row == a, drift_ref[a], drifts)
    for k, (d, a) in enumerate(kinds):
        side_out[d, a] = spread[k * part : (k + 1) * part]
    for d in range(durables):
        side_out[d, ill_rows] = drifts

    with scope("bar"):
        dur_peers = jnp.minimum(dur_me, 1) + jnp.minimum(dur_n - 1 - dur_me, 1)
        pl.semaphore_wait(barrier, len(peers) + dur_peers)

    @pl.when((dur_me < dur_n - 1) & (ill_me == 0))
    def _():
        pl.semaphore_signal(ready_sem, inc=1, device_id={"dur": dur_me + 1}, device_id_type=MESH_ID)

    def bundle_copy(out_ref, in_ref, send, recv, step, flip):
        there = at(step, flip)
        return pltpu.make_async_remote_copy(
            src_ref=out_ref.at[pl.ds((there["ill"] * liq_n + there["liq"]) * per_dest, per_dest)],
            dst_ref=in_ref.at[pl.ds((liq_me * ill_n + ill_me) * per_dest, per_dest)],
            send_sem=send.at[slot_of(step, flip)], recv_sem=recv.at[slot_of(step, flip)],
            device_id=there, device_id_type=MESH_ID,
        )

    def near_copy(step, flip):
        return bundle_copy(near_out, near_in, near_send, near_recv, step, flip)

    def late_copy(step, flip):
        return bundle_copy(late_out, late_in, late_send, late_recv, step, flip)

    def side_copy(flip):
        there = at(0, flip)
        return pltpu.make_async_remote_copy(
            src_ref=side_out.at[there["ill"]], dst_ref=side_in.at[ill_me],
            send_sem=side_send.at[flip], recv_sem=side_recv.at[flip], device_id=there, device_id_type=MESH_ID,
        )

    for step, flip in peers:
        near_copy(step, flip).start()
    for flip in range(1, ill_n):
        side_copy(flip).start()

    for load in loads[7:]:
        load.wait()
    for d, a in kinds:
        for q in range(liq_n):
            base = (d * liq_n + q) * per_dest
            span = rows_at(d, a, q)
            late_out[base + a] = lottery_ref[span, :] - SLOPE_GAIN * steady_ref[span, :]
            late_out[base + ill_rows + a] = population_ref[span, :]
            late_out[base + 2 * ill_rows + a] = target_ref[span, :].astype(f32)
    for step, flip in peers:
        late_copy(step, flip).start()

    own_out = (ill_me * liq_n + liq_me) * per_dest
    own_in = (liq_me * ill_n + ill_me) * per_dest
    for k in range(per_dest):
        near_in[own_in + k] = near_out[own_out + k]
        late_in[own_in + k] = late_out[own_out + k]
    for k in range(ill_rows + 1):
        side_in[ill_me, k] = side_out[ill_me, k]

    @pl.when(ill_me == ill_n - 1)
    def _():
        for d in range(durables):
            for h in range(liq_n):
                values_in[d * planes + grid_tiles + h] = jnp.zeros((incomes, liq_rows), f32)

    @pl.when(dur_me == dur_n - 1)
    def _():
        for a in range(ill_rows):
            mass_in[group + a] = jnp.zeros((incomes, liq_rows), f32)

    stay = [keep_ref[d] for d in range(durables)]
    first_d = as_float(dur_me == 0)
    stay[0] = first_d + (1.0 - first_d) * stay[0]

    def received(ref, kind, h, ag):
        return ref[(h * ill_n + ag // ill_rows) * per_dest + kind * ill_rows + ag % ill_rows]

    def interpolate(blocks, index, weight):
        index = index.astype(jnp.int32)
        low_block, low_lane = split_by(index, liq_rows)
        high_block, high_lane = split_by(index + 1, liq_rows)
        low = high = None
        for h, block in enumerate(blocks):
            low_h = jnp.take_along_axis(block, low_lane, axis=1, mode="promise_in_bounds")
            high_h = jnp.take_along_axis(block, high_lane, axis=1, mode="promise_in_bounds")
            low = low_h if h == 0 else jnp.where(low_block == h, low_h, low)
            high = high_h if h == 0 else jnp.where(high_block == h, high_h, high)
        return weight * low + (1.0 - weight) * high

    def main_copy(i, step):
        flip = lax.rem(i - ill_me + ill_n, ill_n)
        return pltpu.make_async_remote_copy(
            src_ref=value_two.at[pl.ds(i * grid_tiles, grid_tiles)],
            dst_ref=values_in.at[pl.ds(ill_me * planes, grid_tiles), pl.ds(pl.multiple_of(liq_me * part, TILE), part)],
            send_sem=value_send.at[i * liq_n + step], recv_sem=value_recv.at[flip * liq_n + step],
            device_id={"liq": peer_of(liq_me, step, liq_n), "ill": i}, device_id_type=MESH_ID,
        )

    def plane_copy(i, step):
        flip = lax.rem(i - ill_me + ill_n, ill_n)
        return pltpu.make_async_remote_copy(
            src_ref=value_two.at[pl.ds((i + 1) * grid_tiles, liq_n)],
            dst_ref=values_in.at[
                pl.ds(ill_me * planes + grid_tiles, liq_n), pl.ds(pl.multiple_of(liq_me * part, TILE), part)
            ],
            send_sem=plane_send.at[i * liq_n + step], recv_sem=plane_recv.at[flip * liq_n + step],
            device_id={"liq": peer_of(liq_me, step, liq_n), "ill": i}, device_id_type=MESH_ID,
        )

    own_z = pl.ds(pl.multiple_of(liq_me * part, TILE), part)

    def send_values(i):
        for step in range(liq_n - 1, 0, -1):
            main_copy(i, step).start()

        @pl.when(ill_me != i)
        def _():
            main_copy(i, 0).start()

        @pl.when(ill_me == i)
        def _():
            for k in range(grid_tiles):
                values_in[i * planes + k, own_z, :] = value_two[i * grid_tiles + k]

    def send_plane(i):
        for step in range(liq_n - 1, 0, -1):
            plane_copy(i, step).start()

        @pl.when(ill_me != i)
        def _():
            plane_copy(i, 0).start()

        @pl.when(ill_me == i)
        def _():
            for k in range(liq_n):
                values_in[i * planes + grid_tiles + k, own_z, :] = value_two[(i + 1) * grid_tiles + k]

    with scope("near"):
        for flip in range(1, ill_n):
            side_copy(flip).wait_recv()
        for step, flip in peers:
            near_copy(step, flip).wait_recv()

    with scope("policy"):
        for ag in range(ill_all):
            i, a = divmod(ag, ill_rows)
            own = jnp.broadcast_to(side_in[i, ill_rows, a : a + 1, :], (TILE, liq_rows))
            for h in range(liq_n):
                drifted = own * received(near_in, 0, h, ag) + (1.0 - own) * received(near_in, 0, h, min(ag + 1, ill_all - 1))
                pencil_one[ag * liq_n + h] = lax.rsqrt(drifted)
        for i in range(ill_n - 1, -1, -1):
            for ag in range(i * ill_rows, (i + 1) * ill_rows):
                blocks = [pencil_one[ag * liq_n + h] for h in range(liq_n)]
                for h in range(liq_n):
                    chosen = interpolate(blocks, received(near_in, 1, h, ag), received(near_in, 2, h, ag))
                    value_two[ag * liq_n + h] = GROSS_RATE / (chosen * chosen)
                    pencil_one[ill_all * liq_n + ag * liq_n + h] = chosen
            send_values(i)
            if i > 0:
                send_plane(i - 1)

    with scope("late"):
        for step, flip in peers:
            late_copy(step, flip).wait_recv()

    lanes = 2 * liq_n
    sub = iota((lanes, liq_rows), 0)
    lane_at = iota((TILE, liq_rows), 1)
    sub_block = jnp.where(sub < liq_n, sub, sub - liq_n).astype(f32)
    lane_row = iota((liq_rows, liq_rows), 0).astype(f32).astype(jnp.bfloat16)
    one = jnp.ones((liq_rows, liq_rows), jnp.bfloat16)
    nil = jnp.zeros((liq_rows, liq_rows), jnp.bfloat16)

    with scope("scatter"):
        held = {}
        for ag in range(ill_all):
            for h in range(liq_n):
                chosen = pencil_one[ill_all * liq_n + ag * liq_n + h]
                share = jnp.clip(received(late_in, 0, h, ag) + SLOPE_GAIN * chosen, 0.0, 1.0)
                mass = received(late_in, 1, h, ag)
                target = received(late_in, 2, h, ag)
                block = jnp.zeros(target.shape, f32)
                for other in range(1, liq_n):
                    block = block + jnp.where(target >= other * liq_rows, 1.0, 0.0)
                held[ag, h] = (mass * share, mass * (1.0 - share), block, target - liq_rows * block)
        for s in range(part):
            totals = []
            for ag in range(ill_all):
                lefts, hots = [], []
                for h in range(liq_n):
                    low_t, high_t, hi_t, lo_t = (x[s : s + 1, :] for x in held[ag, h])
                    both = jnp.where(sub < liq_n, low_t, high_t)
                    both = jnp.where(hi_t == sub_block, both, 0.0)
                    rounded = both.astype(jnp.bfloat16).astype(f32)
                    lefts.append(jnp.concatenate([both, both - rounded], axis=0).astype(jnp.bfloat16))
                    place = jnp.broadcast_to(lo_t, (2 * TILE, liq_rows)).astype(jnp.bfloat16)
                    place = jnp.concatenate([place] * (liq_rows // (2 * TILE)), axis=0)
                    hots.append(jnp.where(lane_row == place, one, nil))
                found = lax.dot_general(
                    jnp.concatenate(lefts, axis=1), jnp.concatenate(hots, axis=1), NT, preferred_element_type=f32
                )
                totals.append(found[:lanes] + found[lanes:])
            to_row = [
                jnp.broadcast_to(side_in[ag // ill_rows, ag % ill_rows, s : s + 1, :], (lanes, liq_rows))
                for ag in range(ill_all)
            ]
            for dest in range(ill_all):
                out = None
                for ag in range(ill_all):
                    here = jnp.where(to_row[ag] == dest, totals[ag], 0.0)
                    out = here if out is None else out + here
                placed[pl.ds(dest * part + s, lanes, stride=ill_all * part), :] = out

    with scope("massout"):
        for dest in range(ill_all):
            carried = None
            for h in range(liq_n):
                low = placed[pl.ds((h * ill_all + dest) * part, part), :]
                moved = pltpu.roll(placed[pl.ds(((liq_n + h) * ill_all + dest) * part, part), :], 1, 1)
                total = low + jnp.where(lane_at > 0, moved, 0.0 if carried is None else carried)
                carried = moved
                mass_out[h * ill_all + dest] = total
                depart_out[h * ill_all + dest] = (1.0 - stay[0]) * total

    def mass_copy(step, flip):
        there = at(step, flip)
        return pltpu.make_async_remote_copy(
            src_ref=mass_out.at[pl.ds(there["liq"] * ill_all + there["ill"] * ill_rows, ill_rows)],
            dst_ref=mass_in.at[pl.ds(ill_me * ill_rows, ill_rows), own_z],
            send_sem=mass_send.at[slot_of(step, flip)], recv_sem=mass_recv.at[slot_of(step, flip)],
            device_id=there, device_id_type=MESH_ID,
        )

    def depart_copy(step, i):
        liq_there = peer_of(liq_me, step, liq_n)
        return pltpu.make_async_remote_copy(
            src_ref=depart_out.at[pl.ds(liq_there * ill_all + i * ill_rows, ill_rows)],
            dst_ref=mass_in.at[pl.ds(group, ill_rows), own_z],
            send_sem=depart_send.at[step * ill_n + i], recv_sem=depart_recv.at[step],
            device_id={"dur": jnp.maximum(dur_me - 1, 0), "liq": liq_there, "ill": i}, device_id_type=MESH_ID,
        )

    departs = (dur_me > 0) & (ill_me == 0)

    @pl.when(departs)
    def _():
        pl.semaphore_wait(ready_sem, 1)
        for step in range(liq_n - 1, -1, -1):
            for i in range(ill_n):
                depart_copy(step, i).start()

    for step, flip in peers:
        mass_copy(step, flip).start()
    for a in range(ill_rows):
        mass_in[ill_me * ill_rows + a, own_z, :] = mass_out[liq_me * ill_all + ill_me * ill_rows + a]

    with scope("values"):
        for step, flip in peers:
            pltpu.make_async_remote_copy(
                src_ref=value_two.at[pl.ds(0, grid_tiles)],
                dst_ref=values_in.at[pl.ds(0, grid_tiles), pl.ds(0, part)],
                send_sem=value_send.at[0], recv_sem=value_recv.at[slot_of(step, flip)],
                device_id=at(step, flip), device_id_type=MESH_ID,
            ).wait_recv()

        @pl.when(ill_me < ill_n - 1)
        def _():
            for step, flip in peers:
                pltpu.make_async_remote_copy(
                    src_ref=value_two.at[pl.ds(0, liq_n)],
                    dst_ref=values_in.at[pl.ds(0, liq_n), pl.ds(0, part)],
                    send_sem=plane_send.at[0], recv_sem=plane_recv.at[slot_of(step, flip)],
                    device_id=at(step, flip), device_id_type=MESH_ID,
                ).wait_recv()

    with scope("second"):
        is_last = ill_me == ill_n - 1
        for d in range(durables):
            expected = []
            for a in range(ill_rows + 1):
                wide = jnp.concatenate([values_in[d * planes + a * liq_n + h] for h in range(liq_n)], axis=1)
                expected.append(times(left_two, wide))
            expected[ill_rows] = jnp.where(is_last, expected[ill_rows - 1], expected[ill_rows])
            for a in range(ill_rows):
                own = drift_ref[a]
                found = lax.rsqrt(own * expected[a] + (1.0 - own) * expected[a + 1])
                for h in range(liq_n):
                    pencil_two[(d * ill_rows + a) * liq_n + h] = found[:, h * liq_rows : (h + 1) * liq_rows]
        for k, (d, a) in enumerate(kinds):
            for q in range(liq_n):
                base = (d * liq_n + q) * per_dest
                blocks = [pencil_two[k * liq_n + h, pl.ds(q * part, part), :] for h in range(liq_n)]
                consumption_ref[rows_at(d, a, q), :] = interpolate(
                    blocks, near_out[base + ill_rows + a], near_out[base + 2 * ill_rows + a]
                )

    with scope("mass"):
        for step, flip in peers:
            mass_copy(step, flip).wait_recv()

        @pl.when(dur_me < dur_n - 1)
        def _():
            for step in range(liq_n):
                depart_copy(step, 0).wait_recv()

    with scope("next"):
        settled = []
        for d, a in kinds:
            after = mass_in[(d + 1) * ill_rows + a]
            if d + 1 < durables:
                after = (1.0 - stay[d + 1]) * after
            settled.append(stay[d] * mass_in[d * ill_rows + a] + after)
        high, low = halves_of(transition)
        found = lax.dot_general(
            jnp.concatenate([high, high, low], axis=0), stack_data(jnp.concatenate(settled, axis=1)),
            (((0,), (0,)), ((), ())), preferred_element_type=f32,
        )
        for k, (d, a) in enumerate(kinds):
            for q in range(liq_n):
                next_ref[rows_at(d, a, q), :] = found[q * part : (q + 1) * part, k * liq_rows : (k + 1) * liq_rows]

    for flip in range(1, ill_n):
        side_copy(flip).wait_send()
    for step, flip in peers:
        near_copy(step, flip).wait_send()
        late_copy(step, flip).wait_send()
        mass_copy(step, flip).wait_send()

    for i in range(ill_n):
        for step in range(1, liq_n):
            main_copy(i, step).wait_send()
            if i < ill_n - 1:
                plane_copy(i, step).wait_send()

        @pl.when(ill_me != i)
        def _():
            main_copy(i, 0).wait_send()
            if i < ill_n - 1:
                plane_copy(i, 0).wait_send()

    @pl.when(departs)
    def _():
        for step in range(liq_n):
            for i in range(ill_n):
                depart_copy(step, i).wait_send()


def store(consumption_ref, next_ref, consumption_hbm, next_hbm, sem):
    copies = [
        pltpu.make_async_copy(consumption_ref, consumption_hbm, sem.at[0]),
        pltpu.make_async_copy(next_ref, next_hbm, sem.at[1]),
    ]
    for copy in copies:
        copy.start()
    for copy in copies:
        copy.wait()


def window_scratch(dims):
    incomes, durables, ill_rows, liq_rows, liq_n, ill_n, dur_n = dims
    f32 = jnp.float32
    rows, plane_rows = incomes * durables * ill_rows, incomes * ill_rows
    block = (rows, liq_rows)
    dma = pltpu.SemaphoreType.DMA
    return [
        pltpu.VMEM(block, f32),
        pltpu.VMEM((incomes, incomes), f32),
        pltpu.VMEM((1, incomes), f32),
        pltpu.VMEM(block, jnp.int32),
        pltpu.VMEM(block, f32),
        pltpu.VMEM(block, f32),
        pltpu.VMEM(block, f32),
        pltpu.VMEM(block, jnp.int32),
        pltpu.VMEM(block, f32),
        pltpu.SMEM((ill_rows,), f32),
        pltpu.SMEM((durables,), f32),
        pltpu.SMEM((durables * ill_rows, incomes), jnp.int32),
        dma((12,)),
        pltpu.VMEM((rows, rows), f32),
        pltpu.VMEM((rows, rows), f32),
        pltpu.VMEM((rows, rows), f32),
        pltpu.VMEM((rows, rows), f32),
        pltpu.VMEM((rows, rows), f32),
        pltpu.VMEM((rows, plane_rows), f32),
        pltpu.VMEM((2,) + block, f32),
        pltpu.VMEM(block, f32),
        pltpu.VMEM((2 * liq_n,) + block, f32),
        pltpu.VMEM(block, f32),
        pltpu.VMEM(block, f32),
        pltpu.VMEM(block, jnp.int32),
        pltpu.VMEM(block, f32),
        pltpu.VMEM((2 * ill_n * liq_n * plane_rows, liq_rows), f32),
        pltpu.VMEM((ill_n * liq_n * rows, liq_rows), f32),
        pltpu.VMEM((durables * (ill_n - 1), liq_n * plane_rows, liq_rows), f32),
        pltpu.VMEM((durables * liq_n, plane_rows, liq_rows), f32),
        pltpu.VMEM((durables * (liq_n - 1), plane_rows, liq_rows), f32),
        pltpu.VMEM(block, f32),
        pltpu.VMEM((plane_rows, liq_rows), f32),
        pltpu.VMEM((plane_rows, liq_rows), f32),
        dma((2,)),
        dma((2,)),
        dma((4 * liq_n,)),
        dma((4 * liq_n,)),
        dma((durables * (ill_n - 1),)),
        dma((durables * (ill_n - 1),)),
        dma((durables * (liq_n - 1),)),
        dma((durables * (liq_n - 1),)),
        dma((1,)),
        dma((1,)),
    ]


def transposed_scratch(dims):
    incomes, durables, ill_rows, liq_rows, liq_n, ill_n, dur_n = dims
    f32 = jnp.float32
    block = (incomes * durables * ill_rows, liq_rows)
    dma = pltpu.SemaphoreType.DMA
    part = incomes // liq_n
    ill_all = ill_n * ill_rows
    tiles = lambda n: pltpu.VMEM((n, part, liq_rows), f32)
    slabs = lambda n: pltpu.VMEM((n, incomes, liq_rows), f32)
    bundle = durables * liq_n * 3 * ill_rows
    peers = liq_n * ill_n
    return [
        pltpu.VMEM(block, f32),
        pltpu.VMEM((incomes, incomes), f32),
        pltpu.VMEM((1, incomes), f32),
        pltpu.VMEM(block, jnp.int32),
        pltpu.VMEM(block, f32),
        pltpu.VMEM(block, f32),
        pltpu.VMEM(block, f32),
        pltpu.VMEM(block, jnp.int32),
        pltpu.VMEM(block, f32),
        pltpu.VMEM((durables * ill_rows, incomes), jnp.int32),
        pltpu.SMEM((ill_rows,), f32),
        pltpu.SMEM((durables,), f32),
        dma((12,)),
        tiles(bundle),
        tiles(bundle),
        tiles(bundle),
        tiles(bundle),
        pltpu.VMEM((durables, ill_rows + 1, TILE, liq_rows), f32),
        pltpu.VMEM((ill_n, ill_rows + 1, TILE, liq_rows), f32),
        tiles(2 * ill_all * liq_n),
        tiles(ill_all * liq_n),
        slabs(durables * (ill_rows + 1) * liq_n),
        slabs(durables * ill_rows * liq_n),
        pltpu.VMEM((2 * liq_n * ill_all * part, liq_rows), f32),
        tiles(liq_n * ill_all),
        tiles(liq_n * ill_all),
        slabs((durables + 1) * ill_rows),
    ] + [
        dma((n,))
        for n in (
            peers, peers, peers, peers, ill_n, ill_n, peers, peers, peers, peers, peers, peers, peers, liq_n,
        )
    ] + [pltpu.SemaphoreType.REGULAR]


def body(
    marginal_value,
    transition,
    discount_shock,
    illiquid_drift,
    durable_keep,
    bracket_index,
    bracket_weight,
    steady_consumption,
    lottery_weight,
    liquid_target,
    illiquid_target,
    population,
):
    shape = marginal_value.shape
    incomes, durables, ill_rows, liq_rows = shape
    liq_n, ill_n, dur_n = (lax.axis_size(name) for name in ("liq", "ill", "dur"))
    rows = incomes * durables * ill_rows
    flat = lambda x: x.reshape(rows, liq_rows)
    anywhere = pl.BlockSpec(memory_space=pl.ANY)
    f32 = jnp.float32
    block = (rows, liq_rows)
    dma = pltpu.SemaphoreType.DMA
    vmem = pl.BlockSpec(memory_space=pltpu.VMEM)
    held = pltpu.VMEM(block, f32)
    result = jax.ShapeDtypeStruct(block, f32)
    dims = (incomes, durables, ill_rows, liq_rows, liq_n, ill_n, dur_n)
    transposed = (
        ill_n == 2 and durables == ill_n and liq_n * 2 == TILE and incomes == liq_n * TILE and ill_rows < TILE
    )
    if transposed:
        step_kernel, scratch, name = transposed_kernel, transposed_scratch(dims), "transposed_window"
    else:
        step_kernel, scratch, name = kernel, window_scratch(dims), "window"
    outs = pl.pallas_call(
        functools.partial(step_kernel, dims),
        out_shape=(held, held),
        in_specs=[anywhere] * 12,
        out_specs=(vmem, vmem),
        scratch_shapes=scratch,
        compiler_params=pltpu.CompilerParams(collective_id=0, has_side_effects=True),
        name=name,
    )(
        flat(marginal_value),
        transition,
        discount_shock.reshape(1, incomes),
        illiquid_drift,
        durable_keep,
        flat(bracket_index),
        flat(bracket_weight),
        flat(steady_consumption),
        flat(lottery_weight),
        flat(liquid_target),
        jnp.transpose(illiquid_target, (1, 2, 0)).reshape(durables * ill_rows, incomes),
        flat(population),
    )
    outs = pl.pallas_call(
        store,
        out_shape=(result, result),
        in_specs=[vmem, vmem],
        out_specs=(anywhere, anywhere),
        scratch_shapes=[dma((2,))],
        name="store",
    )(*(pltpu.with_memory_space_constraint(out, pltpu.VMEM) for out in outs))
    return tuple(out.reshape(shape) for out in outs)


def solution(mesh):
    in_specs = (
        P(None, "dur", "ill", "liq"),
        P(),
        P(),
        P("ill"),
        P("dur"),
        P(None, "dur", "ill", "liq"),
        P(None, "dur", "ill", "liq"),
        P(None, "dur", "ill", "liq"),
        P(None, "dur", "ill", "liq"),
        P(None, "dur", "ill", "liq"),
        P(None, "dur", "ill"),
        P(None, "dur", "ill", "liq"),
    )
    out_specs = (P(None, "dur", "ill", "liq"), P(None, "dur", "ill", "liq"))
    return jax.shard_map(body, mesh=mesh, in_specs=in_specs, out_specs=out_specs, check_vma=False)
```

```python
import contextlib
import functools

import jax
import jax.numpy as jnp
from jax import lax
from jax.experimental import pallas as pl
from jax.experimental.pallas import tpu as pltpu
from jax.sharding import PartitionSpec as P

DISCOUNT = 0.96
GROSS_RATE = 1.01
SLOPE_GAIN = 0.5
HIGHEST_PREC = lax.Precision.HIGHEST
MESH_ID = pl.DeviceIdType.MESH
NT = (((1,), (1,)), ((), ()))
TILE = 8


def scope(name):
    return contextlib.nullcontext()


def split_by(x, n):
    if n & (n - 1) == 0:
        return x >> (n.bit_length() - 1), x & (n - 1)
    return lax.div(x, jnp.int32(n)), lax.rem(x, jnp.int32(n))


def dot(a, b):
    return jnp.dot(a, b, precision=HIGHEST_PREC, preferred_element_type=jnp.float32)


def iota(shape, axis):
    return lax.broadcasted_iota(jnp.int32, shape, axis)


def as_float(flag):
    return jnp.where(flag, jnp.float32(1.0), jnp.float32(0.0))


def peer_of(me, step, n):
    if n & (n - 1):
        return lax.rem(me + step, n)
    out = me
    for bit in range(n.bit_length() - 1):
        if step >> bit & 1:
            out = out + (1 - 2 * lax.rem(lax.div(me, jnp.int32(1 << bit)), jnp.int32(2))) * (1 << bit)
    return out


def kernel(
    dims,
    value_hbm, transition_hbm, shock_hbm, drift_hbm, keep_hbm, index_hbm, weight_hbm,
    steady_hbm, lottery_hbm, target_hbm, ill_target_hbm, population_hbm,
    consumption_ref, next_ref,
    value_ref, transition_ref, shock_ref, index_ref, weight_ref, steady_ref, lottery_ref, target_ref,
    population_ref, drift_ref, keep_ref, ill_target_ref, load_sem,
    first_mat, first_up, second_mat, second_up, next_mat, next_in,
    near_value, value_two, pencil, mass_low, mass_high, target_hi, target_lo,
    placed_rows, terms, terms_in, owner_sum, owner_in, settled, depart, depart_in,
    value_send, value_recv, pencil_send, pencil_recv, terms_send, terms_recv,
    owner_send, owner_recv, depart_send, depart_recv,
):
    incomes, durables, ill_rows, liq_rows, liq_n, ill_n, dur_n = dims
    group = durables * ill_rows
    rows = incomes * group
    half_rows = rows // 2
    plane_rows = incomes * ill_rows
    liq_me, ill_me, dur_me = (lax.axis_index(name) for name in ("liq", "ill", "dur"))
    far_first = range(liq_n - 1, 0, -1)

    barrier = pltpu.get_barrier_semaphore()
    for step in far_first:
        pl.semaphore_signal(barrier, inc=1, device_id={"liq": peer_of(liq_me, step, liq_n)}, device_id_type=MESH_ID)
    for step in range(1, ill_n):
        pl.semaphore_signal(barrier, inc=1, device_id={"ill": peer_of(ill_me, step, ill_n)}, device_id_type=MESH_ID)

    @pl.when(dur_me > 0)
    def _():
        pl.semaphore_signal(barrier, inc=1, device_id={"dur": dur_me - 1}, device_id_type=MESH_ID)

    @pl.when(dur_me < dur_n - 1)
    def _():
        pl.semaphore_signal(barrier, inc=1, device_id={"dur": dur_me + 1}, device_id_type=MESH_ID)

    loads = [
        pltpu.make_async_copy(source, held, load_sem.at[slot])
        for slot, (source, held) in enumerate((
            (transition_hbm, transition_ref), (shock_hbm, shock_ref), (drift_hbm, drift_ref), (value_hbm, value_ref),
            (keep_hbm, keep_ref), (ill_target_hbm, ill_target_ref),
            (index_hbm, index_ref), (weight_hbm, weight_ref), (target_hbm, target_ref),
            (lottery_hbm, lottery_ref), (steady_hbm, steady_ref), (population_hbm, population_ref),
        ))
    ]
    for load in loads:
        load.start()
    for load in loads[:3]:
        load.wait()

    transition = transition_ref[...]
    row_z, row_rest = split_by(iota((rows, rows), 0), group)
    col_z, col_rest = split_by(iota((rows, rows), 1), group)
    row_d, row_a = split_by(row_rest, ill_rows)
    col_d, col_a = split_by(col_rest, ill_rows)
    spread = as_float(split_by(iota((rows, incomes), 0), group)[0] == iota((rows, incomes), 1))
    spread_t = as_float(iota((incomes, rows), 0) == split_by(iota((incomes, rows), 1), group)[0])
    drift = jnp.zeros((rows, rows), jnp.float32)
    for a in range(ill_rows):
        drift = jnp.where(row_a == a, drift_ref[a], drift)
    is_last = as_float(ill_me == ill_n - 1)
    same_d = row_d == col_d
    top_row = row_a == ill_rows - 1
    local = jnp.where(col_a == row_a, drift, 0.0)
    local = local + jnp.where(col_a == row_a + 1, 1.0 - drift, 0.0)
    local = local + jnp.where(top_row & (col_a == ill_rows - 1), is_last * (1.0 - drift), 0.0)
    local = jnp.where(same_d, local, 0.0)
    upper = jnp.where(same_d & top_row & (col_a == 0), (1.0 - is_last) * (1.0 - drift), 0.0)
    constant = jnp.float32(DISCOUNT * GROSS_RATE)
    eye = iota((incomes, incomes), 0) == iota((incomes, incomes), 1)
    scaled = dot(jnp.where(eye, constant * shock_ref[...], 0.0), transition)
    wide = dot(dot(spread, scaled), spread_t)
    first_mat[...] = wide * local
    first_up[...] = wide * upper

    dur_peers = jnp.minimum(dur_me, 1) + jnp.minimum(dur_n - 1 - dur_me, 1)
    pl.semaphore_wait(barrier, liq_n - 1 + ill_n - 1 + dur_peers)

    ill_below = lax.rem(ill_me + ill_n - 1, ill_n)

    def value_copy(k, source):
        return pltpu.make_async_remote_copy(
            src_ref=source, dst_ref=near_value.at[k], send_sem=value_send.at[k],
            recv_sem=value_recv.at[k], device_id={"ill": ill_below}, device_id_type=MESH_ID,
        )

    def pencil_copy(k, half, step):
        slot = (k * 2 + half) * liq_n + step
        part = pencil.at[k * liq_n + liq_me, pl.ds(half * half_rows, half_rows)]
        return pltpu.make_async_remote_copy(
            src_ref=part, dst_ref=part, send_sem=pencil_send.at[slot], recv_sem=pencil_recv.at[slot],
            device_id={"liq": peer_of(liq_me, step, liq_n)}, device_id_type=MESH_ID,
        )

    def pencil_relay(half):
        near, far = (1, 2) if half == 0 else (2, 1)
        slot = (2 + half) * liq_n
        part = pencil.at[liq_n + peer_of(liq_me, near, liq_n), pl.ds(half * half_rows, half_rows)]
        return pltpu.make_async_remote_copy(
            src_ref=part, dst_ref=part, send_sem=pencil_send.at[slot], recv_sem=pencil_recv.at[slot],
            device_id={"liq": peer_of(liq_me, far, liq_n)}, device_id_type=MESH_ID,
        )

    relayed = liq_n == 4
    if relayed:
        early, late = [(0, 1), (1, 2)], [(1, 1), (0, 2)]
    else:
        early, late = [(0, step) for step in far_first], [(1, step) for step in far_first]

    def terms_copy(d, step):
        peer = peer_of(ill_me, step, ill_n)
        slot = d * (ill_n - 1) + step - 1
        return pltpu.make_async_remote_copy(
            src_ref=terms.at[pl.ds((d * ill_n + peer) * (liq_n * plane_rows), liq_n * plane_rows)],
            dst_ref=terms_in.at[slot], send_sem=terms_send.at[slot], recv_sem=terms_recv.at[slot],
            device_id={"ill": peer}, device_id_type=MESH_ID,
        )

    def owner_copy(d, step):
        peer = peer_of(liq_me, step, liq_n)
        slot = d * (liq_n - 1) + step - 1
        return pltpu.make_async_remote_copy(
            src_ref=owner_sum.at[d * liq_n + peer], dst_ref=owner_in.at[slot],
            send_sem=owner_send.at[slot], recv_sem=owner_recv.at[slot],
            device_id={"liq": peer}, device_id_type=MESH_ID,
        )

    loads[3].wait()
    value_copy(0, value_ref).start()
    drifted = dot(first_mat[...], value_ref[...])
    value_copy(0, value_ref).wait_recv()
    drifted = drifted + dot(first_up[...], near_value[0])
    pencil[liq_me] = lax.rsqrt(drifted)
    for half in range(2):
        for step in far_first:
            pencil_copy(0, half, step).start()

    wide = constant * dot(dot(spread, transition), spread_t)
    second_mat[...] = wide * local
    second_up[...] = wide * upper

    for load in loads[4:]:
        load.wait()

    first_d = as_float(dur_me == 0)
    stay = [keep_ref[d] for d in range(durables)]
    stay[0] = first_d + (1.0 - first_d) * stay[0]
    back_d, back_rest = split_by(iota((rows, rows), 1), plane_rows)
    back_a = split_by(back_rest, ill_rows)[1]
    stays = jnp.zeros((rows, rows), jnp.float32)
    for d in range(durables):
        stays = jnp.where(back_d == d, stay[d], stays)
    mix = jnp.where(back_d == row_d, stays, 0.0) + jnp.where(back_d == row_d + 1, 1.0 - stays, 0.0)
    mix = jnp.where(back_a == row_a, mix, 0.0)
    back_z = split_by(split_by(iota((incomes, rows), 1), plane_rows)[1], ill_rows)[0]
    turned = lax.dot_general(spread, transition, NT, precision=HIGHEST_PREC, preferred_element_type=jnp.float32)
    wide = dot(turned, as_float(iota((incomes, rows), 0) == back_z))
    next_mat[...] = wide * mix
    in_z, in_a = split_by(iota((incomes, plane_rows), 1), ill_rows)
    wide = dot(turned, as_float(iota((incomes, plane_rows), 0) == in_z))
    in_row = split_by(iota((rows, plane_rows), 0), group)[1]
    in_row_d, in_row_a = split_by(in_row, ill_rows)
    in_col_a = split_by(iota((rows, plane_rows), 1), ill_rows)[1]
    next_in[...] = jnp.where((in_row_d == durables - 1) & (in_row_a == in_col_a), wide, 0.0)

    def block_of(position):
        block = jnp.zeros(position.shape, jnp.int32)
        for h in range(1, liq_n):
            block = block + jnp.where(position >= h * liq_rows, 1, 0)
        return block, position - block * liq_rows

    target_hi[...], lo = block_of(target_ref[...])
    target_lo[...] = lo.astype(jnp.float32)

    def interpolate(k, tile):
        span = pl.ds(tile * TILE, TILE)
        index = index_ref[span, :]
        low_block, low_lane = block_of(index)
        high_block, high_lane = block_of(index + 1)
        low = high = None
        for h in range(liq_n):
            block = pencil[k * liq_n + h, span, :]
            low_h = jnp.take_along_axis(block, low_lane, axis=1, mode="promise_in_bounds")
            high_h = jnp.take_along_axis(block, high_lane, axis=1, mode="promise_in_bounds")
            low = low_h if h == 0 else jnp.where(low_block == h, low_h, low)
            high = high_h if h == 0 else jnp.where(high_block == h, high_h, high)
        weight = weight_ref[span, :]
        return weight * low + (1.0 - weight) * high

    tiles = rows // TILE
    halves = (range(tiles // 2), range(tiles // 2, tiles))

    def first_policy(half):
        for step in far_first:
            pencil_copy(0, half, step).wait_recv()
        for tile in halves[half]:
            span = pl.ds(tile * TILE, TILE)
            chosen = interpolate(0, tile)
            value_two[span, :] = GROSS_RATE / (chosen * chosen)
            share = jnp.clip(lottery_ref[span, :] + SLOPE_GAIN * (chosen - steady_ref[span, :]), 0.0, 1.0)
            mass = population_ref[span, :]
            mass_low[span, :] = mass * share
            mass_high[span, :] = mass * (1.0 - share)

    lanes = 2 * liq_n
    sub = iota((lanes, liq_rows), 0)
    lane_at = iota((TILE, liq_rows), 1)
    sub_block = jnp.where(sub < liq_n, sub, sub - liq_n)
    lane_row = iota((liq_rows, liq_rows), 0).astype(jnp.float32).astype(jnp.bfloat16)
    one = jnp.ones((liq_rows, liq_rows), jnp.bfloat16)
    nil = jnp.zeros((liq_rows, liq_rows), jnp.bfloat16)
    per_tile = TILE // group

    def scatter_tile(d, tile):
        span = pl.ds(pl.multiple_of(tile * TILE, TILE), TILE)
        low_t, high_t, hi_t, lo_t = mass_low[span, :], mass_high[span, :], target_hi[span, :], target_lo[span, :]
        for zz in range(per_tile):
            z = tile * per_tile + zz
            totals = []
            for a in range(ill_rows):
                k = zz * group + d * ill_rows + a
                both = jnp.where(sub < liq_n, low_t[k : k + 1, :], high_t[k : k + 1, :])
                both = jnp.where(hi_t[k : k + 1, :] == sub_block, both, 0.0)
                rounded = both.astype(jnp.bfloat16).astype(jnp.float32)
                parts = jnp.concatenate([both, both - rounded], axis=0).astype(jnp.bfloat16)
                place = jnp.broadcast_to(lo_t[k : k + 1, :], (2 * TILE, liq_rows)).astype(jnp.bfloat16)
                place = jnp.concatenate([place] * (liq_rows // (2 * TILE)), axis=0)
                hot = jnp.where(lane_row == place, one, nil)
                placed = lax.dot_general(parts, hot, NT, preferred_element_type=jnp.float32)
                placed = placed[:lanes] + placed[lanes:]
                totals.append(placed)
            for dest in range(ill_n * ill_rows):
                out = None
                for a in range(ill_rows):
                    here = as_float(ill_target_ref[d * ill_rows + a, z] == dest) * totals[a]
                    out = here if out is None else out + here
                base = dest // ill_rows * lanes * plane_rows + z * ill_rows + dest % ill_rows
                placed_rows[pl.ds(base, lanes, stride=plane_rows), :] = out

    unroll = tiles // 2

    def scatter(d, half):
        def step(pair, carry):
            for turn in range(unroll):
                scatter_tile(d, halves[half].start + unroll * pair + turn)
            return carry

        lax.fori_loop(0, tiles // 2 // unroll, step, 0)

    def send_terms(d):
        for owner in range(ill_n):
            for piece in range(plane_rows // TILE):
                carried = None
                for h in range(liq_n):
                    low_at = (owner * lanes + h) * plane_rows + piece * TILE
                    low = placed_rows[pl.ds(low_at, TILE), :]
                    moved = pltpu.roll(placed_rows[pl.ds(low_at + liq_n * plane_rows, TILE), :], 1, 1)
                    edge = jnp.where(lane_at > 0, moved, 0.0 if carried is None else carried)
                    carried = moved
                    out_at = ((d * ill_n + owner) * liq_n + h) * plane_rows + piece * TILE
                    terms[pl.ds(out_at, TILE), :] = low + edge
        for step in range(1, ill_n):
            terms_copy(d, step).start()

    def send_owners(d):
        for step in range(1, ill_n):
            terms_copy(d, step).wait_recv()
        for h in range(liq_n):
            start = pl.multiple_of(((d * ill_n + ill_me) * liq_n + h) * plane_rows, TILE)
            total = terms[pl.ds(start, plane_rows), :]
            for step in range(1, ill_n):
                total = total + terms_in[d * (ill_n - 1) + step - 1, pl.ds(h * plane_rows, plane_rows), :]
            owner_sum[d * liq_n + h] = total
        for step in far_first:
            owner_copy(d, step).start()

    def collect(d):
        for step in far_first:
            owner_copy(d, step).wait_recv()
        total = owner_sum[d * liq_n + liq_me]
        for step in range(1, liq_n):
            total = total + owner_in[d * (liq_n - 1) + step - 1]
        settled[pl.ds(d * plane_rows, plane_rows), :] = total
        return total

    def second_policy():
        if relayed:
            for half in range(2):
                pencil_relay(half).wait_recv()
        else:
            for half, step in early:
                pencil_copy(1, half, step).wait_recv()
        for half, step in late:
            pencil_copy(1, half, step).wait_recv()
        for tile in range(tiles):
            consumption_ref[pl.ds(tile * TILE, TILE), :] = interpolate(1, tile)

    first_policy(0)
    scatter(0, 0)
    first_policy(1)
    value_copy(1, value_two).start()
    scatter(0, 1)
    send_terms(0)
    value_copy(1, value_two).wait_recv()
    drifted = dot(second_mat[...], value_two[...]) + dot(second_up[...], near_value[1])
    pencil[liq_n + liq_me] = lax.rsqrt(drifted)
    for half, step in early:
        pencil_copy(1, half, step).start()
    for d in range(1, durables):
        scatter(d, 0)
        if d == 1:
            send_owners(0)
            for half, step in late:
                pencil_copy(1, half, step).start()
        scatter(d, 1)
        send_terms(d)
    for d in range(1, durables):
        send_owners(d)
    if relayed:
        for half, step in early:
            pencil_copy(1, half, step).wait_recv()
        for half in range(2):
            pencil_relay(half).start()

    depart_copy = pltpu.make_async_remote_copy(
        src_ref=depart, dst_ref=depart_in, send_sem=depart_send.at[0], recv_sem=depart_recv.at[0],
        device_id={"dur": jnp.maximum(dur_me - 1, 0)}, device_id_type=MESH_ID,
    )

    depart[...] = (1.0 - stay[0]) * collect(0)

    @pl.when(dur_me > 0)
    def _():
        depart_copy.start()

    for d in range(1, durables):
        collect(d)
    next_ref[...] = dot(next_mat[...], settled[...])
    second_policy()

    @pl.when(dur_me < dur_n - 1)
    def _():
        depart_copy.wait_recv()
        next_ref[...] += dot(next_in[...], depart_in[...])

    value_copy(0, value_ref).wait_send()
    value_copy(1, value_two).wait_send()
    for step in range(1, liq_n):
        for half in range(2):
            pencil_copy(0, half, step).wait_send()
        for d in range(durables):
            owner_copy(d, step).wait_send()
    for half, step in early + late:
        pencil_copy(1, half, step).wait_send()
    if relayed:
        for half in range(2):
            pencil_relay(half).wait_send()
    for step in range(1, ill_n):
        for d in range(durables):
            terms_copy(d, step).wait_send()

    @pl.when(dur_me > 0)
    def _():
        depart_copy.wait_send()


def halves_of(x):
    high = x.astype(jnp.bfloat16)
    return high, (x - high.astype(jnp.float32)).astype(jnp.bfloat16)


def stack_data(x):
    high, low = halves_of(x)
    return jnp.concatenate([high, low, high], axis=0)


def transposed_kernel(
    dims,
    value_hbm, transition_hbm, shock_hbm, drift_hbm, keep_hbm, index_hbm, weight_hbm,
    steady_hbm, lottery_hbm, target_hbm, ill_target_hbm, population_hbm,
    consumption_ref, next_ref,
    value_ref, transition_ref, shock_ref, index_ref, weight_ref, steady_ref, lottery_ref, target_ref,
    population_ref, ill_target_ref, drift_ref, keep_ref, load_sem,
    near_out, near_in, late_out, late_in, side_out, side_in, pair_in,
    pencil_one, value_two, values_in, pencil_two, found_out, found_in, placed, mass_out, depart_out, mass_in,
    near_send, near_recv, late_send, late_recv, side_send, side_recv, pair_send, pair_recv,
    value_send, value_recv, found_send, found_recv, mass_send, mass_recv, depart_send, depart_recv, ready_sem,
):
    incomes, durables, ill_rows, liq_rows, liq_n, ill_n, dur_n = dims
    group = durables * ill_rows
    ill_all = ill_n * ill_rows
    part = incomes // liq_n
    per_dest = 3 * ill_rows
    constant = jnp.float32(DISCOUNT * GROSS_RATE)
    f32 = jnp.float32
    liq_me, ill_me, dur_me = (lax.axis_index(name) for name in ("liq", "ill", "dur"))
    far_first = range(liq_n - 1, 0, -1)
    peers = [(step, flip) for step in range(liq_n - 1, -1, -1) for flip in range(ill_n) if step or flip]

    def at(step, flip):
        return {"liq": peer_of(liq_me, step, liq_n), "ill": peer_of(ill_me, flip, ill_n)}

    barrier = pltpu.get_barrier_semaphore()
    for step, flip in peers:
        pl.semaphore_signal(barrier, inc=1, device_id=at(step, flip), device_id_type=MESH_ID)

    @pl.when(dur_me > 0)
    def _():
        pl.semaphore_signal(barrier, inc=1, device_id={"dur": dur_me - 1}, device_id_type=MESH_ID)

    @pl.when(dur_me < dur_n - 1)
    def _():
        pl.semaphore_signal(barrier, inc=1, device_id={"dur": dur_me + 1}, device_id_type=MESH_ID)

    loads = [
        pltpu.make_async_copy(source, held, load_sem.at[slot])
        for slot, (source, held) in enumerate((
            (transition_hbm, transition_ref), (shock_hbm, shock_ref), (value_hbm, value_ref),
            (index_hbm, index_ref), (weight_hbm, weight_ref), (drift_hbm, drift_ref), (ill_target_hbm, ill_target_ref),
            (target_hbm, target_ref), (lottery_hbm, lottery_ref), (steady_hbm, steady_ref),
            (population_hbm, population_ref), (keep_hbm, keep_ref),
        ))
    ]
    for load in loads:
        load.start()

    def rows_at(d, a, z_part):
        return pl.ds(z_part * part * group + d * ill_rows + a, part, stride=group)

    def whole_rows(d, a):
        return pl.ds(d * ill_rows + a, incomes, stride=group)

    kinds = [(d, a) for d in range(durables) for a in range(ill_rows)]
    for load in loads[:2]:
        load.wait()
    transition = transition_ref[...]
    eye = iota((incomes, incomes), 0) == iota((incomes, incomes), 1)
    scaled = dot(jnp.where(eye, constant * shock_ref[...], 0.0), transition)

    def stack_left(x):
        high, low = halves_of(x)
        return jnp.concatenate([high, high, low], axis=1)

    def times(left, x):
        return jnp.dot(left, stack_data(x), preferred_element_type=f32)

    left_one = stack_left(scaled)
    left_two = stack_left(constant * transition)
    loads[2].wait()
    wide = jnp.concatenate([value_ref[whole_rows(d, a), :] for d, a in kinds], axis=1)
    wide = times(left_one, wide)
    for load in loads[3:5]:
        load.wait()
    for k, (d, a) in enumerate(kinds):
        for q in range(liq_n):
            near_out[d * liq_n + q, a] = wide[q * part : (q + 1) * part, k * liq_rows : (k + 1) * liq_rows]
            near_out[d * liq_n + q, ill_rows + a] = index_ref[rows_at(d, a, q), :].astype(f32)
            near_out[d * liq_n + q, 2 * ill_rows + a] = weight_ref[rows_at(d, a, q), :]

    for load in loads[5:7]:
        load.wait()
    column = iota((part, incomes), 1)
    wanted = column == liq_me * part + iota((part, incomes), 0)
    picked = jnp.concatenate(
        [
            jnp.where(wanted, jnp.broadcast_to(ill_target_ref[k : k + 1, :], (part, incomes)), 0)
            for k in range(group)
        ],
        axis=0,
    )
    spread = jnp.dot(
        picked.astype(f32).astype(jnp.bfloat16), jnp.ones((incomes, liq_rows), jnp.bfloat16), preferred_element_type=f32
    )
    row = iota((TILE, liq_rows), 0)
    drifts = jnp.zeros((TILE, liq_rows), f32)
    for a in range(ill_rows):
        drifts = jnp.where(row == a, drift_ref[a], drifts)
    for k, (d, a) in enumerate(kinds):
        side_out[d, a] = spread[k * part : (k + 1) * part]
    for d in range(durables):
        side_out[d, ill_rows] = drifts

    with scope("bar"):
        dur_peers = jnp.minimum(dur_me, 1) + jnp.minimum(dur_n - 1 - dur_me, 1)
        pl.semaphore_wait(barrier, len(peers) + dur_peers)

    @pl.when((dur_me < dur_n - 1) & (ill_me == 0))
    def _():
        pl.semaphore_signal(ready_sem, inc=1, device_id={"dur": dur_me + 1}, device_id_type=MESH_ID)

    def bundle_copy(out_ref, in_ref, send, recv, step, flip):
        there = at(step, flip)
        return pltpu.make_async_remote_copy(
            src_ref=out_ref.at[there["ill"] * liq_n + there["liq"]], dst_ref=in_ref.at[liq_me * ill_n + ill_me],
            send_sem=send.at[0], recv_sem=recv.at[0], device_id=there, device_id_type=MESH_ID,
        )

    def bundle_all(out_ref, in_ref, send, recv):
        span = pl.ds(0, len(peers))
        return pltpu.make_async_remote_copy(
            src_ref=out_ref.at[span], dst_ref=in_ref.at[span], send_sem=send.at[0], recv_sem=recv.at[0],
            device_id=at(0, 1), device_id_type=MESH_ID,
        )

    def near_all():
        return bundle_all(near_out, near_in, near_send, near_recv)

    def late_all():
        return bundle_all(late_out, late_in, late_send, late_recv)

    def near_copy(step, flip):
        return bundle_copy(near_out, near_in, near_send, near_recv, step, flip)

    def late_copy(step, flip):
        return bundle_copy(late_out, late_in, late_send, late_recv, step, flip)

    def side_copy(flip):
        there = at(0, flip)
        return pltpu.make_async_remote_copy(
            src_ref=side_out.at[there["ill"]], dst_ref=side_in.at[ill_me],
            send_sem=side_send.at[flip - 1], recv_sem=side_recv.at[flip - 1], device_id=there, device_id_type=MESH_ID,
        )

    def pair_copy(flip):
        there = at(0, flip)
        return pltpu.make_async_remote_copy(
            src_ref=near_out.at[pl.ds(there["ill"] * liq_n, liq_n), pl.ds(ill_rows, 2 * ill_rows)],
            dst_ref=pair_in.at[ill_me], send_sem=pair_send.at[flip - 1], recv_sem=pair_recv.at[flip - 1],
            device_id=there, device_id_type=MESH_ID,
        )

    for step, flip in peers:
        near_copy(step, flip).start()
    for flip in range(1, ill_n):
        side_copy(flip).start()

    for load in loads[7:]:
        load.wait()
    for d, a in kinds:
        for q in range(liq_n):
            span = rows_at(d, a, q)
            late_out[d * liq_n + q, a] = lottery_ref[span, :] - SLOPE_GAIN * steady_ref[span, :]
            late_out[d * liq_n + q, ill_rows + a] = population_ref[span, :]
            late_out[d * liq_n + q, 2 * ill_rows + a] = target_ref[span, :].astype(f32)
    for step, flip in peers:
        late_copy(step, flip).start()
    for flip in range(1, ill_n):
        pair_copy(flip).start()

    own_out = ill_me * liq_n + liq_me
    own_in = liq_me * ill_n + ill_me
    for k in range(per_dest):
        near_in[own_in, k] = near_out[own_out, k]
        late_in[own_in, k] = late_out[own_out, k]
    for k in range(ill_rows + 1):
        side_in[ill_me, k] = side_out[ill_me, k]
    for q in range(liq_n):
        for k in range(2 * ill_rows):
            pair_in[ill_me, q, k] = near_out[ill_me * liq_n + q, ill_rows + k]

    @pl.when(dur_me == dur_n - 1)
    def _():
        for a in range(ill_rows):
            mass_in[group + a] = jnp.zeros((incomes, liq_rows), f32)

    stay = [keep_ref[d] for d in range(durables)]
    first_d = as_float(dur_me == 0)
    stay[0] = first_d + (1.0 - first_d) * stay[0]

    def received(ref, kind, h, ag):
        return ref[h * ill_n + ag // ill_rows, kind * ill_rows + ag % ill_rows]

    def interpolate(blocks, index, weight):
        index = index.astype(jnp.int32)
        low_block, low_lane = split_by(index, liq_rows)
        high_block, high_lane = split_by(index + 1, liq_rows)
        low = high = None
        for h, block in enumerate(blocks):
            low_h = jnp.take_along_axis(block, low_lane, axis=1, mode="promise_in_bounds")
            high_h = jnp.take_along_axis(block, high_lane, axis=1, mode="promise_in_bounds")
            low = low_h if h == 0 else jnp.where(low_block == h, low_h, low)
            high = high_h if h == 0 else jnp.where(high_block == h, high_h, high)
        return weight * low + (1.0 - weight) * high

    own_z = pl.ds(pl.multiple_of(liq_me * part, TILE), part)

    chunk = ill_rows * liq_n

    def value_copy(i, step):
        span = pl.ds(i * chunk, chunk)
        return pltpu.make_async_remote_copy(
            src_ref=value_two.at[span], dst_ref=values_in.at[span, own_z], send_sem=value_send.at[0],
            recv_sem=value_recv.at[0], device_id={"liq": peer_of(liq_me, step, liq_n)}, device_id_type=MESH_ID,
        )

    def value_all():
        span = pl.ds(0, (liq_n - 1) * ill_all)
        return pltpu.make_async_remote_copy(
            src_ref=values_in.at[span], dst_ref=values_in.at[span], send_sem=value_send.at[0],
            recv_sem=value_recv.at[0], device_id=at(1, 0), device_id_type=MESH_ID,
        )

    with scope("near"):
        for flip in range(1, ill_n):
            side_copy(flip).wait_recv()
        near_all().wait_recv()

    with scope("policy"):
        for ag in range(ill_all):
            i, a = divmod(ag, ill_rows)
            own = jnp.broadcast_to(side_in[i, ill_rows, a : a + 1, :], (TILE, liq_rows))
            for h in range(liq_n):
                drifted = own * received(near_in, 0, h, ag) + (1.0 - own) * received(near_in, 0, h, min(ag + 1, ill_all - 1))
                pencil_one[ag * liq_n + h] = lax.rsqrt(drifted)
        for ag in range(ill_all):
            blocks = [pencil_one[ag * liq_n + h] for h in range(liq_n)]
            for h in range(liq_n):
                chosen = interpolate(blocks, received(near_in, 1, h, ag), received(near_in, 2, h, ag))
                found = GROSS_RATE / (chosen * chosen)
                value_two[ag * liq_n + h] = found
                values_in[ag * liq_n + h, own_z, :] = found
                pencil_one[ill_all * liq_n + ag * liq_n + h] = chosen
            if ag % ill_rows == ill_rows - 1:
                for step in far_first:
                    value_copy(ag // ill_rows, step).start()

    lanes = 2 * liq_n
    sub = iota((lanes, liq_rows), 0)
    lane_at = iota((TILE, liq_rows), 1)
    sub_block = jnp.where(sub < liq_n, sub, sub - liq_n).astype(f32)
    lane_row = iota((liq_rows, liq_rows), 0).astype(f32).astype(jnp.bfloat16)
    one = jnp.ones((liq_rows, liq_rows), jnp.bfloat16)
    nil = jnp.zeros((liq_rows, liq_rows), jnp.bfloat16)

    def scattered(steps):
        held = {}
        for ag in range(ill_all):
            for step in steps:
                h = step
                chosen = pencil_one[ill_all * liq_n + ag * liq_n + h]
                share = jnp.clip(received(late_in, 0, h, ag) + SLOPE_GAIN * chosen, 0.0, 1.0)
                mass = received(late_in, 1, h, ag)
                target = received(late_in, 2, h, ag)
                block = jnp.zeros(target.shape, f32)
                for other in range(1, liq_n):
                    block = block + jnp.where(target >= other * liq_rows, 1.0, 0.0)
                held[ag, step] = (mass * share, mass * (1.0 - share), block, target - liq_rows * block)
        for s in range(part):
            for ag in range(ill_all):
                lefts, hots = [], []
                for step in steps:
                    low_t, high_t, hi_t, lo_t = (x[s : s + 1, :] for x in held[ag, step])
                    both = jnp.where(sub < liq_n, low_t, high_t)
                    both = jnp.where(hi_t == sub_block, both, 0.0)
                    rounded = both.astype(jnp.bfloat16).astype(f32)
                    lefts.append(jnp.concatenate([both, both - rounded], axis=0).astype(jnp.bfloat16))
                    place = jnp.broadcast_to(lo_t, (2 * TILE, liq_rows)).astype(jnp.bfloat16)
                    place = jnp.concatenate([place] * (liq_rows // (2 * TILE)), axis=0)
                    hots.append(jnp.where(lane_row == place, one, nil))
                found = lax.dot_general(
                    jnp.concatenate(lefts, axis=1), jnp.concatenate(hots, axis=1), NT, preferred_element_type=f32
                )
                yield s, ag, found[:lanes] + found[lanes:]

    with scope("late"):
        late_all().wait_recv()
    with scope("scatter"):
        totals = []
        for s, ag, total in scattered(range(liq_n)):
            totals.append(total)
            if ag == ill_all - 1:
                to_row = [
                    jnp.broadcast_to(side_in[k // ill_rows, k % ill_rows, s : s + 1, :], (lanes, liq_rows))
                    for k in range(ill_all)
                ]
                for dest in range(ill_all):
                    out = None
                    for k in range(ill_all):
                        here = jnp.where(to_row[k] == dest, totals[k], 0.0)
                        out = here if out is None else out + here
                    placed[pl.ds(dest * part + s, lanes, stride=ill_all * part), :] = out
                totals = []

    with scope("massout"):
        for dest in range(ill_all):
            carried = None
            for h in range(liq_n):
                low = placed[pl.ds((h * ill_all + dest) * part, part), :]
                moved = pltpu.roll(placed[pl.ds(((liq_n + h) * ill_all + dest) * part, part), :], 1, 1)
                total = low + jnp.where(lane_at > 0, moved, 0.0 if carried is None else carried)
                carried = moved
                mass_out[h * ill_all + dest] = total
                depart_out[h * ill_all + dest] = (1.0 - stay[0]) * total

    def mass_copy(step, flip):
        there = at(step, flip)
        return pltpu.make_async_remote_copy(
            src_ref=mass_out.at[pl.ds(there["liq"] * ill_all + there["ill"] * ill_rows, ill_rows)],
            dst_ref=mass_in.at[pl.ds(ill_me * ill_rows, ill_rows), own_z],
            send_sem=mass_send.at[0], recv_sem=mass_recv.at[0], device_id=there, device_id_type=MESH_ID,
        )

    def mass_all():
        span = pl.ds(0, len(peers) * ill_rows)
        return pltpu.make_async_remote_copy(
            src_ref=mass_out.at[span], dst_ref=mass_out.at[span], send_sem=mass_send.at[0],
            recv_sem=mass_recv.at[0], device_id=at(0, 1), device_id_type=MESH_ID,
        )

    def depart_all(count):
        span = pl.ds(0, count * ill_rows)
        return pltpu.make_async_remote_copy(
            src_ref=depart_out.at[span], dst_ref=depart_out.at[span], send_sem=depart_send.at[0],
            recv_sem=depart_recv.at[0], device_id=at(0, 1), device_id_type=MESH_ID,
        )

    def depart_copy(step, i):
        liq_there = peer_of(liq_me, step, liq_n)
        return pltpu.make_async_remote_copy(
            src_ref=depart_out.at[pl.ds(liq_there * ill_all + i * ill_rows, ill_rows)],
            dst_ref=mass_in.at[pl.ds(group, ill_rows), own_z],
            send_sem=depart_send.at[0], recv_sem=depart_recv.at[0],
            device_id={"dur": jnp.maximum(dur_me - 1, 0), "liq": liq_there, "ill": i}, device_id_type=MESH_ID,
        )

    departs = (dur_me > 0) & (ill_me == 0)

    @pl.when(departs)
    def _():
        pl.semaphore_wait(ready_sem, 1)
        for step in range(liq_n - 1, -1, -1):
            for i in range(ill_n):
                depart_copy(step, i).start()

    for step, flip in peers:
        mass_copy(step, flip).start()
    for a in range(ill_rows):
        mass_in[ill_me * ill_rows + a, own_z, :] = mass_out[liq_me * ill_all + ill_me * ill_rows + a]

    def found_copy(flip):
        there = at(0, flip)
        return pltpu.make_async_remote_copy(
            src_ref=found_out.at[flip - 1], dst_ref=found_in.at[flip - 1],
            send_sem=found_send.at[flip - 1], recv_sem=found_recv.at[flip - 1], device_id=there, device_id_type=MESH_ID,
        )

    for flip in range(1, ill_n):
        side_copy(flip).wait_send()
        pair_copy(flip).wait_send()
        pair_copy(flip).wait_recv()
    near_all().wait_send()
    late_all().wait_send()
    with scope("values"):
        value_all().wait_recv()

    with scope("second"):
        expected = []
        for ag in range(ill_all):
            wide = jnp.concatenate([values_in[ag * liq_n + h] for h in range(liq_n)], axis=1)
            expected.append(times(left_two, wide))
        for ag in range(ill_all):
            i, a = divmod(ag, ill_rows)
            own = jnp.broadcast_to(side_in[i, ill_rows, a : a + 1, :], (incomes, liq_rows))
            own = jnp.concatenate([own] * liq_n, axis=1)
            found = lax.rsqrt(own * expected[ag] + (1.0 - own) * expected[min(ag + 1, ill_all - 1)])
            for h in range(liq_n):
                pencil_two[ag * liq_n + h] = found[:, h * liq_rows : (h + 1) * liq_rows]
        for flip in range(ill_n - 1, -1, -1):
            i = peer_of(ill_me, flip, ill_n)
            for a in range(ill_rows):
                for q in range(liq_n):
                    blocks = [
                        pencil_two[(i * ill_rows + a) * liq_n + h, pl.ds(q * part, part), :] for h in range(liq_n)
                    ]
                    found = interpolate(blocks, pair_in[i, q, a], pair_in[i, q, ill_rows + a])
                    if flip:
                        found_out[flip - 1, q * ill_rows + a] = found
                    else:
                        consumption_ref[rows_at(ill_me, a, q), :] = found
            if flip:
                found_copy(flip).start()

    with scope("sends"):
        value_all().wait_send()
        mass_all().wait_send()

        @pl.when(departs)
        def _():
            depart_all(liq_n * ill_n).wait_send()

    with scope("found"):
        for flip in range(1, ill_n):
            found_copy(flip).wait_send()
            found_copy(flip).wait_recv()
            for q in range(liq_n):
                for a in range(ill_rows):
                    consumption_ref[rows_at(peer_of(ill_me, flip, ill_n), a, q), :] = found_in[flip - 1, q * ill_rows + a]

    with scope("mass"):
        mass_all().wait_recv()

        @pl.when(dur_me < dur_n - 1)
        def _():
            depart_all(liq_n).wait_recv()

    with scope("next"):
        settled = []
        for d, a in kinds:
            after = mass_in[(d + 1) * ill_rows + a]
            if d + 1 < durables:
                after = (1.0 - stay[d + 1]) * after
            settled.append(stay[d] * mass_in[d * ill_rows + a] + after)
        high, low = halves_of(transition)
        found = lax.dot_general(
            jnp.concatenate([high, high, low], axis=0), stack_data(jnp.concatenate(settled, axis=1)),
            (((0,), (0,)), ((), ())), preferred_element_type=f32,
        )
        for k, (d, a) in enumerate(kinds):
            for q in range(liq_n):
                next_ref[rows_at(d, a, q), :] = found[q * part : (q + 1) * part, k * liq_rows : (k + 1) * liq_rows]


def store(consumption_ref, next_ref, consumption_hbm, next_hbm, sem):
    copies = [
        pltpu.make_async_copy(consumption_ref, consumption_hbm, sem.at[0]),
        pltpu.make_async_copy(next_ref, next_hbm, sem.at[1]),
    ]
    for copy in copies:
        copy.start()
    for copy in copies:
        copy.wait()


def window_scratch(dims):
    incomes, durables, ill_rows, liq_rows, liq_n, ill_n, dur_n = dims
    f32 = jnp.float32
    rows, plane_rows = incomes * durables * ill_rows, incomes * ill_rows
    block = (rows, liq_rows)
    dma = pltpu.SemaphoreType.DMA
    return [
        pltpu.VMEM(block, f32),
        pltpu.VMEM((incomes, incomes), f32),
        pltpu.VMEM((1, incomes), f32),
        pltpu.VMEM(block, jnp.int32),
        pltpu.VMEM(block, f32),
        pltpu.VMEM(block, f32),
        pltpu.VMEM(block, f32),
        pltpu.VMEM(block, jnp.int32),
        pltpu.VMEM(block, f32),
        pltpu.SMEM((ill_rows,), f32),
        pltpu.SMEM((durables,), f32),
        pltpu.SMEM((durables * ill_rows, incomes), jnp.int32),
        dma((12,)),
        pltpu.VMEM((rows, rows), f32),
        pltpu.VMEM((rows, rows), f32),
        pltpu.VMEM((rows, rows), f32),
        pltpu.VMEM((rows, rows), f32),
        pltpu.VMEM((rows, rows), f32),
        pltpu.VMEM((rows, plane_rows), f32),
        pltpu.VMEM((2,) + block, f32),
        pltpu.VMEM(block, f32),
        pltpu.VMEM((2 * liq_n,) + block, f32),
        pltpu.VMEM(block, f32),
        pltpu.VMEM(block, f32),
        pltpu.VMEM(block, jnp.int32),
        pltpu.VMEM(block, f32),
        pltpu.VMEM((2 * ill_n * liq_n * plane_rows, liq_rows), f32),
        pltpu.VMEM((ill_n * liq_n * rows, liq_rows), f32),
        pltpu.VMEM((durables * (ill_n - 1), liq_n * plane_rows, liq_rows), f32),
        pltpu.VMEM((durables * liq_n, plane_rows, liq_rows), f32),
        pltpu.VMEM((durables * (liq_n - 1), plane_rows, liq_rows), f32),
        pltpu.VMEM(block, f32),
        pltpu.VMEM((plane_rows, liq_rows), f32),
        pltpu.VMEM((plane_rows, liq_rows), f32),
        dma((2,)),
        dma((2,)),
        dma((4 * liq_n,)),
        dma((4 * liq_n,)),
        dma((durables * (ill_n - 1),)),
        dma((durables * (ill_n - 1),)),
        dma((durables * (liq_n - 1),)),
        dma((durables * (liq_n - 1),)),
        dma((1,)),
        dma((1,)),
    ]


def transposed_scratch(dims):
    incomes, durables, ill_rows, liq_rows, liq_n, ill_n, dur_n = dims
    f32 = jnp.float32
    block = (incomes * durables * ill_rows, liq_rows)
    dma = pltpu.SemaphoreType.DMA
    part = incomes // liq_n
    ill_all = ill_n * ill_rows
    tiles = lambda n: pltpu.VMEM((n, part, liq_rows), f32)
    slabs = lambda n: pltpu.VMEM((n, incomes, liq_rows), f32)
    bundles = pltpu.VMEM((durables * liq_n, 3 * ill_rows, part, liq_rows), f32)
    return [
        pltpu.VMEM(block, f32),
        pltpu.VMEM((incomes, incomes), f32),
        pltpu.VMEM((1, incomes), f32),
        pltpu.VMEM(block, jnp.int32),
        pltpu.VMEM(block, f32),
        pltpu.VMEM(block, f32),
        pltpu.VMEM(block, f32),
        pltpu.VMEM(block, jnp.int32),
        pltpu.VMEM(block, f32),
        pltpu.VMEM((durables * ill_rows, incomes), jnp.int32),
        pltpu.SMEM((ill_rows,), f32),
        pltpu.SMEM((durables,), f32),
        dma((12,)),
        bundles,
        bundles,
        bundles,
        bundles,
        pltpu.VMEM((durables, ill_rows + 1, TILE, liq_rows), f32),
        pltpu.VMEM((ill_n, ill_rows + 1, TILE, liq_rows), f32),
        pltpu.VMEM((ill_n, liq_n, 2 * ill_rows, part, liq_rows), f32),
        tiles(2 * ill_all * liq_n),
        tiles(ill_all * liq_n),
        slabs(ill_all * liq_n),
        slabs(ill_all * liq_n),
        pltpu.VMEM((ill_n - 1, liq_n * ill_rows, part, liq_rows), f32),
        pltpu.VMEM((ill_n - 1, liq_n * ill_rows, part, liq_rows), f32),
        pltpu.VMEM((2 * liq_n * ill_all * part, liq_rows), f32),
        tiles(liq_n * ill_all),
        tiles(liq_n * ill_all),
        slabs((durables + 1) * ill_rows),
    ] + [
        dma((n,)) for n in (1, 1, 1, 1, ill_n - 1, ill_n - 1, ill_n - 1, ill_n - 1, 1, 1, ill_n - 1, ill_n - 1, 1, 1, 1, 1)
    ] + [pltpu.SemaphoreType.REGULAR]


def body(
    marginal_value,
    transition,
    discount_shock,
    illiquid_drift,
    durable_keep,
    bracket_index,
    bracket_weight,
    steady_consumption,
    lottery_weight,
    liquid_target,
    illiquid_target,
    population,
):
    shape = marginal_value.shape
    incomes, durables, ill_rows, liq_rows = shape
    liq_n, ill_n, dur_n = (lax.axis_size(name) for name in ("liq", "ill", "dur"))
    rows = incomes * durables * ill_rows
    flat = lambda x: x.reshape(rows, liq_rows)
    anywhere = pl.BlockSpec(memory_space=pl.ANY)
    f32 = jnp.float32
    block = (rows, liq_rows)
    dma = pltpu.SemaphoreType.DMA
    vmem = pl.BlockSpec(memory_space=pltpu.VMEM)
    held = pltpu.VMEM(block, f32)
    result = jax.ShapeDtypeStruct(block, f32)
    dims = (incomes, durables, ill_rows, liq_rows, liq_n, ill_n, dur_n)
    transposed = (
        ill_n == 2 and durables == ill_n and liq_n * 2 == TILE and incomes == liq_n * TILE and ill_rows < TILE
    )
    if transposed:
        step_kernel, scratch, name = transposed_kernel, transposed_scratch(dims), "transposed_window"
    else:
        step_kernel, scratch, name = kernel, window_scratch(dims), "window"
    outs = pl.pallas_call(
        functools.partial(step_kernel, dims),
        out_shape=(held, held),
        in_specs=[anywhere] * 12,
        out_specs=(vmem, vmem),
        scratch_shapes=scratch,
        compiler_params=pltpu.CompilerParams(collective_id=0, has_side_effects=True),
        name=name,
    )(
        flat(marginal_value),
        transition,
        discount_shock.reshape(1, incomes),
        illiquid_drift,
        durable_keep,
        flat(bracket_index),
        flat(bracket_weight),
        flat(steady_consumption),
        flat(lottery_weight),
        flat(liquid_target),
        jnp.transpose(illiquid_target, (1, 2, 0)).reshape(durables * ill_rows, incomes),
        flat(population),
    )
    outs = pl.pallas_call(
        store,
        out_shape=(result, result),
        in_specs=[vmem, vmem],
        out_specs=(anywhere, anywhere),
        scratch_shapes=[dma((2,))],
        name="store",
    )(*(pltpu.with_memory_space_constraint(out, pltpu.VMEM) for out in outs))
    return tuple(out.reshape(shape) for out in outs)


def solution(mesh):
    in_specs = (
        P(None, "dur", "ill", "liq"),
        P(),
        P(),
        P("ill"),
        P("dur"),
        P(None, "dur", "ill", "liq"),
        P(None, "dur", "ill", "liq"),
        P(None, "dur", "ill", "liq"),
        P(None, "dur", "ill", "liq"),
        P(None, "dur", "ill", "liq"),
        P(None, "dur", "ill"),
        P(None, "dur", "ill", "liq"),
    )
    out_specs = (P(None, "dur", "ill", "liq"), P(None, "dur", "ill", "liq"))
    return jax.shard_map(body, mesh=mesh, in_specs=in_specs, out_specs=out_specs, check_vma=False)
```

```python
import contextlib
import functools

import jax
import jax.numpy as jnp
from jax import lax
from jax.experimental import pallas as pl
from jax.experimental.pallas import tpu as pltpu
from jax.sharding import PartitionSpec as P

DISCOUNT = 0.96
GROSS_RATE = 1.01
SLOPE_GAIN = 0.5
HIGHEST_PREC = lax.Precision.HIGHEST
MESH_ID = pl.DeviceIdType.MESH
NT = (((1,), (1,)), ((), ()))
TILE = 8


def scope(name):
    return contextlib.nullcontext()


def split_by(x, n):
    if n & (n - 1) == 0:
        return x >> (n.bit_length() - 1), x & (n - 1)
    return lax.div(x, jnp.int32(n)), lax.rem(x, jnp.int32(n))


def dot(a, b):
    return jnp.dot(a, b, precision=HIGHEST_PREC, preferred_element_type=jnp.float32)


def iota(shape, axis):
    return lax.broadcasted_iota(jnp.int32, shape, axis)


def as_float(flag):
    return jnp.where(flag, jnp.float32(1.0), jnp.float32(0.0))


def peer_of(me, step, n):
    if n & (n - 1):
        return lax.rem(me + step, n)
    out = me
    for bit in range(n.bit_length() - 1):
        if step >> bit & 1:
            out = out + (1 - 2 * lax.rem(lax.div(me, jnp.int32(1 << bit)), jnp.int32(2))) * (1 << bit)
    return out


def kernel(
    dims,
    value_hbm, transition_hbm, shock_hbm, drift_hbm, keep_hbm, index_hbm, weight_hbm,
    steady_hbm, lottery_hbm, target_hbm, ill_target_hbm, population_hbm,
    consumption_ref, next_ref,
    value_ref, transition_ref, shock_ref, index_ref, weight_ref, steady_ref, lottery_ref, target_ref,
    population_ref, drift_ref, keep_ref, ill_target_ref, load_sem,
    first_mat, first_up, second_mat, second_up, next_mat, next_in,
    near_value, value_two, pencil, mass_low, mass_high, target_hi, target_lo,
    placed_rows, terms, terms_in, owner_sum, owner_in, settled, depart, depart_in,
    value_send, value_recv, pencil_send, pencil_recv, terms_send, terms_recv,
    owner_send, owner_recv, depart_send, depart_recv,
):
    incomes, durables, ill_rows, liq_rows, liq_n, ill_n, dur_n = dims
    group = durables * ill_rows
    rows = incomes * group
    half_rows = rows // 2
    plane_rows = incomes * ill_rows
    liq_me, ill_me, dur_me = (lax.axis_index(name) for name in ("liq", "ill", "dur"))
    far_first = range(liq_n - 1, 0, -1)

    barrier = pltpu.get_barrier_semaphore()
    for step in far_first:
        pl.semaphore_signal(barrier, inc=1, device_id={"liq": peer_of(liq_me, step, liq_n)}, device_id_type=MESH_ID)
    for step in range(1, ill_n):
        pl.semaphore_signal(barrier, inc=1, device_id={"ill": peer_of(ill_me, step, ill_n)}, device_id_type=MESH_ID)

    @pl.when(dur_me > 0)
    def _():
        pl.semaphore_signal(barrier, inc=1, device_id={"dur": dur_me - 1}, device_id_type=MESH_ID)

    @pl.when(dur_me < dur_n - 1)
    def _():
        pl.semaphore_signal(barrier, inc=1, device_id={"dur": dur_me + 1}, device_id_type=MESH_ID)

    loads = [
        pltpu.make_async_copy(source, held, load_sem.at[slot])
        for slot, (source, held) in enumerate((
            (transition_hbm, transition_ref), (shock_hbm, shock_ref), (drift_hbm, drift_ref), (value_hbm, value_ref),
            (keep_hbm, keep_ref), (ill_target_hbm, ill_target_ref),
            (index_hbm, index_ref), (weight_hbm, weight_ref), (target_hbm, target_ref),
            (lottery_hbm, lottery_ref), (steady_hbm, steady_ref), (population_hbm, population_ref),
        ))
    ]
    for load in loads:
        load.start()
    for load in loads[:3]:
        load.wait()

    transition = transition_ref[...]
    row_z, row_rest = split_by(iota((rows, rows), 0), group)
    col_z, col_rest = split_by(iota((rows, rows), 1), group)
    row_d, row_a = split_by(row_rest, ill_rows)
    col_d, col_a = split_by(col_rest, ill_rows)
    spread = as_float(split_by(iota((rows, incomes), 0), group)[0] == iota((rows, incomes), 1))
    spread_t = as_float(iota((incomes, rows), 0) == split_by(iota((incomes, rows), 1), group)[0])
    drift = jnp.zeros((rows, rows), jnp.float32)
    for a in range(ill_rows):
        drift = jnp.where(row_a == a, drift_ref[a], drift)
    is_last = as_float(ill_me == ill_n - 1)
    same_d = row_d == col_d
    top_row = row_a == ill_rows - 1
    local = jnp.where(col_a == row_a, drift, 0.0)
    local = local + jnp.where(col_a == row_a + 1, 1.0 - drift, 0.0)
    local = local + jnp.where(top_row & (col_a == ill_rows - 1), is_last * (1.0 - drift), 0.0)
    local = jnp.where(same_d, local, 0.0)
    upper = jnp.where(same_d & top_row & (col_a == 0), (1.0 - is_last) * (1.0 - drift), 0.0)
    constant = jnp.float32(DISCOUNT * GROSS_RATE)
    eye = iota((incomes, incomes), 0) == iota((incomes, incomes), 1)
    scaled = dot(jnp.where(eye, constant * shock_ref[...], 0.0), transition)
    wide = dot(dot(spread, scaled), spread_t)
    first_mat[...] = wide * local
    first_up[...] = wide * upper

    dur_peers = jnp.minimum(dur_me, 1) + jnp.minimum(dur_n - 1 - dur_me, 1)
    pl.semaphore_wait(barrier, liq_n - 1 + ill_n - 1 + dur_peers)

    ill_below = lax.rem(ill_me + ill_n - 1, ill_n)

    def value_copy(k, source):
        return pltpu.make_async_remote_copy(
            src_ref=source, dst_ref=near_value.at[k], send_sem=value_send.at[k],
            recv_sem=value_recv.at[k], device_id={"ill": ill_below}, device_id_type=MESH_ID,
        )

    def pencil_copy(k, half, step):
        slot = (k * 2 + half) * liq_n + step
        part = pencil.at[k * liq_n + liq_me, pl.ds(half * half_rows, half_rows)]
        return pltpu.make_async_remote_copy(
            src_ref=part, dst_ref=part, send_sem=pencil_send.at[slot], recv_sem=pencil_recv.at[slot],
            device_id={"liq": peer_of(liq_me, step, liq_n)}, device_id_type=MESH_ID,
        )

    def pencil_relay(half):
        near, far = (1, 2) if half == 0 else (2, 1)
        slot = (2 + half) * liq_n
        part = pencil.at[liq_n + peer_of(liq_me, near, liq_n), pl.ds(half * half_rows, half_rows)]
        return pltpu.make_async_remote_copy(
            src_ref=part, dst_ref=part, send_sem=pencil_send.at[slot], recv_sem=pencil_recv.at[slot],
            device_id={"liq": peer_of(liq_me, far, liq_n)}, device_id_type=MESH_ID,
        )

    relayed = liq_n == 4
    if relayed:
        early, late = [(0, 1), (1, 2)], [(1, 1), (0, 2)]
    else:
        early, late = [(0, step) for step in far_first], [(1, step) for step in far_first]

    def terms_copy(d, step):
        peer = peer_of(ill_me, step, ill_n)
        slot = d * (ill_n - 1) + step - 1
        return pltpu.make_async_remote_copy(
            src_ref=terms.at[pl.ds((d * ill_n + peer) * (liq_n * plane_rows), liq_n * plane_rows)],
            dst_ref=terms_in.at[slot], send_sem=terms_send.at[slot], recv_sem=terms_recv.at[slot],
            device_id={"ill": peer}, device_id_type=MESH_ID,
        )

    def owner_copy(d, step):
        peer = peer_of(liq_me, step, liq_n)
        slot = d * (liq_n - 1) + step - 1
        return pltpu.make_async_remote_copy(
            src_ref=owner_sum.at[d * liq_n + peer], dst_ref=owner_in.at[slot],
            send_sem=owner_send.at[slot], recv_sem=owner_recv.at[slot],
            device_id={"liq": peer}, device_id_type=MESH_ID,
        )

    loads[3].wait()
    value_copy(0, value_ref).start()
    drifted = dot(first_mat[...], value_ref[...])
    value_copy(0, value_ref).wait_recv()
    drifted = drifted + dot(first_up[...], near_value[0])
    pencil[liq_me] = lax.rsqrt(drifted)
    for half in range(2):
        for step in far_first:
            pencil_copy(0, half, step).start()

    wide = constant * dot(dot(spread, transition), spread_t)
    second_mat[...] = wide * local
    second_up[...] = wide * upper

    for load in loads[4:]:
        load.wait()

    first_d = as_float(dur_me == 0)
    stay = [keep_ref[d] for d in range(durables)]
    stay[0] = first_d + (1.0 - first_d) * stay[0]
    back_d, back_rest = split_by(iota((rows, rows), 1), plane_rows)
    back_a = split_by(back_rest, ill_rows)[1]
    stays = jnp.zeros((rows, rows), jnp.float32)
    for d in range(durables):
        stays = jnp.where(back_d == d, stay[d], stays)
    mix = jnp.where(back_d == row_d, stays, 0.0) + jnp.where(back_d == row_d + 1, 1.0 - stays, 0.0)
    mix = jnp.where(back_a == row_a, mix, 0.0)
    back_z = split_by(split_by(iota((incomes, rows), 1), plane_rows)[1], ill_rows)[0]
    turned = lax.dot_general(spread, transition, NT, precision=HIGHEST_PREC, preferred_element_type=jnp.float32)
    wide = dot(turned, as_float(iota((incomes, rows), 0) == back_z))
    next_mat[...] = wide * mix
    in_z, in_a = split_by(iota((incomes, plane_rows), 1), ill_rows)
    wide = dot(turned, as_float(iota((incomes, plane_rows), 0) == in_z))
    in_row = split_by(iota((rows, plane_rows), 0), group)[1]
    in_row_d, in_row_a = split_by(in_row, ill_rows)
    in_col_a = split_by(iota((rows, plane_rows), 1), ill_rows)[1]
    next_in[...] = jnp.where((in_row_d == durables - 1) & (in_row_a == in_col_a), wide, 0.0)

    def block_of(position):
        block = jnp.zeros(position.shape, jnp.int32)
        for h in range(1, liq_n):
            block = block + jnp.where(position >= h * liq_rows, 1, 0)
        return block, position - block * liq_rows

    target_hi[...], lo = block_of(target_ref[...])
    target_lo[...] = lo.astype(jnp.float32)

    def interpolate(k, tile):
        span = pl.ds(tile * TILE, TILE)
        index = index_ref[span, :]
        low_block, low_lane = block_of(index)
        high_block, high_lane = block_of(index + 1)
        low = high = None
        for h in range(liq_n):
            block = pencil[k * liq_n + h, span, :]
            low_h = jnp.take_along_axis(block, low_lane, axis=1, mode="promise_in_bounds")
            high_h = jnp.take_along_axis(block, high_lane, axis=1, mode="promise_in_bounds")
            low = low_h if h == 0 else jnp.where(low_block == h, low_h, low)
            high = high_h if h == 0 else jnp.where(high_block == h, high_h, high)
        weight = weight_ref[span, :]
        return weight * low + (1.0 - weight) * high

    tiles = rows // TILE
    halves = (range(tiles // 2), range(tiles // 2, tiles))

    def first_policy(half):
        for step in far_first:
            pencil_copy(0, half, step).wait_recv()
        for tile in halves[half]:
            span = pl.ds(tile * TILE, TILE)
            chosen = interpolate(0, tile)
            value_two[span, :] = GROSS_RATE / (chosen * chosen)
            share = jnp.clip(lottery_ref[span, :] + SLOPE_GAIN * (chosen - steady_ref[span, :]), 0.0, 1.0)
            mass = population_ref[span, :]
            mass_low[span, :] = mass * share
            mass_high[span, :] = mass * (1.0 - share)

    lanes = 2 * liq_n
    sub = iota((lanes, liq_rows), 0)
    lane_at = iota((TILE, liq_rows), 1)
    sub_block = jnp.where(sub < liq_n, sub, sub - liq_n)
    lane_row = iota((liq_rows, liq_rows), 0).astype(jnp.float32).astype(jnp.bfloat16)
    one = jnp.ones((liq_rows, liq_rows), jnp.bfloat16)
    nil = jnp.zeros((liq_rows, liq_rows), jnp.bfloat16)
    per_tile = TILE // group

    def scatter_tile(d, tile):
        span = pl.ds(pl.multiple_of(tile * TILE, TILE), TILE)
        low_t, high_t, hi_t, lo_t = mass_low[span, :], mass_high[span, :], target_hi[span, :], target_lo[span, :]
        for zz in range(per_tile):
            z = tile * per_tile + zz
            totals = []
            for a in range(ill_rows):
                k = zz * group + d * ill_rows + a
                both = jnp.where(sub < liq_n, low_t[k : k + 1, :], high_t[k : k + 1, :])
                both = jnp.where(hi_t[k : k + 1, :] == sub_block, both, 0.0)
                rounded = both.astype(jnp.bfloat16).astype(jnp.float32)
                parts = jnp.concatenate([both, both - rounded], axis=0).astype(jnp.bfloat16)
                place = jnp.broadcast_to(lo_t[k : k + 1, :], (2 * TILE, liq_rows)).astype(jnp.bfloat16)
                place = jnp.concatenate([place] * (liq_rows // (2 * TILE)), axis=0)
                hot = jnp.where(lane_row == place, one, nil)
                placed = lax.dot_general(parts, hot, NT, preferred_element_type=jnp.float32)
                placed = placed[:lanes] + placed[lanes:]
                totals.append(placed)
            for dest in range(ill_n * ill_rows):
                out = None
                for a in range(ill_rows):
                    here = as_float(ill_target_ref[d * ill_rows + a, z] == dest) * totals[a]
                    out = here if out is None else out + here
                base = dest // ill_rows * lanes * plane_rows + z * ill_rows + dest % ill_rows
                placed_rows[pl.ds(base, lanes, stride=plane_rows), :] = out

    unroll = tiles // 2

    def scatter(d, half):
        def step(pair, carry):
            for turn in range(unroll):
                scatter_tile(d, halves[half].start + unroll * pair + turn)
            return carry

        lax.fori_loop(0, tiles // 2 // unroll, step, 0)

    def send_terms(d):
        for owner in range(ill_n):
            for piece in range(plane_rows // TILE):
                carried = None
                for h in range(liq_n):
                    low_at = (owner * lanes + h) * plane_rows + piece * TILE
                    low = placed_rows[pl.ds(low_at, TILE), :]
                    moved = pltpu.roll(placed_rows[pl.ds(low_at + liq_n * plane_rows, TILE), :], 1, 1)
                    edge = jnp.where(lane_at > 0, moved, 0.0 if carried is None else carried)
                    carried = moved
                    out_at = ((d * ill_n + owner) * liq_n + h) * plane_rows + piece * TILE
                    terms[pl.ds(out_at, TILE), :] = low + edge
        for step in range(1, ill_n):
            terms_copy(d, step).start()

    def send_owners(d):
        for step in range(1, ill_n):
            terms_copy(d, step).wait_recv()
        for h in range(liq_n):
            start = pl.multiple_of(((d * ill_n + ill_me) * liq_n + h) * plane_rows, TILE)
            total = terms[pl.ds(start, plane_rows), :]
            for step in range(1, ill_n):
                total = total + terms_in[d * (ill_n - 1) + step - 1, pl.ds(h * plane_rows, plane_rows), :]
            owner_sum[d * liq_n + h] = total
        for step in far_first:
            owner_copy(d, step).start()

    def collect(d):
        for step in far_first:
            owner_copy(d, step).wait_recv()
        total = owner_sum[d * liq_n + liq_me]
        for step in range(1, liq_n):
            total = total + owner_in[d * (liq_n - 1) + step - 1]
        settled[pl.ds(d * plane_rows, plane_rows), :] = total
        return total

    def second_policy():
        if relayed:
            for half in range(2):
                pencil_relay(half).wait_recv()
        else:
            for half, step in early:
                pencil_copy(1, half, step).wait_recv()
        for half, step in late:
            pencil_copy(1, half, step).wait_recv()
        for tile in range(tiles):
            consumption_ref[pl.ds(tile * TILE, TILE), :] = interpolate(1, tile)

    first_policy(0)
    scatter(0, 0)
    first_policy(1)
    value_copy(1, value_two).start()
    scatter(0, 1)
    send_terms(0)
    value_copy(1, value_two).wait_recv()
    drifted = dot(second_mat[...], value_two[...]) + dot(second_up[...], near_value[1])
    pencil[liq_n + liq_me] = lax.rsqrt(drifted)
    for half, step in early:
        pencil_copy(1, half, step).start()
    for d in range(1, durables):
        scatter(d, 0)
        if d == 1:
            send_owners(0)
            for half, step in late:
                pencil_copy(1, half, step).start()
        scatter(d, 1)
        send_terms(d)
    for d in range(1, durables):
        send_owners(d)
    if relayed:
        for half, step in early:
            pencil_copy(1, half, step).wait_recv()
        for half in range(2):
            pencil_relay(half).start()

    depart_copy = pltpu.make_async_remote_copy(
        src_ref=depart, dst_ref=depart_in, send_sem=depart_send.at[0], recv_sem=depart_recv.at[0],
        device_id={"dur": jnp.maximum(dur_me - 1, 0)}, device_id_type=MESH_ID,
    )

    depart[...] = (1.0 - stay[0]) * collect(0)

    @pl.when(dur_me > 0)
    def _():
        depart_copy.start()

    for d in range(1, durables):
        collect(d)
    next_ref[...] = dot(next_mat[...], settled[...])
    second_policy()

    @pl.when(dur_me < dur_n - 1)
    def _():
        depart_copy.wait_recv()
        next_ref[...] += dot(next_in[...], depart_in[...])

    value_copy(0, value_ref).wait_send()
    value_copy(1, value_two).wait_send()
    for step in range(1, liq_n):
        for half in range(2):
            pencil_copy(0, half, step).wait_send()
        for d in range(durables):
            owner_copy(d, step).wait_send()
    for half, step in early + late:
        pencil_copy(1, half, step).wait_send()
    if relayed:
        for half in range(2):
            pencil_relay(half).wait_send()
    for step in range(1, ill_n):
        for d in range(durables):
            terms_copy(d, step).wait_send()

    @pl.when(dur_me > 0)
    def _():
        depart_copy.wait_send()


def halves_of(x):
    high = x.astype(jnp.bfloat16)
    return high, (x - high.astype(jnp.float32)).astype(jnp.bfloat16)


def stack_data(x):
    high, low = halves_of(x)
    return jnp.concatenate([high, low, high], axis=0)


def transposed_kernel(
    dims,
    value_hbm, transition_hbm, shock_hbm, drift_hbm, keep_hbm, index_hbm, weight_hbm,
    steady_hbm, lottery_hbm, target_hbm, ill_target_hbm, population_hbm,
    consumption_ref, next_ref,
    value_ref, transition_ref, shock_ref, index_ref, weight_ref, steady_ref, lottery_ref, target_ref,
    population_ref, ill_target_ref, drift_ref, keep_ref, load_sem,
    near_out, near_in, late_out, late_in, side_out, side_in, pair_in,
    pencil_one, value_two, values_in, pencil_two, found_out, found_in, hots, placed, mass_out, depart_out, mass_in,
    near_send, near_recv, late_send, late_recv, goal_send, goal_recv, side_send, side_recv, pair_send, pair_recv,
    value_send, value_recv, found_send, found_recv, mass_send, mass_recv, depart_send, depart_recv, ready_sem,
):
    incomes, durables, ill_rows, liq_rows, liq_n, ill_n, dur_n = dims
    group = durables * ill_rows
    ill_all = ill_n * ill_rows
    part = incomes // liq_n
    per_dest = 3 * ill_rows
    constant = jnp.float32(DISCOUNT * GROSS_RATE)
    f32 = jnp.float32
    liq_me, ill_me, dur_me = (lax.axis_index(name) for name in ("liq", "ill", "dur"))
    far_first = range(liq_n - 1, 0, -1)
    peers = [(step, flip) for step in range(liq_n - 1, -1, -1) for flip in range(ill_n) if step or flip]

    def at(step, flip):
        return {"liq": peer_of(liq_me, step, liq_n), "ill": peer_of(ill_me, flip, ill_n)}

    barrier = pltpu.get_barrier_semaphore()
    for step, flip in peers:
        pl.semaphore_signal(barrier, inc=1, device_id=at(step, flip), device_id_type=MESH_ID)

    @pl.when(dur_me > 0)
    def _():
        pl.semaphore_signal(barrier, inc=1, device_id={"dur": dur_me - 1}, device_id_type=MESH_ID)

    @pl.when(dur_me < dur_n - 1)
    def _():
        pl.semaphore_signal(barrier, inc=1, device_id={"dur": dur_me + 1}, device_id_type=MESH_ID)

    loads = [
        pltpu.make_async_copy(source, held, load_sem.at[slot])
        for slot, (source, held) in enumerate((
            (transition_hbm, transition_ref), (shock_hbm, shock_ref), (value_hbm, value_ref),
            (index_hbm, index_ref), (weight_hbm, weight_ref), (drift_hbm, drift_ref), (ill_target_hbm, ill_target_ref),
            (target_hbm, target_ref), (lottery_hbm, lottery_ref), (steady_hbm, steady_ref),
            (population_hbm, population_ref), (keep_hbm, keep_ref),
        ))
    ]
    for load in loads:
        load.start()

    def rows_at(d, a, z_part):
        return pl.ds(z_part * part * group + d * ill_rows + a, part, stride=group)

    def whole_rows(d, a):
        return pl.ds(d * ill_rows + a, incomes, stride=group)

    kinds = [(d, a) for d in range(durables) for a in range(ill_rows)]
    for load in loads[:2]:
        load.wait()
    transition = transition_ref[...]
    eye = iota((incomes, incomes), 0) == iota((incomes, incomes), 1)
    scaled = dot(jnp.where(eye, constant * shock_ref[...], 0.0), transition)

    def stack_left(x):
        high, low = halves_of(x)
        return jnp.concatenate([high, high, low], axis=1)

    def times(left, x):
        return jnp.dot(left, stack_data(x), preferred_element_type=f32)

    left_one = stack_left(scaled)
    left_two = stack_left(constant * transition)
    loads[2].wait()
    wide = jnp.concatenate([value_ref[whole_rows(d, a), :] for d, a in kinds], axis=1)
    wide = times(left_one, wide)
    for load in loads[3:5]:
        load.wait()
    for k, (d, a) in enumerate(kinds):
        for q in range(liq_n):
            near_out[d * liq_n + q, a] = wide[q * part : (q + 1) * part, k * liq_rows : (k + 1) * liq_rows]
            near_out[d * liq_n + q, ill_rows + a] = index_ref[rows_at(d, a, q), :].astype(f32)
            near_out[d * liq_n + q, 2 * ill_rows + a] = weight_ref[rows_at(d, a, q), :]

    for load in loads[5:7]:
        load.wait()
    column = iota((part, incomes), 1)
    wanted = column == liq_me * part + iota((part, incomes), 0)
    picked = jnp.concatenate(
        [
            jnp.where(wanted, jnp.broadcast_to(ill_target_ref[k : k + 1, :], (part, incomes)), 0)
            for k in range(group)
        ],
        axis=0,
    )
    spread = jnp.dot(
        picked.astype(f32).astype(jnp.bfloat16), jnp.ones((incomes, liq_rows), jnp.bfloat16), preferred_element_type=f32
    )
    row = iota((TILE, liq_rows), 0)
    drifts = jnp.zeros((TILE, liq_rows), f32)
    for a in range(ill_rows):
        drifts = jnp.where(row == a, drift_ref[a], drifts)
    for k, (d, a) in enumerate(kinds):
        side_out[d, a] = spread[k * part : (k + 1) * part]
    for d in range(durables):
        side_out[d, ill_rows] = drifts

    with scope("bar"):
        dur_peers = jnp.minimum(dur_me, 1) + jnp.minimum(dur_n - 1 - dur_me, 1)
        pl.semaphore_wait(barrier, len(peers) + dur_peers)

    @pl.when((dur_me < dur_n - 1) & (ill_me == 0))
    def _():
        pl.semaphore_signal(ready_sem, inc=1, device_id={"dur": dur_me + 1}, device_id_type=MESH_ID)

    def bundle_copy(out_ref, in_ref, send, recv, first, count, step, flip):
        there, kept = at(step, flip), pl.ds(first, count)
        return pltpu.make_async_remote_copy(
            src_ref=out_ref.at[there["ill"] * liq_n + there["liq"], kept],
            dst_ref=in_ref.at[liq_me * ill_n + ill_me, kept],
            send_sem=send.at[0], recv_sem=recv.at[0], device_id=there, device_id_type=MESH_ID,
        )

    def bundle_all(out_ref, in_ref, send, recv, first, count):
        span, kept = pl.ds(0, len(peers)), pl.ds(first, count)
        return pltpu.make_async_remote_copy(
            src_ref=out_ref.at[span, kept], dst_ref=in_ref.at[span, kept], send_sem=send.at[0], recv_sem=recv.at[0],
            device_id=at(0, 1), device_id_type=MESH_ID,
        )

    def near_all():
        return bundle_all(near_out, near_in, near_send, near_recv, 0, per_dest)

    def late_all():
        return bundle_all(late_out, late_in, late_send, late_recv, 0, 2 * ill_rows)

    def goal_all():
        return bundle_all(late_out, late_in, goal_send, goal_recv, 2 * ill_rows, ill_rows)

    def near_copy(step, flip):
        return bundle_copy(near_out, near_in, near_send, near_recv, 0, per_dest, step, flip)

    def late_copy(step, flip):
        return bundle_copy(late_out, late_in, late_send, late_recv, 0, 2 * ill_rows, step, flip)

    def goal_copy(step, flip):
        return bundle_copy(late_out, late_in, goal_send, goal_recv, 2 * ill_rows, ill_rows, step, flip)

    def side_copy(flip):
        there = at(0, flip)
        return pltpu.make_async_remote_copy(
            src_ref=side_out.at[there["ill"]], dst_ref=side_in.at[ill_me],
            send_sem=side_send.at[flip - 1], recv_sem=side_recv.at[flip - 1], device_id=there, device_id_type=MESH_ID,
        )

    def pair_copy(flip):
        there = at(0, flip)
        return pltpu.make_async_remote_copy(
            src_ref=near_out.at[pl.ds(there["ill"] * liq_n, liq_n), pl.ds(ill_rows, 2 * ill_rows)],
            dst_ref=pair_in.at[ill_me], send_sem=pair_send.at[flip - 1], recv_sem=pair_recv.at[flip - 1],
            device_id=there, device_id_type=MESH_ID,
        )

    for step, flip in peers:
        near_copy(step, flip).start()
    for flip in range(1, ill_n):
        side_copy(flip).start()

    for load in loads[7:]:
        load.wait()
    for d, a in kinds:
        for q in range(liq_n):
            span = rows_at(d, a, q)
            late_out[d * liq_n + q, a] = lottery_ref[span, :] - SLOPE_GAIN * steady_ref[span, :]
            late_out[d * liq_n + q, ill_rows + a] = population_ref[span, :]
            late_out[d * liq_n + q, 2 * ill_rows + a] = target_ref[span, :].astype(f32)
    for step, flip in peers:
        goal_copy(step, flip).start()
    for step, flip in peers:
        late_copy(step, flip).start()
    for flip in range(1, ill_n):
        pair_copy(flip).start()

    own_out = ill_me * liq_n + liq_me
    own_in = liq_me * ill_n + ill_me
    for k in range(per_dest):
        near_in[own_in, k] = near_out[own_out, k]
        late_in[own_in, k] = late_out[own_out, k]
    for k in range(ill_rows + 1):
        side_in[ill_me, k] = side_out[ill_me, k]
    for q in range(liq_n):
        for k in range(2 * ill_rows):
            pair_in[ill_me, q, k] = near_out[ill_me * liq_n + q, ill_rows + k]

    @pl.when(dur_me == dur_n - 1)
    def _():
        for a in range(ill_rows):
            mass_in[group + a] = jnp.zeros((incomes, liq_rows), f32)

    stay = [keep_ref[d] for d in range(durables)]
    first_d = as_float(dur_me == 0)
    stay[0] = first_d + (1.0 - first_d) * stay[0]

    def received(ref, kind, h, ag):
        return ref[h * ill_n + ag // ill_rows, kind * ill_rows + ag % ill_rows]

    def interpolate(blocks, index, weight):
        index = index.astype(jnp.int32)
        low_block, low_lane = split_by(index, liq_rows)
        high_block, high_lane = split_by(index + 1, liq_rows)
        low = high = None
        for h, block in enumerate(blocks):
            low_h = jnp.take_along_axis(block, low_lane, axis=1, mode="promise_in_bounds")
            high_h = jnp.take_along_axis(block, high_lane, axis=1, mode="promise_in_bounds")
            low = low_h if h == 0 else jnp.where(low_block == h, low_h, low)
            high = high_h if h == 0 else jnp.where(high_block == h, high_h, high)
        return weight * low + (1.0 - weight) * high

    own_z = pl.ds(pl.multiple_of(liq_me * part, TILE), part)

    ill_pair = peer_of(ill_me, 1, ill_n)
    pieces = [(ill_pair * ill_rows, ill_rows)] + [(ill_me * ill_rows + a, 1) for a in range(ill_rows)]

    def value_copy(k, step):
        start, count = pieces[k]
        span = pl.ds(start * liq_n, count * liq_n)
        return pltpu.make_async_remote_copy(
            src_ref=value_two.at[span], dst_ref=values_in.at[span, own_z], send_sem=value_send.at[0],
            recv_sem=value_recv.at[k], device_id={"liq": peer_of(liq_me, step, liq_n)}, device_id_type=MESH_ID,
        )

    def value_all(k, count):
        span = pl.ds(0, (liq_n - 1) * count)
        return pltpu.make_async_remote_copy(
            src_ref=values_in.at[span], dst_ref=values_in.at[span], send_sem=value_send.at[0],
            recv_sem=value_recv.at[k], device_id=at(1, 0), device_id_type=MESH_ID,
        )

    with scope("near"):
        for flip in range(1, ill_n):
            side_copy(flip).wait_recv()
        near_all().wait_recv()

    with scope("policy"):
        for ag in range(ill_all):
            i, a = divmod(ag, ill_rows)
            own = jnp.broadcast_to(side_in[i, ill_rows, a : a + 1, :], (TILE, liq_rows))
            for h in range(liq_n):
                drifted = own * received(near_in, 0, h, ag) + (1.0 - own) * received(near_in, 0, h, min(ag + 1, ill_all - 1))
                pencil_one[ag * liq_n + h] = lax.rsqrt(drifted)
        for k, (start, count) in enumerate(pieces):
            for turn in range(count):
                i, a = (ill_pair, turn) if k == 0 else (ill_me, k - 1)
                ag = i * ill_rows + a
                blocks = [pencil_one[ag * liq_n + h] for h in range(liq_n)]
                for h in range(liq_n):
                    source = h * ill_n + i
                    chosen = interpolate(blocks, near_in[source, ill_rows + a], near_in[source, 2 * ill_rows + a])
                    found = GROSS_RATE / (chosen * chosen)
                    value_two[ag * liq_n + h] = found
                    values_in[ag * liq_n + h, own_z, :] = found
                    pencil_one[ill_all * liq_n + ag * liq_n + h] = chosen
            for step in far_first:
                value_copy(k, step).start()

    half = liq_rows // 2
    cuts = 2 * liq_n
    sub = iota((cuts, liq_rows), 0).astype(f32)
    lane_at = iota((TILE, liq_rows), 1)
    lane_row = iota((half, liq_rows), 0).astype(f32).astype(jnp.bfloat16)
    one = jnp.ones((half, liq_rows), jnp.bfloat16)
    nil = jnp.zeros((half, liq_rows), jnp.bfloat16)

    with scope("goal"):
        goal_all().wait_recv()
    with scope("hots"):
        cut_at = {}
        for ag in range(ill_all):
            places = []
            for h in range(liq_n):
                target = received(late_in, 2, h, ag)
                cut = jnp.zeros(target.shape, f32)
                for other in range(1, cuts):
                    cut = cut + jnp.where(target >= other * half, 1.0, 0.0)
                cut_at[ag, h] = cut
                places.append(target - half * cut)
            for s in range(part):
                for h in range(liq_n):
                    place = jnp.broadcast_to(places[h][s : s + 1, :], (2 * TILE, liq_rows)).astype(jnp.bfloat16)
                    place = jnp.concatenate([place] * (half // (2 * TILE)), axis=0)
                    hots[s * ill_all + ag, :, h * liq_rows : (h + 1) * liq_rows] = jnp.where(lane_row == place, one, nil)
    with scope("late"):
        late_all().wait_recv()
    with scope("scatter"):
        held = {}
        for ag in range(ill_all):
            for h in range(liq_n):
                chosen = pencil_one[ill_all * liq_n + ag * liq_n + h]
                share = jnp.clip(received(late_in, 0, h, ag) + SLOPE_GAIN * chosen, 0.0, 1.0)
                mass = received(late_in, 1, h, ag)
                held[ag, h] = (mass * share, mass * (1.0 - share), cut_at[ag, h])
        for s in range(part):
            totals, to_row = [], []
            for ag in range(ill_all):
                lefts = []
                for h in range(liq_n):
                    low_t, high_t, cut_t = (x[s : s + 1, :] for x in held[ag, h])
                    here = cut_t == sub
                    both = jnp.concatenate([jnp.where(here, low_t, 0.0), jnp.where(here, high_t, 0.0)], axis=0)
                    first = both.astype(jnp.bfloat16)
                    lefts.append(jnp.concatenate([first, (both - first.astype(f32)).astype(jnp.bfloat16)], axis=0))
                found = lax.dot_general(
                    jnp.concatenate(lefts, axis=1), hots[s * ill_all + ag], NT, preferred_element_type=f32
                )
                totals.append(found[: 2 * cuts] + found[2 * cuts :])
                to_row.append(jnp.broadcast_to(side_in[ag // ill_rows, ag % ill_rows, s : s + 1, :half], (2 * cuts, half)))
            for dest in range(ill_all):
                out = None
                for ag in range(ill_all):
                    here = jnp.where(to_row[ag] == dest, totals[ag], 0.0)
                    out = here if out is None else out + here
                placed[pl.ds(dest * 2 * cuts * part + s, 2 * cuts, stride=part), :half] = out

    with scope("massout"):
        def joined(dest, side, h):
            start = ((dest * 2 + side) * cuts + 2 * h) * part
            return jnp.concatenate(
                [placed[pl.ds(start, part), :half], placed[pl.ds(start + part, part), :half]], axis=1
            )

        for dest in range(ill_all):
            carried = None
            for h in range(liq_n):
                low = joined(dest, 0, h)
                moved = pltpu.roll(joined(dest, 1, h), 1, 1)
                total = low + jnp.where(lane_at > 0, moved, 0.0 if carried is None else carried)
                carried = moved
                mass_out[h * ill_all + dest] = total
                depart_out[h * ill_all + dest] = (1.0 - stay[0]) * total

    def mass_copy(step, flip):
        there = at(step, flip)
        return pltpu.make_async_remote_copy(
            src_ref=mass_out.at[pl.ds(there["liq"] * ill_all + there["ill"] * ill_rows, ill_rows)],
            dst_ref=mass_in.at[pl.ds(ill_me * ill_rows, ill_rows), own_z],
            send_sem=mass_send.at[0], recv_sem=mass_recv.at[0], device_id=there, device_id_type=MESH_ID,
        )

    def mass_all():
        span = pl.ds(0, len(peers) * ill_rows)
        return pltpu.make_async_remote_copy(
            src_ref=mass_out.at[span], dst_ref=mass_out.at[span], send_sem=mass_send.at[0],
            recv_sem=mass_recv.at[0], device_id=at(0, 1), device_id_type=MESH_ID,
        )

    def depart_all(count):
        span = pl.ds(0, count * ill_rows)
        return pltpu.make_async_remote_copy(
            src_ref=depart_out.at[span], dst_ref=depart_out.at[span], send_sem=depart_send.at[0],
            recv_sem=depart_recv.at[0], device_id=at(0, 1), device_id_type=MESH_ID,
        )

    def depart_copy(step, i):
        liq_there = peer_of(liq_me, step, liq_n)
        return pltpu.make_async_remote_copy(
            src_ref=depart_out.at[pl.ds(liq_there * ill_all + i * ill_rows, ill_rows)],
            dst_ref=mass_in.at[pl.ds(group, ill_rows), own_z],
            send_sem=depart_send.at[0], recv_sem=depart_recv.at[0],
            device_id={"dur": jnp.maximum(dur_me - 1, 0), "liq": liq_there, "ill": i}, device_id_type=MESH_ID,
        )

    departs = (dur_me > 0) & (ill_me == 0)

    @pl.when(departs)
    def _():
        pl.semaphore_wait(ready_sem, 1)
        for step in range(liq_n - 1, -1, -1):
            for i in range(ill_n):
                depart_copy(step, i).start()

    for step, flip in peers:
        mass_copy(step, flip).start()
    for a in range(ill_rows):
        mass_in[ill_me * ill_rows + a, own_z, :] = mass_out[liq_me * ill_all + ill_me * ill_rows + a]

    def found_copy(flip):
        there = at(0, flip)
        return pltpu.make_async_remote_copy(
            src_ref=found_out.at[flip - 1], dst_ref=found_in.at[flip - 1],
            send_sem=found_send.at[flip - 1], recv_sem=found_recv.at[flip - 1], device_id=there, device_id_type=MESH_ID,
        )

    for flip in range(1, ill_n):
        side_copy(flip).wait_send()
        pair_copy(flip).wait_send()
        pair_copy(flip).wait_recv()
    near_all().wait_send()
    late_all().wait_send()
    goal_all().wait_send()
    is_last = ill_me == ill_n - 1

    def expect(ag):
        wide = jnp.concatenate([values_in[ag * liq_n + h] for h in range(liq_n)], axis=1)
        return times(left_two, wide)

    def consume(i, expected, store_tile):
        for a in range(ill_rows):
            own = jnp.broadcast_to(side_in[i, ill_rows, a : a + 1, :], (incomes, liq_rows))
            own = jnp.concatenate([own] * liq_n, axis=1)
            found = lax.rsqrt(own * expected[a] + (1.0 - own) * expected[a + 1])
            for h in range(liq_n):
                pencil_two[a * liq_n + h] = found[:, h * liq_rows : (h + 1) * liq_rows]
        for a in range(ill_rows):
            for q in range(liq_n):
                blocks = [pencil_two[a * liq_n + h, pl.ds(q * part, part), :] for h in range(liq_n)]
                store_tile(a, q, interpolate(blocks, pair_in[i, q, a], pair_in[i, q, ill_rows + a]))

    def store_found(a, q, found):
        found_out[0, q * ill_rows + a] = found

    def store_own(a, q, found):
        consumption_ref[rows_at(ill_me, a, q), :] = found

    with scope("values"):
        value_all(0, ill_rows).wait_recv()

        @pl.when(is_last)
        def _():
            value_all(1, 1).wait_recv()

    with scope("second_a"):
        above = jnp.minimum(ill_pair * ill_rows + ill_rows, ill_all - 1)
        expected = [expect(ill_pair * ill_rows + a) for a in range(ill_rows)]
        lowest = expected[0]
        consume(ill_pair, expected + [expect(above)], store_found)
        found_copy(1).start()

    with scope("values_b"):
        @pl.when(jnp.logical_not(is_last))
        def _():
            value_all(1, 1).wait_recv()

        for a in range(1, ill_rows):
            value_all(1 + a, 1).wait_recv()

    with scope("second_b"):
        expected = [expect(ill_me * ill_rows + a) for a in range(ill_rows)]
        expected.append(jnp.where(is_last, expected[-1], lowest))
        consume(ill_me, expected, store_own)

    with scope("sends"):
        value_all(0, ill_all).wait_send()
        mass_all().wait_send()

        @pl.when(departs)
        def _():
            depart_all(liq_n * ill_n).wait_send()

    with scope("found"):
        for flip in range(1, ill_n):
            found_copy(flip).wait_send()
            found_copy(flip).wait_recv()
            for q in range(liq_n):
                for a in range(ill_rows):
                    consumption_ref[rows_at(peer_of(ill_me, flip, ill_n), a, q), :] = found_in[flip - 1, q * ill_rows + a]

    with scope("mass"):
        mass_all().wait_recv()

        @pl.when(dur_me < dur_n - 1)
        def _():
            depart_all(liq_n).wait_recv()

    with scope("next"):
        settled = []
        for d, a in kinds:
            after = mass_in[(d + 1) * ill_rows + a]
            if d + 1 < durables:
                after = (1.0 - stay[d + 1]) * after
            settled.append(stay[d] * mass_in[d * ill_rows + a] + after)
        high, low = halves_of(transition)
        found = lax.dot_general(
            jnp.concatenate([high, high, low], axis=0), stack_data(jnp.concatenate(settled, axis=1)),
            (((0,), (0,)), ((), ())), preferred_element_type=f32,
        )
        for k, (d, a) in enumerate(kinds):
            for q in range(liq_n):
                next_ref[rows_at(d, a, q), :] = found[q * part : (q + 1) * part, k * liq_rows : (k + 1) * liq_rows]


def store(consumption_ref, next_ref, consumption_hbm, next_hbm, sem):
    copies = [
        pltpu.make_async_copy(consumption_ref, consumption_hbm, sem.at[0]),
        pltpu.make_async_copy(next_ref, next_hbm, sem.at[1]),
    ]
    for copy in copies:
        copy.start()
    for copy in copies:
        copy.wait()


def window_scratch(dims):
    incomes, durables, ill_rows, liq_rows, liq_n, ill_n, dur_n = dims
    f32 = jnp.float32
    rows, plane_rows = incomes * durables * ill_rows, incomes * ill_rows
    block = (rows, liq_rows)
    dma = pltpu.SemaphoreType.DMA
    return [
        pltpu.VMEM(block, f32),
        pltpu.VMEM((incomes, incomes), f32),
        pltpu.VMEM((1, incomes), f32),
        pltpu.VMEM(block, jnp.int32),
        pltpu.VMEM(block, f32),
        pltpu.VMEM(block, f32),
        pltpu.VMEM(block, f32),
        pltpu.VMEM(block, jnp.int32),
        pltpu.VMEM(block, f32),
        pltpu.SMEM((ill_rows,), f32),
        pltpu.SMEM((durables,), f32),
        pltpu.SMEM((durables * ill_rows, incomes), jnp.int32),
        dma((12,)),
        pltpu.VMEM((rows, rows), f32),
        pltpu.VMEM((rows, rows), f32),
        pltpu.VMEM((rows, rows), f32),
        pltpu.VMEM((rows, rows), f32),
        pltpu.VMEM((rows, rows), f32),
        pltpu.VMEM((rows, plane_rows), f32),
        pltpu.VMEM((2,) + block, f32),
        pltpu.VMEM(block, f32),
        pltpu.VMEM((2 * liq_n,) + block, f32),
        pltpu.VMEM(block, f32),
        pltpu.VMEM(block, f32),
        pltpu.VMEM(block, jnp.int32),
        pltpu.VMEM(block, f32),
        pltpu.VMEM((2 * ill_n * liq_n * plane_rows, liq_rows), f32),
        pltpu.VMEM((ill_n * liq_n * rows, liq_rows), f32),
        pltpu.VMEM((durables * (ill_n - 1), liq_n * plane_rows, liq_rows), f32),
        pltpu.VMEM((durables * liq_n, plane_rows, liq_rows), f32),
        pltpu.VMEM((durables * (liq_n - 1), plane_rows, liq_rows), f32),
        pltpu.VMEM(block, f32),
        pltpu.VMEM((plane_rows, liq_rows), f32),
        pltpu.VMEM((plane_rows, liq_rows), f32),
        dma((2,)),
        dma((2,)),
        dma((4 * liq_n,)),
        dma((4 * liq_n,)),
        dma((durables * (ill_n - 1),)),
        dma((durables * (ill_n - 1),)),
        dma((durables * (liq_n - 1),)),
        dma((durables * (liq_n - 1),)),
        dma((1,)),
        dma((1,)),
    ]


def transposed_scratch(dims):
    incomes, durables, ill_rows, liq_rows, liq_n, ill_n, dur_n = dims
    f32 = jnp.float32
    block = (incomes * durables * ill_rows, liq_rows)
    dma = pltpu.SemaphoreType.DMA
    part = incomes // liq_n
    ill_all = ill_n * ill_rows
    tiles = lambda n: pltpu.VMEM((n, part, liq_rows), f32)
    slabs = lambda n: pltpu.VMEM((n, incomes, liq_rows), f32)
    bundles = pltpu.VMEM((durables * liq_n, 3 * ill_rows, part, liq_rows), f32)
    return [
        pltpu.VMEM(block, f32),
        pltpu.VMEM((incomes, incomes), f32),
        pltpu.VMEM((1, incomes), f32),
        pltpu.VMEM(block, jnp.int32),
        pltpu.VMEM(block, f32),
        pltpu.VMEM(block, f32),
        pltpu.VMEM(block, f32),
        pltpu.VMEM(block, jnp.int32),
        pltpu.VMEM(block, f32),
        pltpu.VMEM((durables * ill_rows, incomes), jnp.int32),
        pltpu.SMEM((ill_rows,), f32),
        pltpu.SMEM((durables,), f32),
        dma((12,)),
        bundles,
        bundles,
        bundles,
        bundles,
        pltpu.VMEM((durables, ill_rows + 1, TILE, liq_rows), f32),
        pltpu.VMEM((ill_n, ill_rows + 1, TILE, liq_rows), f32),
        pltpu.VMEM((ill_n, liq_n, 2 * ill_rows, part, liq_rows), f32),
        tiles(2 * ill_all * liq_n),
        tiles(ill_all * liq_n),
        slabs(ill_all * liq_n),
        slabs(ill_rows * liq_n),
        pltpu.VMEM((ill_n - 1, liq_n * ill_rows, part, liq_rows), f32),
        pltpu.VMEM((ill_n - 1, liq_n * ill_rows, part, liq_rows), f32),
        pltpu.VMEM((part * ill_all, liq_rows // 2, liq_n * liq_rows), jnp.bfloat16),
        pltpu.VMEM((4 * liq_n * ill_all * part, liq_rows), f32),
        tiles(liq_n * ill_all),
        tiles(liq_n * ill_all),
        slabs((durables + 1) * ill_rows),
    ] + [
        dma((n,)) for n in (1, 1, 1, 1, 1, 1, 1, 1, 1, 1, 1, ill_rows + 1, 1, 1, 1, 1, 1, 1)
    ] + [pltpu.SemaphoreType.REGULAR]


def body(
    marginal_value,
    transition,
    discount_shock,
    illiquid_drift,
    durable_keep,
    bracket_index,
    bracket_weight,
    steady_consumption,
    lottery_weight,
    liquid_target,
    illiquid_target,
    population,
):
    shape = marginal_value.shape
    incomes, durables, ill_rows, liq_rows = shape
    liq_n, ill_n, dur_n = (lax.axis_size(name) for name in ("liq", "ill", "dur"))
    rows = incomes * durables * ill_rows
    flat = lambda x: x.reshape(rows, liq_rows)
    anywhere = pl.BlockSpec(memory_space=pl.ANY)
    f32 = jnp.float32
    block = (rows, liq_rows)
    dma = pltpu.SemaphoreType.DMA
    vmem = pl.BlockSpec(memory_space=pltpu.VMEM)
    held = pltpu.VMEM(block, f32)
    result = jax.ShapeDtypeStruct(block, f32)
    dims = (incomes, durables, ill_rows, liq_rows, liq_n, ill_n, dur_n)
    transposed = (
        ill_n == 2 and durables == ill_n and liq_n * 2 == TILE and incomes == liq_n * TILE and ill_rows < TILE
    )
    if transposed:
        step_kernel, scratch, name = transposed_kernel, transposed_scratch(dims), "transposed_window"
    else:
        step_kernel, scratch, name = kernel, window_scratch(dims), "window"
    outs = pl.pallas_call(
        functools.partial(step_kernel, dims),
        out_shape=(held, held),
        in_specs=[anywhere] * 12,
        out_specs=(vmem, vmem),
        scratch_shapes=scratch,
        compiler_params=pltpu.CompilerParams(collective_id=0, has_side_effects=True),
        name=name,
    )(
        flat(marginal_value),
        transition,
        discount_shock.reshape(1, incomes),
        illiquid_drift,
        durable_keep,
        flat(bracket_index),
        flat(bracket_weight),
        flat(steady_consumption),
        flat(lottery_weight),
        flat(liquid_target),
        jnp.transpose(illiquid_target, (1, 2, 0)).reshape(durables * ill_rows, incomes),
        flat(population),
    )
    outs = pl.pallas_call(
        store,
        out_shape=(result, result),
        in_specs=[vmem, vmem],
        out_specs=(anywhere, anywhere),
        scratch_shapes=[dma((2,))],
        name="store",
    )(*(pltpu.with_memory_space_constraint(out, pltpu.VMEM) for out in outs))
    return tuple(out.reshape(shape) for out in outs)


def solution(mesh):
    in_specs = (
        P(None, "dur", "ill", "liq"),
        P(),
        P(),
        P("ill"),
        P("dur"),
        P(None, "dur", "ill", "liq"),
        P(None, "dur", "ill", "liq"),
        P(None, "dur", "ill", "liq"),
        P(None, "dur", "ill", "liq"),
        P(None, "dur", "ill", "liq"),
        P(None, "dur", "ill"),
        P(None, "dur", "ill", "liq"),
    )
    out_specs = (P(None, "dur", "ill", "liq"), P(None, "dur", "ill", "liq"))
    return jax.shard_map(body, mesh=mesh, in_specs=in_specs, out_specs=out_specs, check_vma=False)
```

```python
import contextlib
import functools

import jax
import jax.numpy as jnp
from jax import lax
from jax.experimental import pallas as pl
from jax.experimental.pallas import tpu as pltpu
from jax.sharding import PartitionSpec as P

DISCOUNT = 0.96
GROSS_RATE = 1.01
SLOPE_GAIN = 0.5
HIGHEST_PREC = lax.Precision.HIGHEST
MESH_ID = pl.DeviceIdType.MESH
NT = (((1,), (1,)), ((), ()))
TILE = 8


def scope(name):
    return contextlib.nullcontext()


def split_by(x, n):
    if n & (n - 1) == 0:
        return x >> (n.bit_length() - 1), x & (n - 1)
    return lax.div(x, jnp.int32(n)), lax.rem(x, jnp.int32(n))


def dot(a, b):
    return jnp.dot(a, b, precision=HIGHEST_PREC, preferred_element_type=jnp.float32)


def iota(shape, axis):
    return lax.broadcasted_iota(jnp.int32, shape, axis)


def as_float(flag):
    return jnp.where(flag, jnp.float32(1.0), jnp.float32(0.0))


def peer_of(me, step, n):
    if n & (n - 1):
        return lax.rem(me + step, n)
    out = me
    for bit in range(n.bit_length() - 1):
        if step >> bit & 1:
            out = out + (1 - 2 * lax.rem(lax.div(me, jnp.int32(1 << bit)), jnp.int32(2))) * (1 << bit)
    return out


def kernel(
    dims,
    value_hbm, transition_hbm, shock_hbm, drift_hbm, keep_hbm, index_hbm, weight_hbm,
    steady_hbm, lottery_hbm, target_hbm, ill_target_hbm, population_hbm,
    consumption_ref, next_ref,
    value_ref, transition_ref, shock_ref, index_ref, weight_ref, steady_ref, lottery_ref, target_ref,
    population_ref, drift_ref, keep_ref, ill_target_ref, load_sem,
    first_mat, first_up, second_mat, second_up, next_mat, next_in,
    near_value, value_two, pencil, mass_low, mass_high, target_hi, target_lo,
    placed_rows, terms, terms_in, owner_sum, owner_in, settled, depart, depart_in,
    value_send, value_recv, pencil_send, pencil_recv, terms_send, terms_recv,
    owner_send, owner_recv, depart_send, depart_recv,
):
    incomes, durables, ill_rows, liq_rows, liq_n, ill_n, dur_n = dims
    group = durables * ill_rows
    rows = incomes * group
    half_rows = rows // 2
    plane_rows = incomes * ill_rows
    liq_me, ill_me, dur_me = (lax.axis_index(name) for name in ("liq", "ill", "dur"))
    far_first = range(liq_n - 1, 0, -1)

    barrier = pltpu.get_barrier_semaphore()
    for step in far_first:
        pl.semaphore_signal(barrier, inc=1, device_id={"liq": peer_of(liq_me, step, liq_n)}, device_id_type=MESH_ID)
    for step in range(1, ill_n):
        pl.semaphore_signal(barrier, inc=1, device_id={"ill": peer_of(ill_me, step, ill_n)}, device_id_type=MESH_ID)

    @pl.when(dur_me > 0)
    def _():
        pl.semaphore_signal(barrier, inc=1, device_id={"dur": dur_me - 1}, device_id_type=MESH_ID)

    @pl.when(dur_me < dur_n - 1)
    def _():
        pl.semaphore_signal(barrier, inc=1, device_id={"dur": dur_me + 1}, device_id_type=MESH_ID)

    loads = [
        pltpu.make_async_copy(source, held, load_sem.at[slot])
        for slot, (source, held) in enumerate((
            (transition_hbm, transition_ref), (shock_hbm, shock_ref), (drift_hbm, drift_ref), (value_hbm, value_ref),
            (keep_hbm, keep_ref), (ill_target_hbm, ill_target_ref),
            (index_hbm, index_ref), (weight_hbm, weight_ref), (target_hbm, target_ref),
            (lottery_hbm, lottery_ref), (steady_hbm, steady_ref), (population_hbm, population_ref),
        ))
    ]
    for load in loads:
        load.start()
    for load in loads[:3]:
        load.wait()

    transition = transition_ref[...]
    row_z, row_rest = split_by(iota((rows, rows), 0), group)
    col_z, col_rest = split_by(iota((rows, rows), 1), group)
    row_d, row_a = split_by(row_rest, ill_rows)
    col_d, col_a = split_by(col_rest, ill_rows)
    spread = as_float(split_by(iota((rows, incomes), 0), group)[0] == iota((rows, incomes), 1))
    spread_t = as_float(iota((incomes, rows), 0) == split_by(iota((incomes, rows), 1), group)[0])
    drift = jnp.zeros((rows, rows), jnp.float32)
    for a in range(ill_rows):
        drift = jnp.where(row_a == a, drift_ref[a], drift)
    is_last = as_float(ill_me == ill_n - 1)
    same_d = row_d == col_d
    top_row = row_a == ill_rows - 1
    local = jnp.where(col_a == row_a, drift, 0.0)
    local = local + jnp.where(col_a == row_a + 1, 1.0 - drift, 0.0)
    local = local + jnp.where(top_row & (col_a == ill_rows - 1), is_last * (1.0 - drift), 0.0)
    local = jnp.where(same_d, local, 0.0)
    upper = jnp.where(same_d & top_row & (col_a == 0), (1.0 - is_last) * (1.0 - drift), 0.0)
    constant = jnp.float32(DISCOUNT * GROSS_RATE)
    eye = iota((incomes, incomes), 0) == iota((incomes, incomes), 1)
    scaled = dot(jnp.where(eye, constant * shock_ref[...], 0.0), transition)
    wide = dot(dot(spread, scaled), spread_t)
    first_mat[...] = wide * local
    first_up[...] = wide * upper

    dur_peers = jnp.minimum(dur_me, 1) + jnp.minimum(dur_n - 1 - dur_me, 1)
    pl.semaphore_wait(barrier, liq_n - 1 + ill_n - 1 + dur_peers)

    ill_below = lax.rem(ill_me + ill_n - 1, ill_n)

    def value_copy(k, source):
        return pltpu.make_async_remote_copy(
            src_ref=source, dst_ref=near_value.at[k], send_sem=value_send.at[k],
            recv_sem=value_recv.at[k], device_id={"ill": ill_below}, device_id_type=MESH_ID,
        )

    def pencil_copy(k, half, step):
        slot = (k * 2 + half) * liq_n + step
        part = pencil.at[k * liq_n + liq_me, pl.ds(half * half_rows, half_rows)]
        return pltpu.make_async_remote_copy(
            src_ref=part, dst_ref=part, send_sem=pencil_send.at[slot], recv_sem=pencil_recv.at[slot],
            device_id={"liq": peer_of(liq_me, step, liq_n)}, device_id_type=MESH_ID,
        )

    def pencil_relay(half):
        near, far = (1, 2) if half == 0 else (2, 1)
        slot = (2 + half) * liq_n
        part = pencil.at[liq_n + peer_of(liq_me, near, liq_n), pl.ds(half * half_rows, half_rows)]
        return pltpu.make_async_remote_copy(
            src_ref=part, dst_ref=part, send_sem=pencil_send.at[slot], recv_sem=pencil_recv.at[slot],
            device_id={"liq": peer_of(liq_me, far, liq_n)}, device_id_type=MESH_ID,
        )

    relayed = liq_n == 4
    if relayed:
        early, late = [(0, 1), (1, 2)], [(1, 1), (0, 2)]
    else:
        early, late = [(0, step) for step in far_first], [(1, step) for step in far_first]

    def terms_copy(d, step):
        peer = peer_of(ill_me, step, ill_n)
        slot = d * (ill_n - 1) + step - 1
        return pltpu.make_async_remote_copy(
            src_ref=terms.at[pl.ds((d * ill_n + peer) * (liq_n * plane_rows), liq_n * plane_rows)],
            dst_ref=terms_in.at[slot], send_sem=terms_send.at[slot], recv_sem=terms_recv.at[slot],
            device_id={"ill": peer}, device_id_type=MESH_ID,
        )

    def owner_copy(d, step):
        peer = peer_of(liq_me, step, liq_n)
        slot = d * (liq_n - 1) + step - 1
        return pltpu.make_async_remote_copy(
            src_ref=owner_sum.at[d * liq_n + peer], dst_ref=owner_in.at[slot],
            send_sem=owner_send.at[slot], recv_sem=owner_recv.at[slot],
            device_id={"liq": peer}, device_id_type=MESH_ID,
        )

    loads[3].wait()
    value_copy(0, value_ref).start()
    drifted = dot(first_mat[...], value_ref[...])
    value_copy(0, value_ref).wait_recv()
    drifted = drifted + dot(first_up[...], near_value[0])
    pencil[liq_me] = lax.rsqrt(drifted)
    for half in range(2):
        for step in far_first:
            pencil_copy(0, half, step).start()

    wide = constant * dot(dot(spread, transition), spread_t)
    second_mat[...] = wide * local
    second_up[...] = wide * upper

    for load in loads[4:]:
        load.wait()

    first_d = as_float(dur_me == 0)
    stay = [keep_ref[d] for d in range(durables)]
    stay[0] = first_d + (1.0 - first_d) * stay[0]
    back_d, back_rest = split_by(iota((rows, rows), 1), plane_rows)
    back_a = split_by(back_rest, ill_rows)[1]
    stays = jnp.zeros((rows, rows), jnp.float32)
    for d in range(durables):
        stays = jnp.where(back_d == d, stay[d], stays)
    mix = jnp.where(back_d == row_d, stays, 0.0) + jnp.where(back_d == row_d + 1, 1.0 - stays, 0.0)
    mix = jnp.where(back_a == row_a, mix, 0.0)
    back_z = split_by(split_by(iota((incomes, rows), 1), plane_rows)[1], ill_rows)[0]
    turned = lax.dot_general(spread, transition, NT, precision=HIGHEST_PREC, preferred_element_type=jnp.float32)
    wide = dot(turned, as_float(iota((incomes, rows), 0) == back_z))
    next_mat[...] = wide * mix
    in_z, in_a = split_by(iota((incomes, plane_rows), 1), ill_rows)
    wide = dot(turned, as_float(iota((incomes, plane_rows), 0) == in_z))
    in_row = split_by(iota((rows, plane_rows), 0), group)[1]
    in_row_d, in_row_a = split_by(in_row, ill_rows)
    in_col_a = split_by(iota((rows, plane_rows), 1), ill_rows)[1]
    next_in[...] = jnp.where((in_row_d == durables - 1) & (in_row_a == in_col_a), wide, 0.0)

    def block_of(position):
        block = jnp.zeros(position.shape, jnp.int32)
        for h in range(1, liq_n):
            block = block + jnp.where(position >= h * liq_rows, 1, 0)
        return block, position - block * liq_rows

    target_hi[...], lo = block_of(target_ref[...])
    target_lo[...] = lo.astype(jnp.float32)

    def interpolate(k, tile):
        span = pl.ds(tile * TILE, TILE)
        index = index_ref[span, :]
        low_block, low_lane = block_of(index)
        high_block, high_lane = block_of(index + 1)
        low = high = None
        for h in range(liq_n):
            block = pencil[k * liq_n + h, span, :]
            low_h = jnp.take_along_axis(block, low_lane, axis=1, mode="promise_in_bounds")
            high_h = jnp.take_along_axis(block, high_lane, axis=1, mode="promise_in_bounds")
            low = low_h if h == 0 else jnp.where(low_block == h, low_h, low)
            high = high_h if h == 0 else jnp.where(high_block == h, high_h, high)
        weight = weight_ref[span, :]
        return weight * low + (1.0 - weight) * high

    tiles = rows // TILE
    halves = (range(tiles // 2), range(tiles // 2, tiles))

    def first_policy(half):
        for step in far_first:
            pencil_copy(0, half, step).wait_recv()
        for tile in halves[half]:
            span = pl.ds(tile * TILE, TILE)
            chosen = interpolate(0, tile)
            value_two[span, :] = GROSS_RATE / (chosen * chosen)
            share = jnp.clip(lottery_ref[span, :] + SLOPE_GAIN * (chosen - steady_ref[span, :]), 0.0, 1.0)
            mass = population_ref[span, :]
            mass_low[span, :] = mass * share
            mass_high[span, :] = mass * (1.0 - share)

    lanes = 2 * liq_n
    sub = iota((lanes, liq_rows), 0)
    lane_at = iota((TILE, liq_rows), 1)
    sub_block = jnp.where(sub < liq_n, sub, sub - liq_n)
    lane_row = iota((liq_rows, liq_rows), 0).astype(jnp.float32).astype(jnp.bfloat16)
    one = jnp.ones((liq_rows, liq_rows), jnp.bfloat16)
    nil = jnp.zeros((liq_rows, liq_rows), jnp.bfloat16)
    per_tile = TILE // group

    def scatter_tile(d, tile):
        span = pl.ds(pl.multiple_of(tile * TILE, TILE), TILE)
        low_t, high_t, hi_t, lo_t = mass_low[span, :], mass_high[span, :], target_hi[span, :], target_lo[span, :]
        for zz in range(per_tile):
            z = tile * per_tile + zz
            totals = []
            for a in range(ill_rows):
                k = zz * group + d * ill_rows + a
                both = jnp.where(sub < liq_n, low_t[k : k + 1, :], high_t[k : k + 1, :])
                both = jnp.where(hi_t[k : k + 1, :] == sub_block, both, 0.0)
                rounded = both.astype(jnp.bfloat16).astype(jnp.float32)
                parts = jnp.concatenate([both, both - rounded], axis=0).astype(jnp.bfloat16)
                place = jnp.broadcast_to(lo_t[k : k + 1, :], (2 * TILE, liq_rows)).astype(jnp.bfloat16)
                place = jnp.concatenate([place] * (liq_rows // (2 * TILE)), axis=0)
                hot = jnp.where(lane_row == place, one, nil)
                placed = lax.dot_general(parts, hot, NT, preferred_element_type=jnp.float32)
                placed = placed[:lanes] + placed[lanes:]
                totals.append(placed)
            for dest in range(ill_n * ill_rows):
                out = None
                for a in range(ill_rows):
                    here = as_float(ill_target_ref[d * ill_rows + a, z] == dest) * totals[a]
                    out = here if out is None else out + here
                base = dest // ill_rows * lanes * plane_rows + z * ill_rows + dest % ill_rows
                placed_rows[pl.ds(base, lanes, stride=plane_rows), :] = out

    unroll = tiles // 2

    def scatter(d, half):
        def step(pair, carry):
            for turn in range(unroll):
                scatter_tile(d, halves[half].start + unroll * pair + turn)
            return carry

        lax.fori_loop(0, tiles // 2 // unroll, step, 0)

    def send_terms(d):
        for owner in range(ill_n):
            for piece in range(plane_rows // TILE):
                carried = None
                for h in range(liq_n):
                    low_at = (owner * lanes + h) * plane_rows + piece * TILE
                    low = placed_rows[pl.ds(low_at, TILE), :]
                    moved = pltpu.roll(placed_rows[pl.ds(low_at + liq_n * plane_rows, TILE), :], 1, 1)
                    edge = jnp.where(lane_at > 0, moved, 0.0 if carried is None else carried)
                    carried = moved
                    out_at = ((d * ill_n + owner) * liq_n + h) * plane_rows + piece * TILE
                    terms[pl.ds(out_at, TILE), :] = low + edge
        for step in range(1, ill_n):
            terms_copy(d, step).start()

    def send_owners(d):
        for step in range(1, ill_n):
            terms_copy(d, step).wait_recv()
        for h in range(liq_n):
            start = pl.multiple_of(((d * ill_n + ill_me) * liq_n + h) * plane_rows, TILE)
            total = terms[pl.ds(start, plane_rows), :]
            for step in range(1, ill_n):
                total = total + terms_in[d * (ill_n - 1) + step - 1, pl.ds(h * plane_rows, plane_rows), :]
            owner_sum[d * liq_n + h] = total
        for step in far_first:
            owner_copy(d, step).start()

    def collect(d):
        for step in far_first:
            owner_copy(d, step).wait_recv()
        total = owner_sum[d * liq_n + liq_me]
        for step in range(1, liq_n):
            total = total + owner_in[d * (liq_n - 1) + step - 1]
        settled[pl.ds(d * plane_rows, plane_rows), :] = total
        return total

    def second_policy():
        if relayed:
            for half in range(2):
                pencil_relay(half).wait_recv()
        else:
            for half, step in early:
                pencil_copy(1, half, step).wait_recv()
        for half, step in late:
            pencil_copy(1, half, step).wait_recv()
        for tile in range(tiles):
            consumption_ref[pl.ds(tile * TILE, TILE), :] = interpolate(1, tile)

    first_policy(0)
    scatter(0, 0)
    first_policy(1)
    value_copy(1, value_two).start()
    scatter(0, 1)
    send_terms(0)
    value_copy(1, value_two).wait_recv()
    drifted = dot(second_mat[...], value_two[...]) + dot(second_up[...], near_value[1])
    pencil[liq_n + liq_me] = lax.rsqrt(drifted)
    for half, step in early:
        pencil_copy(1, half, step).start()
    for d in range(1, durables):
        scatter(d, 0)
        if d == 1:
            send_owners(0)
            for half, step in late:
                pencil_copy(1, half, step).start()
        scatter(d, 1)
        send_terms(d)
    for d in range(1, durables):
        send_owners(d)
    if relayed:
        for half, step in early:
            pencil_copy(1, half, step).wait_recv()
        for half in range(2):
            pencil_relay(half).start()

    depart_copy = pltpu.make_async_remote_copy(
        src_ref=depart, dst_ref=depart_in, send_sem=depart_send.at[0], recv_sem=depart_recv.at[0],
        device_id={"dur": jnp.maximum(dur_me - 1, 0)}, device_id_type=MESH_ID,
    )

    depart[...] = (1.0 - stay[0]) * collect(0)

    @pl.when(dur_me > 0)
    def _():
        depart_copy.start()

    for d in range(1, durables):
        collect(d)
    next_ref[...] = dot(next_mat[...], settled[...])
    second_policy()

    @pl.when(dur_me < dur_n - 1)
    def _():
        depart_copy.wait_recv()
        next_ref[...] += dot(next_in[...], depart_in[...])

    value_copy(0, value_ref).wait_send()
    value_copy(1, value_two).wait_send()
    for step in range(1, liq_n):
        for half in range(2):
            pencil_copy(0, half, step).wait_send()
        for d in range(durables):
            owner_copy(d, step).wait_send()
    for half, step in early + late:
        pencil_copy(1, half, step).wait_send()
    if relayed:
        for half in range(2):
            pencil_relay(half).wait_send()
    for step in range(1, ill_n):
        for d in range(durables):
            terms_copy(d, step).wait_send()

    @pl.when(dur_me > 0)
    def _():
        depart_copy.wait_send()


def halves_of(x):
    high = x.astype(jnp.bfloat16)
    return high, (x - high.astype(jnp.float32)).astype(jnp.bfloat16)


def stack_data(x):
    high, low = halves_of(x)
    return jnp.concatenate([high, low, high], axis=0)


def transposed_kernel(
    dims,
    value_hbm, transition_hbm, shock_hbm, drift_hbm, keep_hbm, index_hbm, weight_hbm,
    steady_hbm, lottery_hbm, target_hbm, ill_target_hbm, population_hbm,
    consumption_ref, next_ref,
    value_ref, transition_ref, shock_ref, index_ref, weight_ref, steady_ref, lottery_ref, target_ref,
    population_ref, ill_target_ref, drift_ref, keep_ref, load_sem,
    near_out, near_in, late_out, late_in, side_out, side_in, pair_in,
    pencil_one, value_two, values_in, pencil_two, found_out, found_in, hots, placed, mass_out, depart_out, mass_in,
    near_send, near_recv, late_send, late_recv, goal_send, goal_recv, side_send, side_recv, pair_send, pair_recv,
    value_send, value_recv, found_send, found_recv, mass_send, mass_recv, depart_send, depart_recv, ready_sem,
):
    incomes, durables, ill_rows, liq_rows, liq_n, ill_n, dur_n = dims
    group = durables * ill_rows
    ill_all = ill_n * ill_rows
    part = incomes // liq_n
    per_dest = 3 * ill_rows
    constant = jnp.float32(DISCOUNT * GROSS_RATE)
    f32 = jnp.float32
    liq_me, ill_me, dur_me = (lax.axis_index(name) for name in ("liq", "ill", "dur"))
    far_first = range(liq_n - 1, 0, -1)
    peers = [(step, flip) for step in range(liq_n - 1, -1, -1) for flip in range(ill_n) if step or flip]

    def at(step, flip):
        return {"liq": peer_of(liq_me, step, liq_n), "ill": peer_of(ill_me, flip, ill_n)}

    barrier = pltpu.get_barrier_semaphore()
    for step, flip in peers:
        pl.semaphore_signal(barrier, inc=1, device_id=at(step, flip), device_id_type=MESH_ID)

    @pl.when(dur_me > 0)
    def _():
        pl.semaphore_signal(barrier, inc=1, device_id={"dur": dur_me - 1}, device_id_type=MESH_ID)

    @pl.when(dur_me < dur_n - 1)
    def _():
        pl.semaphore_signal(barrier, inc=1, device_id={"dur": dur_me + 1}, device_id_type=MESH_ID)

    loads = [
        pltpu.make_async_copy(source, held, load_sem.at[slot])
        for slot, (source, held) in enumerate((
            (transition_hbm, transition_ref), (shock_hbm, shock_ref), (value_hbm, value_ref),
            (index_hbm, index_ref), (weight_hbm, weight_ref), (drift_hbm, drift_ref), (ill_target_hbm, ill_target_ref),
            (target_hbm, target_ref), (lottery_hbm, lottery_ref), (steady_hbm, steady_ref),
            (population_hbm, population_ref), (keep_hbm, keep_ref),
        ))
    ]
    for load in loads:
        load.start()

    def rows_at(d, a, z_part):
        return pl.ds(z_part * part * group + d * ill_rows + a, part, stride=group)

    def whole_rows(d, a):
        return pl.ds(d * ill_rows + a, incomes, stride=group)

    kinds = [(d, a) for d in range(durables) for a in range(ill_rows)]
    for load in loads[:2]:
        load.wait()
    transition = transition_ref[...]
    eye = iota((incomes, incomes), 0) == iota((incomes, incomes), 1)
    scaled = dot(jnp.where(eye, constant * shock_ref[...], 0.0), transition)

    def stack_left(x):
        high, low = halves_of(x)
        return jnp.concatenate([high, high, low], axis=1)

    def times(left, x):
        return jnp.dot(left, stack_data(x), preferred_element_type=f32)

    left_one = stack_left(scaled)
    left_two = stack_left(constant * transition)
    loads[2].wait()
    wide = jnp.concatenate([value_ref[whole_rows(d, a), :] for d, a in kinds], axis=1)
    wide = times(left_one, wide)
    for load in loads[3:5]:
        load.wait()
    for k, (d, a) in enumerate(kinds):
        for q in range(liq_n):
            near_out[d * liq_n + q, a] = wide[q * part : (q + 1) * part, k * liq_rows : (k + 1) * liq_rows]
            near_out[d * liq_n + q, ill_rows + a] = index_ref[rows_at(d, a, q), :].astype(f32)
            near_out[d * liq_n + q, 2 * ill_rows + a] = weight_ref[rows_at(d, a, q), :]

    for load in loads[5:7]:
        load.wait()
    column = iota((part, incomes), 1)
    wanted = column == liq_me * part + iota((part, incomes), 0)
    picked = jnp.concatenate(
        [
            jnp.where(wanted, jnp.broadcast_to(ill_target_ref[k : k + 1, :], (part, incomes)), 0)
            for k in range(group)
        ],
        axis=0,
    )
    spread = jnp.dot(
        picked.astype(f32).astype(jnp.bfloat16), jnp.ones((incomes, liq_rows), jnp.bfloat16), preferred_element_type=f32
    )
    row = iota((TILE, liq_rows), 0)
    drifts = jnp.zeros((TILE, liq_rows), f32)
    for a in range(ill_rows):
        drifts = jnp.where(row == a, drift_ref[a], drifts)
    for k, (d, a) in enumerate(kinds):
        side_out[d, a] = spread[k * part : (k + 1) * part]
    for d in range(durables):
        side_out[d, ill_rows] = drifts

    with scope("bar"):
        dur_peers = jnp.minimum(dur_me, 1) + jnp.minimum(dur_n - 1 - dur_me, 1)
        pl.semaphore_wait(barrier, len(peers) + dur_peers)

    @pl.when((dur_me < dur_n - 1) & (ill_me == 0))
    def _():
        pl.semaphore_signal(ready_sem, inc=1, device_id={"dur": dur_me + 1}, device_id_type=MESH_ID)

    def bundle_copy(out_ref, in_ref, send, recv, first, count, step, i):
        liq_there, kept = peer_of(liq_me, step, liq_n), pl.ds(first, count)
        return pltpu.make_async_remote_copy(
            src_ref=out_ref.at[i * liq_n + liq_there, kept], dst_ref=in_ref.at[liq_me * ill_n + ill_me, kept],
            send_sem=send.at[0], recv_sem=recv.at[0], device_id={"liq": liq_there, "ill": i}, device_id_type=MESH_ID,
        )

    def bundle_all(out_ref, in_ref, send, recv, first, count):
        span, kept = pl.ds(0, len(peers)), pl.ds(first, count)
        return pltpu.make_async_remote_copy(
            src_ref=out_ref.at[span, kept], dst_ref=in_ref.at[span, kept], send_sem=send.at[0], recv_sem=recv.at[0],
            device_id=at(0, 1), device_id_type=MESH_ID,
        )

    def near_all():
        return bundle_all(near_out, near_in, near_send, near_recv, 0, per_dest)

    def late_all():
        return bundle_all(late_out, late_in, late_send, late_recv, 0, 2 * ill_rows)

    def goal_all():
        return bundle_all(late_out, late_in, goal_send, goal_recv, 2 * ill_rows, ill_rows)

    def near_copy(step, i):
        return bundle_copy(near_out, near_in, near_send, near_recv, 0, per_dest, step, i)

    def late_copy(step, i):
        return bundle_copy(late_out, late_in, late_send, late_recv, 0, 2 * ill_rows, step, i)

    def goal_copy(step, i):
        return bundle_copy(late_out, late_in, goal_send, goal_recv, 2 * ill_rows, ill_rows, step, i)

    def side_copy(flip):
        there = at(0, flip)
        return pltpu.make_async_remote_copy(
            src_ref=side_out.at[there["ill"]], dst_ref=side_in.at[ill_me],
            send_sem=side_send.at[flip - 1], recv_sem=side_recv.at[flip - 1], device_id=there, device_id_type=MESH_ID,
        )

    def pair_copy(flip):
        there = at(0, flip)
        return pltpu.make_async_remote_copy(
            src_ref=near_out.at[pl.ds(there["ill"] * liq_n, liq_n), pl.ds(ill_rows, 2 * ill_rows)],
            dst_ref=pair_in.at[ill_me], send_sem=pair_send.at[flip - 1], recv_sem=pair_recv.at[flip - 1],
            device_id=there, device_id_type=MESH_ID,
        )

    def start_to(i, make):
        for step in far_first:
            make(step, i).start()

        @pl.when(ill_me != i)
        def _():
            make(0, i).start()

    for i in range(ill_n):
        start_to(i, near_copy)
    for flip in range(1, ill_n):
        side_copy(flip).start()

    for load in loads[7:]:
        load.wait()
    for d, a in kinds:
        for q in range(liq_n):
            span = rows_at(d, a, q)
            late_out[d * liq_n + q, a] = lottery_ref[span, :] - SLOPE_GAIN * steady_ref[span, :]
            late_out[d * liq_n + q, ill_rows + a] = population_ref[span, :]
            late_out[d * liq_n + q, 2 * ill_rows + a] = target_ref[span, :].astype(f32)
    for i in range(ill_n):
        start_to(i, goal_copy)
        start_to(i, late_copy)
    for flip in range(1, ill_n):
        pair_copy(flip).start()

    own_out = ill_me * liq_n + liq_me
    own_in = liq_me * ill_n + ill_me
    for k in range(per_dest):
        near_in[own_in, k] = near_out[own_out, k]
        late_in[own_in, k] = late_out[own_out, k]
    for k in range(ill_rows + 1):
        side_in[ill_me, k] = side_out[ill_me, k]
    for q in range(liq_n):
        for k in range(2 * ill_rows):
            pair_in[ill_me, q, k] = near_out[ill_me * liq_n + q, ill_rows + k]

    @pl.when(dur_me == dur_n - 1)
    def _():
        for a in range(ill_rows):
            mass_in[group + a] = jnp.zeros((incomes, liq_rows), f32)

    stay = [keep_ref[d] for d in range(durables)]
    first_d = as_float(dur_me == 0)
    stay[0] = first_d + (1.0 - first_d) * stay[0]

    def received(ref, kind, h, ag):
        return ref[h * ill_n + ag // ill_rows, kind * ill_rows + ag % ill_rows]

    def interpolate(blocks, index, weight):
        index = index.astype(jnp.int32)
        low_block, low_lane = split_by(index, liq_rows)
        high_block, high_lane = split_by(index + 1, liq_rows)
        low = high = None
        for h, block in enumerate(blocks):
            low_h = jnp.take_along_axis(block, low_lane, axis=1, mode="promise_in_bounds")
            high_h = jnp.take_along_axis(block, high_lane, axis=1, mode="promise_in_bounds")
            low = low_h if h == 0 else jnp.where(low_block == h, low_h, low)
            high = high_h if h == 0 else jnp.where(high_block == h, high_h, high)
        return weight * low + (1.0 - weight) * high

    own_z = pl.ds(pl.multiple_of(liq_me * part, TILE), part)

    ill_pair = peer_of(ill_me, 1, ill_n)
    pieces = [(ill_pair * ill_rows, ill_rows)] + [(ill_me * ill_rows + a, 1) for a in range(ill_rows)]

    def value_copy(k, step):
        start, count = pieces[k]
        span = pl.ds(start * liq_n, count * liq_n)
        return pltpu.make_async_remote_copy(
            src_ref=value_two.at[span], dst_ref=values_in.at[span, own_z], send_sem=value_send.at[0],
            recv_sem=value_recv.at[k], device_id={"liq": peer_of(liq_me, step, liq_n)}, device_id_type=MESH_ID,
        )

    def value_all(k, count):
        span = pl.ds(0, (liq_n - 1) * count)
        return pltpu.make_async_remote_copy(
            src_ref=values_in.at[span], dst_ref=values_in.at[span], send_sem=value_send.at[0],
            recv_sem=value_recv.at[k], device_id=at(1, 0), device_id_type=MESH_ID,
        )

    with scope("near"):
        for flip in range(1, ill_n):
            side_copy(flip).wait_recv()
        near_all().wait_recv()

    with scope("policy"):
        for ag in range(ill_all):
            i, a = divmod(ag, ill_rows)
            own = jnp.broadcast_to(side_in[i, ill_rows, a : a + 1, :], (TILE, liq_rows))
            for h in range(liq_n):
                drifted = own * received(near_in, 0, h, ag) + (1.0 - own) * received(near_in, 0, h, min(ag + 1, ill_all - 1))
                pencil_one[ag * liq_n + h] = lax.rsqrt(drifted)
        for k, (start, count) in enumerate(pieces):
            for turn in range(count):
                i, a = (ill_pair, turn) if k == 0 else (ill_me, k - 1)
                ag = i * ill_rows + a
                blocks = [pencil_one[ag * liq_n + h] for h in range(liq_n)]
                for h in range(liq_n):
                    source = h * ill_n + i
                    chosen = interpolate(blocks, near_in[source, ill_rows + a], near_in[source, 2 * ill_rows + a])
                    found = GROSS_RATE / (chosen * chosen)
                    value_two[ag * liq_n + h] = found
                    values_in[ag * liq_n + h, own_z, :] = found
                    pencil_one[ill_all * liq_n + ag * liq_n + h] = chosen
            for step in far_first:
                value_copy(k, step).start()

    half = liq_rows // 2
    cuts = 2 * liq_n
    sub = iota((cuts, liq_rows), 0).astype(f32)
    lane_at = iota((TILE, liq_rows), 1)
    lane_row = iota((half, liq_rows), 0).astype(f32).astype(jnp.bfloat16)
    one = jnp.ones((half, liq_rows), jnp.bfloat16)
    nil = jnp.zeros((half, liq_rows), jnp.bfloat16)

    with scope("goal"):
        goal_all().wait_recv()
    with scope("hots"):
        cut_at = {}
        for ag in range(ill_all):
            places = []
            for h in range(liq_n):
                target = received(late_in, 2, h, ag)
                cut = jnp.zeros(target.shape, f32)
                for other in range(1, cuts):
                    cut = cut + jnp.where(target >= other * half, 1.0, 0.0)
                cut_at[ag, h] = cut
                places.append(target - half * cut)
            for s in range(part):
                for h in range(liq_n):
                    place = jnp.broadcast_to(places[h][s : s + 1, :], (2 * TILE, liq_rows)).astype(jnp.bfloat16)
                    place = jnp.concatenate([place] * (half // (2 * TILE)), axis=0)
                    hots[s * ill_all + ag, :, h * liq_rows : (h + 1) * liq_rows] = jnp.where(lane_row == place, one, nil)
    with scope("late"):
        late_all().wait_recv()
    with scope("scatter"):
        held = {}
        for ag in range(ill_all):
            for h in range(liq_n):
                chosen = pencil_one[ill_all * liq_n + ag * liq_n + h]
                share = jnp.clip(received(late_in, 0, h, ag) + SLOPE_GAIN * chosen, 0.0, 1.0)
                mass = received(late_in, 1, h, ag)
                held[ag, h] = (mass * share, mass * (1.0 - share), cut_at[ag, h])
        for s in range(part):
            totals, to_row = [], []
            for ag in range(ill_all):
                lefts = []
                for h in range(liq_n):
                    low_t, high_t, cut_t = (x[s : s + 1, :] for x in held[ag, h])
                    here = cut_t == sub
                    both = jnp.concatenate([jnp.where(here, low_t, 0.0), jnp.where(here, high_t, 0.0)], axis=0)
                    first = both.astype(jnp.bfloat16)
                    lefts.append(jnp.concatenate([first, (both - first.astype(f32)).astype(jnp.bfloat16)], axis=0))
                found = lax.dot_general(
                    jnp.concatenate(lefts, axis=1), hots[s * ill_all + ag], NT, preferred_element_type=f32
                )
                totals.append(found[: 2 * cuts] + found[2 * cuts :])
                to_row.append(jnp.broadcast_to(side_in[ag // ill_rows, ag % ill_rows, s : s + 1, :half], (2 * cuts, half)))
            for dest in range(ill_all):
                out = None
                for ag in range(ill_all):
                    here = jnp.where(to_row[ag] == dest, totals[ag], 0.0)
                    out = here if out is None else out + here
                placed[pl.ds(dest * 2 * cuts * part + s, 2 * cuts, stride=part), :half] = out

    with scope("massout"):
        def joined(dest, side, h):
            start = ((dest * 2 + side) * cuts + 2 * h) * part
            return jnp.concatenate(
                [placed[pl.ds(start, part), :half], placed[pl.ds(start + part, part), :half]], axis=1
            )

        for dest in range(ill_all):
            carried = None
            for h in range(liq_n):
                low = joined(dest, 0, h)
                moved = pltpu.roll(joined(dest, 1, h), 1, 1)
                total = low + jnp.where(lane_at > 0, moved, 0.0 if carried is None else carried)
                carried = moved
                mass_out[h * ill_all + dest] = total
                depart_out[h * ill_all + dest] = (1.0 - stay[0]) * total

    def mass_copy(step, flip):
        there = at(step, flip)
        return pltpu.make_async_remote_copy(
            src_ref=mass_out.at[pl.ds(there["liq"] * ill_all + there["ill"] * ill_rows, ill_rows)],
            dst_ref=mass_in.at[pl.ds(ill_me * ill_rows, ill_rows), own_z],
            send_sem=mass_send.at[0], recv_sem=mass_recv.at[0], device_id=there, device_id_type=MESH_ID,
        )

    def mass_all():
        span = pl.ds(0, len(peers) * ill_rows)
        return pltpu.make_async_remote_copy(
            src_ref=mass_out.at[span], dst_ref=mass_out.at[span], send_sem=mass_send.at[0],
            recv_sem=mass_recv.at[0], device_id=at(0, 1), device_id_type=MESH_ID,
        )

    def depart_all(count):
        span = pl.ds(0, count * ill_rows)
        return pltpu.make_async_remote_copy(
            src_ref=depart_out.at[span], dst_ref=depart_out.at[span], send_sem=depart_send.at[0],
            recv_sem=depart_recv.at[0], device_id=at(0, 1), device_id_type=MESH_ID,
        )

    def depart_copy(step, i):
        liq_there = peer_of(liq_me, step, liq_n)
        return pltpu.make_async_remote_copy(
            src_ref=depart_out.at[pl.ds(liq_there * ill_all + i * ill_rows, ill_rows)],
            dst_ref=mass_in.at[pl.ds(group, ill_rows), own_z],
            send_sem=depart_send.at[0], recv_sem=depart_recv.at[0],
            device_id={"dur": jnp.maximum(dur_me - 1, 0), "liq": liq_there, "ill": i}, device_id_type=MESH_ID,
        )

    departs = (dur_me > 0) & (ill_me == 0)

    @pl.when(departs)
    def _():
        pl.semaphore_wait(ready_sem, 1)
        for step in range(liq_n - 1, -1, -1):
            for i in range(ill_n):
                depart_copy(step, i).start()

    for step, flip in peers:
        mass_copy(step, flip).start()
    for a in range(ill_rows):
        mass_in[ill_me * ill_rows + a, own_z, :] = mass_out[liq_me * ill_all + ill_me * ill_rows + a]

    def found_copy(flip):
        there = at(0, flip)
        return pltpu.make_async_remote_copy(
            src_ref=found_out.at[flip - 1], dst_ref=found_in.at[flip - 1],
            send_sem=found_send.at[flip - 1], recv_sem=found_recv.at[flip - 1], device_id=there, device_id_type=MESH_ID,
        )

    for flip in range(1, ill_n):
        side_copy(flip).wait_send()
        pair_copy(flip).wait_send()
        pair_copy(flip).wait_recv()
    near_all().wait_send()
    late_all().wait_send()
    goal_all().wait_send()
    is_last = ill_me == ill_n - 1

    def expect(ag):
        wide = jnp.concatenate([values_in[ag * liq_n + h] for h in range(liq_n)], axis=1)
        return times(left_two, wide)

    def consume(i, expected, store_tile):
        for a in range(ill_rows):
            own = jnp.broadcast_to(side_in[i, ill_rows, a : a + 1, :], (incomes, liq_rows))
            own = jnp.concatenate([own] * liq_n, axis=1)
            found = lax.rsqrt(own * expected[a] + (1.0 - own) * expected[a + 1])
            for h in range(liq_n):
                pencil_two[a * liq_n + h] = found[:, h * liq_rows : (h + 1) * liq_rows]
        for a in range(ill_rows):
            for q in range(liq_n):
                blocks = [pencil_two[a * liq_n + h, pl.ds(q * part, part), :] for h in range(liq_n)]
                store_tile(a, q, interpolate(blocks, pair_in[i, q, a], pair_in[i, q, ill_rows + a]))

    def store_found(a, q, found):
        found_out[0, q * ill_rows + a] = found

    def store_own(a, q, found):
        consumption_ref[rows_at(ill_me, a, q), :] = found

    with scope("values"):
        value_all(0, ill_rows).wait_recv()

        @pl.when(is_last)
        def _():
            value_all(1, 1).wait_recv()

    with scope("second_a"):
        above = jnp.minimum(ill_pair * ill_rows + ill_rows, ill_all - 1)
        expected = [expect(ill_pair * ill_rows + a) for a in range(ill_rows)]
        lowest = expected[0]
        consume(ill_pair, expected + [expect(above)], store_found)
        found_copy(1).start()

    with scope("values_b"):
        @pl.when(jnp.logical_not(is_last))
        def _():
            value_all(1, 1).wait_recv()

        for a in range(1, ill_rows):
            value_all(1 + a, 1).wait_recv()

    with scope("second_b"):
        expected = [expect(ill_me * ill_rows + a) for a in range(ill_rows)]
        expected.append(jnp.where(is_last, expected[-1], lowest))
        consume(ill_me, expected, store_own)

    with scope("sends"):
        value_all(0, ill_all).wait_send()
        mass_all().wait_send()

        @pl.when(departs)
        def _():
            depart_all(liq_n * ill_n).wait_send()

    with scope("found"):
        for flip in range(1, ill_n):
            found_copy(flip).wait_send()
            found_copy(flip).wait_recv()
            for q in range(liq_n):
                for a in range(ill_rows):
                    consumption_ref[rows_at(peer_of(ill_me, flip, ill_n), a, q), :] = found_in[flip - 1, q * ill_rows + a]

    with scope("mass"):
        mass_all().wait_recv()

        @pl.when(dur_me < dur_n - 1)
        def _():
            depart_all(liq_n).wait_recv()

    with scope("next"):
        settled = []
        for d, a in kinds:
            after = mass_in[(d + 1) * ill_rows + a]
            if d + 1 < durables:
                after = (1.0 - stay[d + 1]) * after
            settled.append(stay[d] * mass_in[d * ill_rows + a] + after)
        high, low = halves_of(transition)
        found = lax.dot_general(
            jnp.concatenate([high, high, low], axis=0), stack_data(jnp.concatenate(settled, axis=1)),
            (((0,), (0,)), ((), ())), preferred_element_type=f32,
        )
        for k, (d, a) in enumerate(kinds):
            for q in range(liq_n):
                next_ref[rows_at(d, a, q), :] = found[q * part : (q + 1) * part, k * liq_rows : (k + 1) * liq_rows]


def store(consumption_ref, next_ref, consumption_hbm, next_hbm, sem):
    copies = [
        pltpu.make_async_copy(consumption_ref, consumption_hbm, sem.at[0]),
        pltpu.make_async_copy(next_ref, next_hbm, sem.at[1]),
    ]
    for copy in copies:
        copy.start()
    for copy in copies:
        copy.wait()


def window_scratch(dims):
    incomes, durables, ill_rows, liq_rows, liq_n, ill_n, dur_n = dims
    f32 = jnp.float32
    rows, plane_rows = incomes * durables * ill_rows, incomes * ill_rows
    block = (rows, liq_rows)
    dma = pltpu.SemaphoreType.DMA
    return [
        pltpu.VMEM(block, f32),
        pltpu.VMEM((incomes, incomes), f32),
        pltpu.VMEM((1, incomes), f32),
        pltpu.VMEM(block, jnp.int32),
        pltpu.VMEM(block, f32),
        pltpu.VMEM(block, f32),
        pltpu.VMEM(block, f32),
        pltpu.VMEM(block, jnp.int32),
        pltpu.VMEM(block, f32),
        pltpu.SMEM((ill_rows,), f32),
        pltpu.SMEM((durables,), f32),
        pltpu.SMEM((durables * ill_rows, incomes), jnp.int32),
        dma((12,)),
        pltpu.VMEM((rows, rows), f32),
        pltpu.VMEM((rows, rows), f32),
        pltpu.VMEM((rows, rows), f32),
        pltpu.VMEM((rows, rows), f32),
        pltpu.VMEM((rows, rows), f32),
        pltpu.VMEM((rows, plane_rows), f32),
        pltpu.VMEM((2,) + block, f32),
        pltpu.VMEM(block, f32),
        pltpu.VMEM((2 * liq_n,) + block, f32),
        pltpu.VMEM(block, f32),
        pltpu.VMEM(block, f32),
        pltpu.VMEM(block, jnp.int32),
        pltpu.VMEM(block, f32),
        pltpu.VMEM((2 * ill_n * liq_n * plane_rows, liq_rows), f32),
        pltpu.VMEM((ill_n * liq_n * rows, liq_rows), f32),
        pltpu.VMEM((durables * (ill_n - 1), liq_n * plane_rows, liq_rows), f32),
        pltpu.VMEM((durables * liq_n, plane_rows, liq_rows), f32),
        pltpu.VMEM((durables * (liq_n - 1), plane_rows, liq_rows), f32),
        pltpu.VMEM(block, f32),
        pltpu.VMEM((plane_rows, liq_rows), f32),
        pltpu.VMEM((plane_rows, liq_rows), f32),
        dma((2,)),
        dma((2,)),
        dma((4 * liq_n,)),
        dma((4 * liq_n,)),
        dma((durables * (ill_n - 1),)),
        dma((durables * (ill_n - 1),)),
        dma((durables * (liq_n - 1),)),
        dma((durables * (liq_n - 1),)),
        dma((1,)),
        dma((1,)),
    ]


def transposed_scratch(dims):
    incomes, durables, ill_rows, liq_rows, liq_n, ill_n, dur_n = dims
    f32 = jnp.float32
    block = (incomes * durables * ill_rows, liq_rows)
    dma = pltpu.SemaphoreType.DMA
    part = incomes // liq_n
    ill_all = ill_n * ill_rows
    tiles = lambda n: pltpu.VMEM((n, part, liq_rows), f32)
    slabs = lambda n: pltpu.VMEM((n, incomes, liq_rows), f32)
    bundles = pltpu.VMEM((durables * liq_n, 3 * ill_rows, part, liq_rows), f32)
    return [
        pltpu.VMEM(block, f32),
        pltpu.VMEM((incomes, incomes), f32),
        pltpu.VMEM((1, incomes), f32),
        pltpu.VMEM(block, jnp.int32),
        pltpu.VMEM(block, f32),
        pltpu.VMEM(block, f32),
        pltpu.VMEM(block, f32),
        pltpu.VMEM(block, jnp.int32),
        pltpu.VMEM(block, f32),
        pltpu.VMEM((durables * ill_rows, incomes), jnp.int32),
        pltpu.SMEM((ill_rows,), f32),
        pltpu.SMEM((durables,), f32),
        dma((12,)),
        bundles,
        bundles,
        bundles,
        bundles,
        pltpu.VMEM((durables, ill_rows + 1, TILE, liq_rows), f32),
        pltpu.VMEM((ill_n, ill_rows + 1, TILE, liq_rows), f32),
        pltpu.VMEM((ill_n, liq_n, 2 * ill_rows, part, liq_rows), f32),
        tiles(2 * ill_all * liq_n),
        tiles(ill_all * liq_n),
        slabs(ill_all * liq_n),
        slabs(ill_rows * liq_n),
        pltpu.VMEM((ill_n - 1, liq_n * ill_rows, part, liq_rows), f32),
        pltpu.VMEM((ill_n - 1, liq_n * ill_rows, part, liq_rows), f32),
        pltpu.VMEM((part * ill_all, liq_rows // 2, liq_n * liq_rows), jnp.bfloat16),
        pltpu.VMEM((4 * liq_n * ill_all * part, liq_rows), f32),
        tiles(liq_n * ill_all),
        tiles(liq_n * ill_all),
        slabs((durables + 1) * ill_rows),
    ] + [
        dma((n,)) for n in (1, 1, 1, 1, 1, 1, 1, 1, 1, 1, 1, ill_rows + 1, 1, 1, 1, 1, 1, 1)
    ] + [pltpu.SemaphoreType.REGULAR]


def body(
    marginal_value,
    transition,
    discount_shock,
    illiquid_drift,
    durable_keep,
    bracket_index,
    bracket_weight,
    steady_consumption,
    lottery_weight,
    liquid_target,
    illiquid_target,
    population,
):
    shape = marginal_value.shape
    incomes, durables, ill_rows, liq_rows = shape
    liq_n, ill_n, dur_n = (lax.axis_size(name) for name in ("liq", "ill", "dur"))
    rows = incomes * durables * ill_rows
    flat = lambda x: x.reshape(rows, liq_rows)
    anywhere = pl.BlockSpec(memory_space=pl.ANY)
    f32 = jnp.float32
    block = (rows, liq_rows)
    dma = pltpu.SemaphoreType.DMA
    vmem = pl.BlockSpec(memory_space=pltpu.VMEM)
    held = pltpu.VMEM(block, f32)
    result = jax.ShapeDtypeStruct(block, f32)
    dims = (incomes, durables, ill_rows, liq_rows, liq_n, ill_n, dur_n)
    transposed = (
        ill_n == 2 and durables == ill_n and liq_n * 2 == TILE and incomes == liq_n * TILE and ill_rows < TILE
    )
    if transposed:
        step_kernel, scratch, name = transposed_kernel, transposed_scratch(dims), "transposed_window"
    else:
        step_kernel, scratch, name = kernel, window_scratch(dims), "window"
    outs = pl.pallas_call(
        functools.partial(step_kernel, dims),
        out_shape=(held, held),
        in_specs=[anywhere] * 12,
        out_specs=(vmem, vmem),
        scratch_shapes=scratch,
        compiler_params=pltpu.CompilerParams(collective_id=0, has_side_effects=True),
        name=name,
    )(
        flat(marginal_value),
        transition,
        discount_shock.reshape(1, incomes),
        illiquid_drift,
        durable_keep,
        flat(bracket_index),
        flat(bracket_weight),
        flat(steady_consumption),
        flat(lottery_weight),
        flat(liquid_target),
        jnp.transpose(illiquid_target, (1, 2, 0)).reshape(durables * ill_rows, incomes),
        flat(population),
    )
    outs = pl.pallas_call(
        store,
        out_shape=(result, result),
        in_specs=[vmem, vmem],
        out_specs=(anywhere, anywhere),
        scratch_shapes=[dma((2,))],
        name="store",
    )(*(pltpu.with_memory_space_constraint(out, pltpu.VMEM) for out in outs))
    return tuple(out.reshape(shape) for out in outs)


def solution(mesh):
    in_specs = (
        P(None, "dur", "ill", "liq"),
        P(),
        P(),
        P("ill"),
        P("dur"),
        P(None, "dur", "ill", "liq"),
        P(None, "dur", "ill", "liq"),
        P(None, "dur", "ill", "liq"),
        P(None, "dur", "ill", "liq"),
        P(None, "dur", "ill", "liq"),
        P(None, "dur", "ill"),
        P(None, "dur", "ill", "liq"),
    )
    out_specs = (P(None, "dur", "ill", "liq"), P(None, "dur", "ill", "liq"))
    return jax.shard_map(body, mesh=mesh, in_specs=in_specs, out_specs=out_specs, check_vma=False)
```

```python
import contextlib
import functools

import jax
import jax.numpy as jnp
from jax import lax
from jax.experimental import pallas as pl
from jax.experimental.pallas import tpu as pltpu
from jax.sharding import PartitionSpec as P

DISCOUNT = 0.96
GROSS_RATE = 1.01
SLOPE_GAIN = 0.5
HIGHEST_PREC = lax.Precision.HIGHEST
MESH_ID = pl.DeviceIdType.MESH
NT = (((1,), (1,)), ((), ()))
TILE = 8


def scope(name):
    return contextlib.nullcontext()


def split_by(x, n):
    if n & (n - 1) == 0:
        return x >> (n.bit_length() - 1), x & (n - 1)
    return lax.div(x, jnp.int32(n)), lax.rem(x, jnp.int32(n))


def dot(a, b):
    return jnp.dot(a, b, precision=HIGHEST_PREC, preferred_element_type=jnp.float32)


def iota(shape, axis):
    return lax.broadcasted_iota(jnp.int32, shape, axis)


def as_float(flag):
    return jnp.where(flag, jnp.float32(1.0), jnp.float32(0.0))


def peer_of(me, step, n):
    if n & (n - 1):
        return lax.rem(me + step, n)
    out = me
    for bit in range(n.bit_length() - 1):
        if step >> bit & 1:
            out = out + (1 - 2 * lax.rem(lax.div(me, jnp.int32(1 << bit)), jnp.int32(2))) * (1 << bit)
    return out


def kernel(
    dims,
    value_hbm, transition_hbm, shock_hbm, drift_hbm, keep_hbm, index_hbm, weight_hbm,
    steady_hbm, lottery_hbm, target_hbm, ill_target_hbm, population_hbm,
    consumption_ref, next_ref,
    value_ref, transition_ref, shock_ref, index_ref, weight_ref, steady_ref, lottery_ref, target_ref,
    population_ref, drift_ref, keep_ref, ill_target_ref, load_sem,
    first_mat, first_up, second_mat, second_up, next_mat, next_in,
    near_value, value_two, pencil, mass_low, mass_high, target_hi, target_lo,
    placed_rows, terms, terms_in, owner_sum, owner_in, settled, depart, depart_in,
    value_send, value_recv, pencil_send, pencil_recv, terms_send, terms_recv,
    owner_send, owner_recv, depart_send, depart_recv,
):
    incomes, durables, ill_rows, liq_rows, liq_n, ill_n, dur_n = dims
    group = durables * ill_rows
    rows = incomes * group
    half_rows = rows // 2
    plane_rows = incomes * ill_rows
    liq_me, ill_me, dur_me = (lax.axis_index(name) for name in ("liq", "ill", "dur"))
    far_first = range(liq_n - 1, 0, -1)

    barrier = pltpu.get_barrier_semaphore()
    for step in far_first:
        pl.semaphore_signal(barrier, inc=1, device_id={"liq": peer_of(liq_me, step, liq_n)}, device_id_type=MESH_ID)
    for step in range(1, ill_n):
        pl.semaphore_signal(barrier, inc=1, device_id={"ill": peer_of(ill_me, step, ill_n)}, device_id_type=MESH_ID)

    @pl.when(dur_me > 0)
    def _():
        pl.semaphore_signal(barrier, inc=1, device_id={"dur": dur_me - 1}, device_id_type=MESH_ID)

    @pl.when(dur_me < dur_n - 1)
    def _():
        pl.semaphore_signal(barrier, inc=1, device_id={"dur": dur_me + 1}, device_id_type=MESH_ID)

    loads = [
        pltpu.make_async_copy(source, held, load_sem.at[slot])
        for slot, (source, held) in enumerate((
            (transition_hbm, transition_ref), (shock_hbm, shock_ref), (drift_hbm, drift_ref), (value_hbm, value_ref),
            (keep_hbm, keep_ref), (ill_target_hbm, ill_target_ref),
            (index_hbm, index_ref), (weight_hbm, weight_ref), (target_hbm, target_ref),
            (lottery_hbm, lottery_ref), (steady_hbm, steady_ref), (population_hbm, population_ref),
        ))
    ]
    for load in loads:
        load.start()
    for load in loads[:3]:
        load.wait()

    transition = transition_ref[...]
    row_z, row_rest = split_by(iota((rows, rows), 0), group)
    col_z, col_rest = split_by(iota((rows, rows), 1), group)
    row_d, row_a = split_by(row_rest, ill_rows)
    col_d, col_a = split_by(col_rest, ill_rows)
    spread = as_float(split_by(iota((rows, incomes), 0), group)[0] == iota((rows, incomes), 1))
    spread_t = as_float(iota((incomes, rows), 0) == split_by(iota((incomes, rows), 1), group)[0])
    drift = jnp.zeros((rows, rows), jnp.float32)
    for a in range(ill_rows):
        drift = jnp.where(row_a == a, drift_ref[a], drift)
    is_last = as_float(ill_me == ill_n - 1)
    same_d = row_d == col_d
    top_row = row_a == ill_rows - 1
    local = jnp.where(col_a == row_a, drift, 0.0)
    local = local + jnp.where(col_a == row_a + 1, 1.0 - drift, 0.0)
    local = local + jnp.where(top_row & (col_a == ill_rows - 1), is_last * (1.0 - drift), 0.0)
    local = jnp.where(same_d, local, 0.0)
    upper = jnp.where(same_d & top_row & (col_a == 0), (1.0 - is_last) * (1.0 - drift), 0.0)
    constant = jnp.float32(DISCOUNT * GROSS_RATE)
    eye = iota((incomes, incomes), 0) == iota((incomes, incomes), 1)
    scaled = dot(jnp.where(eye, constant * shock_ref[...], 0.0), transition)
    wide = dot(dot(spread, scaled), spread_t)
    first_mat[...] = wide * local
    first_up[...] = wide * upper

    dur_peers = jnp.minimum(dur_me, 1) + jnp.minimum(dur_n - 1 - dur_me, 1)
    pl.semaphore_wait(barrier, liq_n - 1 + ill_n - 1 + dur_peers)

    ill_below = lax.rem(ill_me + ill_n - 1, ill_n)

    def value_copy(k, source):
        return pltpu.make_async_remote_copy(
            src_ref=source, dst_ref=near_value.at[k], send_sem=value_send.at[k],
            recv_sem=value_recv.at[k], device_id={"ill": ill_below}, device_id_type=MESH_ID,
        )

    def pencil_copy(k, half, step):
        slot = (k * 2 + half) * liq_n + step
        part = pencil.at[k * liq_n + liq_me, pl.ds(half * half_rows, half_rows)]
        return pltpu.make_async_remote_copy(
            src_ref=part, dst_ref=part, send_sem=pencil_send.at[slot], recv_sem=pencil_recv.at[slot],
            device_id={"liq": peer_of(liq_me, step, liq_n)}, device_id_type=MESH_ID,
        )

    def pencil_relay(half):
        near, far = (1, 2) if half == 0 else (2, 1)
        slot = (2 + half) * liq_n
        part = pencil.at[liq_n + peer_of(liq_me, near, liq_n), pl.ds(half * half_rows, half_rows)]
        return pltpu.make_async_remote_copy(
            src_ref=part, dst_ref=part, send_sem=pencil_send.at[slot], recv_sem=pencil_recv.at[slot],
            device_id={"liq": peer_of(liq_me, far, liq_n)}, device_id_type=MESH_ID,
        )

    relayed = liq_n == 4
    if relayed:
        early, late = [(0, 1), (1, 2)], [(1, 1), (0, 2)]
    else:
        early, late = [(0, step) for step in far_first], [(1, step) for step in far_first]

    def terms_copy(d, step):
        peer = peer_of(ill_me, step, ill_n)
        slot = d * (ill_n - 1) + step - 1
        return pltpu.make_async_remote_copy(
            src_ref=terms.at[pl.ds((d * ill_n + peer) * (liq_n * plane_rows), liq_n * plane_rows)],
            dst_ref=terms_in.at[slot], send_sem=terms_send.at[slot], recv_sem=terms_recv.at[slot],
            device_id={"ill": peer}, device_id_type=MESH_ID,
        )

    def owner_copy(d, step):
        peer = peer_of(liq_me, step, liq_n)
        slot = d * (liq_n - 1) + step - 1
        return pltpu.make_async_remote_copy(
            src_ref=owner_sum.at[d * liq_n + peer], dst_ref=owner_in.at[slot],
            send_sem=owner_send.at[slot], recv_sem=owner_recv.at[slot],
            device_id={"liq": peer}, device_id_type=MESH_ID,
        )

    loads[3].wait()
    value_copy(0, value_ref).start()
    drifted = dot(first_mat[...], value_ref[...])
    value_copy(0, value_ref).wait_recv()
    drifted = drifted + dot(first_up[...], near_value[0])
    pencil[liq_me] = lax.rsqrt(drifted)
    for half in range(2):
        for step in far_first:
            pencil_copy(0, half, step).start()

    wide = constant * dot(dot(spread, transition), spread_t)
    second_mat[...] = wide * local
    second_up[...] = wide * upper

    for load in loads[4:]:
        load.wait()

    first_d = as_float(dur_me == 0)
    stay = [keep_ref[d] for d in range(durables)]
    stay[0] = first_d + (1.0 - first_d) * stay[0]
    back_d, back_rest = split_by(iota((rows, rows), 1), plane_rows)
    back_a = split_by(back_rest, ill_rows)[1]
    stays = jnp.zeros((rows, rows), jnp.float32)
    for d in range(durables):
        stays = jnp.where(back_d == d, stay[d], stays)
    mix = jnp.where(back_d == row_d, stays, 0.0) + jnp.where(back_d == row_d + 1, 1.0 - stays, 0.0)
    mix = jnp.where(back_a == row_a, mix, 0.0)
    back_z = split_by(split_by(iota((incomes, rows), 1), plane_rows)[1], ill_rows)[0]
    turned = lax.dot_general(spread, transition, NT, precision=HIGHEST_PREC, preferred_element_type=jnp.float32)
    wide = dot(turned, as_float(iota((incomes, rows), 0) == back_z))
    next_mat[...] = wide * mix
    in_z, in_a = split_by(iota((incomes, plane_rows), 1), ill_rows)
    wide = dot(turned, as_float(iota((incomes, plane_rows), 0) == in_z))
    in_row = split_by(iota((rows, plane_rows), 0), group)[1]
    in_row_d, in_row_a = split_by(in_row, ill_rows)
    in_col_a = split_by(iota((rows, plane_rows), 1), ill_rows)[1]
    next_in[...] = jnp.where((in_row_d == durables - 1) & (in_row_a == in_col_a), wide, 0.0)

    def block_of(position):
        block = jnp.zeros(position.shape, jnp.int32)
        for h in range(1, liq_n):
            block = block + jnp.where(position >= h * liq_rows, 1, 0)
        return block, position - block * liq_rows

    target_hi[...], lo = block_of(target_ref[...])
    target_lo[...] = lo.astype(jnp.float32)

    def interpolate(k, tile):
        span = pl.ds(tile * TILE, TILE)
        index = index_ref[span, :]
        low_block, low_lane = block_of(index)
        high_block, high_lane = block_of(index + 1)
        low = high = None
        for h in range(liq_n):
            block = pencil[k * liq_n + h, span, :]
            low_h = jnp.take_along_axis(block, low_lane, axis=1, mode="promise_in_bounds")
            high_h = jnp.take_along_axis(block, high_lane, axis=1, mode="promise_in_bounds")
            low = low_h if h == 0 else jnp.where(low_block == h, low_h, low)
            high = high_h if h == 0 else jnp.where(high_block == h, high_h, high)
        weight = weight_ref[span, :]
        return weight * low + (1.0 - weight) * high

    tiles = rows // TILE
    halves = (range(tiles // 2), range(tiles // 2, tiles))

    def first_policy(half):
        for step in far_first:
            pencil_copy(0, half, step).wait_recv()
        for tile in halves[half]:
            span = pl.ds(tile * TILE, TILE)
            chosen = interpolate(0, tile)
            value_two[span, :] = GROSS_RATE / (chosen * chosen)
            share = jnp.clip(lottery_ref[span, :] + SLOPE_GAIN * (chosen - steady_ref[span, :]), 0.0, 1.0)
            mass = population_ref[span, :]
            mass_low[span, :] = mass * share
            mass_high[span, :] = mass * (1.0 - share)

    lanes = 2 * liq_n
    sub = iota((lanes, liq_rows), 0)
    lane_at = iota((TILE, liq_rows), 1)
    sub_block = jnp.where(sub < liq_n, sub, sub - liq_n)
    lane_row = iota((liq_rows, liq_rows), 0).astype(jnp.float32).astype(jnp.bfloat16)
    one = jnp.ones((liq_rows, liq_rows), jnp.bfloat16)
    nil = jnp.zeros((liq_rows, liq_rows), jnp.bfloat16)
    per_tile = TILE // group

    def scatter_tile(d, tile):
        span = pl.ds(pl.multiple_of(tile * TILE, TILE), TILE)
        low_t, high_t, hi_t, lo_t = mass_low[span, :], mass_high[span, :], target_hi[span, :], target_lo[span, :]
        for zz in range(per_tile):
            z = tile * per_tile + zz
            totals = []
            for a in range(ill_rows):
                k = zz * group + d * ill_rows + a
                both = jnp.where(sub < liq_n, low_t[k : k + 1, :], high_t[k : k + 1, :])
                both = jnp.where(hi_t[k : k + 1, :] == sub_block, both, 0.0)
                rounded = both.astype(jnp.bfloat16).astype(jnp.float32)
                parts = jnp.concatenate([both, both - rounded], axis=0).astype(jnp.bfloat16)
                place = jnp.broadcast_to(lo_t[k : k + 1, :], (2 * TILE, liq_rows)).astype(jnp.bfloat16)
                place = jnp.concatenate([place] * (liq_rows // (2 * TILE)), axis=0)
                hot = jnp.where(lane_row == place, one, nil)
                placed = lax.dot_general(parts, hot, NT, preferred_element_type=jnp.float32)
                placed = placed[:lanes] + placed[lanes:]
                totals.append(placed)
            for dest in range(ill_n * ill_rows):
                out = None
                for a in range(ill_rows):
                    here = as_float(ill_target_ref[d * ill_rows + a, z] == dest) * totals[a]
                    out = here if out is None else out + here
                base = dest // ill_rows * lanes * plane_rows + z * ill_rows + dest % ill_rows
                placed_rows[pl.ds(base, lanes, stride=plane_rows), :] = out

    unroll = tiles // 2

    def scatter(d, half):
        def step(pair, carry):
            for turn in range(unroll):
                scatter_tile(d, halves[half].start + unroll * pair + turn)
            return carry

        lax.fori_loop(0, tiles // 2 // unroll, step, 0)

    def send_terms(d):
        for owner in range(ill_n):
            for piece in range(plane_rows // TILE):
                carried = None
                for h in range(liq_n):
                    low_at = (owner * lanes + h) * plane_rows + piece * TILE
                    low = placed_rows[pl.ds(low_at, TILE), :]
                    moved = pltpu.roll(placed_rows[pl.ds(low_at + liq_n * plane_rows, TILE), :], 1, 1)
                    edge = jnp.where(lane_at > 0, moved, 0.0 if carried is None else carried)
                    carried = moved
                    out_at = ((d * ill_n + owner) * liq_n + h) * plane_rows + piece * TILE
                    terms[pl.ds(out_at, TILE), :] = low + edge
        for step in range(1, ill_n):
            terms_copy(d, step).start()

    def send_owners(d):
        for step in range(1, ill_n):
            terms_copy(d, step).wait_recv()
        for h in range(liq_n):
            start = pl.multiple_of(((d * ill_n + ill_me) * liq_n + h) * plane_rows, TILE)
            total = terms[pl.ds(start, plane_rows), :]
            for step in range(1, ill_n):
                total = total + terms_in[d * (ill_n - 1) + step - 1, pl.ds(h * plane_rows, plane_rows), :]
            owner_sum[d * liq_n + h] = total
        for step in far_first:
            owner_copy(d, step).start()

    def collect(d):
        for step in far_first:
            owner_copy(d, step).wait_recv()
        total = owner_sum[d * liq_n + liq_me]
        for step in range(1, liq_n):
            total = total + owner_in[d * (liq_n - 1) + step - 1]
        settled[pl.ds(d * plane_rows, plane_rows), :] = total
        return total

    def second_policy():
        if relayed:
            for half in range(2):
                pencil_relay(half).wait_recv()
        else:
            for half, step in early:
                pencil_copy(1, half, step).wait_recv()
        for half, step in late:
            pencil_copy(1, half, step).wait_recv()
        for tile in range(tiles):
            consumption_ref[pl.ds(tile * TILE, TILE), :] = interpolate(1, tile)

    first_policy(0)
    scatter(0, 0)
    first_policy(1)
    value_copy(1, value_two).start()
    scatter(0, 1)
    send_terms(0)
    value_copy(1, value_two).wait_recv()
    drifted = dot(second_mat[...], value_two[...]) + dot(second_up[...], near_value[1])
    pencil[liq_n + liq_me] = lax.rsqrt(drifted)
    for half, step in early:
        pencil_copy(1, half, step).start()
    for d in range(1, durables):
        scatter(d, 0)
        if d == 1:
            send_owners(0)
            for half, step in late:
                pencil_copy(1, half, step).start()
        scatter(d, 1)
        send_terms(d)
    for d in range(1, durables):
        send_owners(d)
    if relayed:
        for half, step in early:
            pencil_copy(1, half, step).wait_recv()
        for half in range(2):
            pencil_relay(half).start()

    depart_copy = pltpu.make_async_remote_copy(
        src_ref=depart, dst_ref=depart_in, send_sem=depart_send.at[0], recv_sem=depart_recv.at[0],
        device_id={"dur": jnp.maximum(dur_me - 1, 0)}, device_id_type=MESH_ID,
    )

    depart[...] = (1.0 - stay[0]) * collect(0)

    @pl.when(dur_me > 0)
    def _():
        depart_copy.start()

    for d in range(1, durables):
        collect(d)
    next_ref[...] = dot(next_mat[...], settled[...])
    second_policy()

    @pl.when(dur_me < dur_n - 1)
    def _():
        depart_copy.wait_recv()
        next_ref[...] += dot(next_in[...], depart_in[...])

    value_copy(0, value_ref).wait_send()
    value_copy(1, value_two).wait_send()
    for step in range(1, liq_n):
        for half in range(2):
            pencil_copy(0, half, step).wait_send()
        for d in range(durables):
            owner_copy(d, step).wait_send()
    for half, step in early + late:
        pencil_copy(1, half, step).wait_send()
    if relayed:
        for half in range(2):
            pencil_relay(half).wait_send()
    for step in range(1, ill_n):
        for d in range(durables):
            terms_copy(d, step).wait_send()

    @pl.when(dur_me > 0)
    def _():
        depart_copy.wait_send()


def halves_of(x):
    high = x.astype(jnp.bfloat16)
    return high, (x - high.astype(jnp.float32)).astype(jnp.bfloat16)


def stack_data(x):
    high, low = halves_of(x)
    return jnp.concatenate([high, low, high], axis=0)


def transposed_kernel(
    dims,
    value_hbm, transition_hbm, shock_hbm, drift_hbm, keep_hbm, index_hbm, weight_hbm,
    steady_hbm, lottery_hbm, target_hbm, ill_target_hbm, population_hbm,
    consumption_ref, next_ref,
    value_ref, transition_ref, shock_ref, index_ref, weight_ref, steady_ref, lottery_ref, target_ref,
    population_ref, ill_target_ref, drift_ref, keep_ref, load_sem,
    near_out, near_in, late_out, late_in, side_out, side_in, pair_in,
    pencil_one, value_two, values_in, pencil_two, found_out, found_in, hots, placed, mass_out, depart_out, mass_in,
    near_send, near_recv, late_send, late_recv, goal_send, goal_recv, side_send, side_recv, pair_send, pair_recv,
    value_send, value_recv, found_send, found_recv, mass_send, mass_recv, depart_send, depart_recv, ready_sem,
):
    incomes, durables, ill_rows, liq_rows, liq_n, ill_n, dur_n = dims
    group = durables * ill_rows
    ill_all = ill_n * ill_rows
    part = incomes // liq_n
    per_dest = 3 * ill_rows
    constant = jnp.float32(DISCOUNT * GROSS_RATE)
    f32 = jnp.float32
    liq_me, ill_me, dur_me = (lax.axis_index(name) for name in ("liq", "ill", "dur"))
    far_first = range(liq_n - 1, 0, -1)
    peers = [(step, flip) for step in range(liq_n - 1, -1, -1) for flip in range(ill_n) if step or flip]

    def at(step, flip):
        return {"liq": peer_of(liq_me, step, liq_n), "ill": peer_of(ill_me, flip, ill_n)}

    barrier = pltpu.get_barrier_semaphore()
    for step, flip in peers:
        pl.semaphore_signal(barrier, inc=1, device_id=at(step, flip), device_id_type=MESH_ID)

    @pl.when(dur_me > 0)
    def _():
        pl.semaphore_signal(barrier, inc=1, device_id={"dur": dur_me - 1}, device_id_type=MESH_ID)

    @pl.when(dur_me < dur_n - 1)
    def _():
        pl.semaphore_signal(barrier, inc=1, device_id={"dur": dur_me + 1}, device_id_type=MESH_ID)

    loads = [
        pltpu.make_async_copy(source, held, load_sem.at[slot])
        for slot, (source, held) in enumerate((
            (transition_hbm, transition_ref), (shock_hbm, shock_ref), (value_hbm, value_ref),
            (index_hbm, index_ref), (weight_hbm, weight_ref), (drift_hbm, drift_ref), (ill_target_hbm, ill_target_ref),
            (target_hbm, target_ref), (lottery_hbm, lottery_ref), (steady_hbm, steady_ref),
            (population_hbm, population_ref), (keep_hbm, keep_ref),
        ))
    ]
    for load in loads:
        load.start()

    def rows_at(d, a, z_part):
        return pl.ds(z_part * part * group + d * ill_rows + a, part, stride=group)

    def whole_rows(d, a):
        return pl.ds(d * ill_rows + a, incomes, stride=group)

    kinds = [(d, a) for d in range(durables) for a in range(ill_rows)]
    for load in loads[:2]:
        load.wait()
    transition = transition_ref[...]
    eye = iota((incomes, incomes), 0) == iota((incomes, incomes), 1)
    scaled = dot(jnp.where(eye, constant * shock_ref[...], 0.0), transition)

    def stack_left(x):
        high, low = halves_of(x)
        return jnp.concatenate([high, high, low], axis=1)

    def times(left, x):
        return jnp.dot(left, stack_data(x), preferred_element_type=f32)

    left_one = stack_left(scaled)
    left_two = stack_left(constant * transition)
    loads[2].wait()
    wide = jnp.concatenate([value_ref[whole_rows(d, a), :] for d, a in kinds], axis=1)
    wide = times(left_one, wide)
    for load in loads[3:5]:
        load.wait()
    for k, (d, a) in enumerate(kinds):
        for q in range(liq_n):
            near_out[d * liq_n + q, a] = wide[q * part : (q + 1) * part, k * liq_rows : (k + 1) * liq_rows]
            near_out[d * liq_n + q, ill_rows + a] = index_ref[rows_at(d, a, q), :].astype(f32)
            near_out[d * liq_n + q, 2 * ill_rows + a] = weight_ref[rows_at(d, a, q), :]

    for load in loads[5:7]:
        load.wait()
    column = iota((part, incomes), 1)
    wanted = column == liq_me * part + iota((part, incomes), 0)
    picked = jnp.concatenate(
        [
            jnp.where(wanted, jnp.broadcast_to(ill_target_ref[k : k + 1, :], (part, incomes)), 0)
            for k in range(group)
        ],
        axis=0,
    )
    spread = jnp.dot(
        picked.astype(f32).astype(jnp.bfloat16), jnp.ones((incomes, liq_rows), jnp.bfloat16), preferred_element_type=f32
    )
    row = iota((TILE, liq_rows), 0)
    drifts = jnp.zeros((TILE, liq_rows), f32)
    for a in range(ill_rows):
        drifts = jnp.where(row == a, drift_ref[a], drifts)
    for k, (d, a) in enumerate(kinds):
        side_out[d, a] = spread[k * part : (k + 1) * part]
    for d in range(durables):
        side_out[d, ill_rows] = drifts

    with scope("bar"):
        dur_peers = jnp.minimum(dur_me, 1) + jnp.minimum(dur_n - 1 - dur_me, 1)
        pl.semaphore_wait(barrier, len(peers) + dur_peers)

    @pl.when((dur_me < dur_n - 1) & (ill_me == 0))
    def _():
        pl.semaphore_signal(ready_sem, inc=1, device_id={"dur": dur_me + 1}, device_id_type=MESH_ID)

    def bundle_copy(out_ref, in_ref, send, recv, first, count, step, i):
        liq_there, kept = peer_of(liq_me, step, liq_n), pl.ds(first, count)
        return pltpu.make_async_remote_copy(
            src_ref=out_ref.at[i * liq_n + liq_there, kept], dst_ref=in_ref.at[liq_me * ill_n + ill_me, kept],
            send_sem=send.at[0], recv_sem=recv.at[0], device_id={"liq": liq_there, "ill": i}, device_id_type=MESH_ID,
        )

    def bundle_all(out_ref, in_ref, send, recv, first, count):
        span, kept = pl.ds(0, len(peers)), pl.ds(first, count)
        return pltpu.make_async_remote_copy(
            src_ref=out_ref.at[span, kept], dst_ref=in_ref.at[span, kept], send_sem=send.at[0], recv_sem=recv.at[0],
            device_id=at(0, 1), device_id_type=MESH_ID,
        )

    def near_all():
        return bundle_all(near_out, near_in, near_send, near_recv, 0, per_dest)

    def late_all():
        return bundle_all(late_out, late_in, late_send, late_recv, 0, 2 * ill_rows)

    def goal_all():
        return bundle_all(late_out, late_in, goal_send, goal_recv, 2 * ill_rows, ill_rows)

    def near_copy(step, i):
        return bundle_copy(near_out, near_in, near_send, near_recv, 0, per_dest, step, i)

    def late_copy(step, i):
        return bundle_copy(late_out, late_in, late_send, late_recv, 0, 2 * ill_rows, step, i)

    def goal_copy(step, i):
        return bundle_copy(late_out, late_in, goal_send, goal_recv, 2 * ill_rows, ill_rows, step, i)

    def side_copy(flip):
        there = at(0, flip)
        return pltpu.make_async_remote_copy(
            src_ref=side_out.at[there["ill"]], dst_ref=side_in.at[ill_me],
            send_sem=side_send.at[flip - 1], recv_sem=side_recv.at[flip - 1], device_id=there, device_id_type=MESH_ID,
        )

    def pair_copy(flip):
        there = at(0, flip)
        return pltpu.make_async_remote_copy(
            src_ref=near_out.at[pl.ds(there["ill"] * liq_n, liq_n), pl.ds(ill_rows, 2 * ill_rows)],
            dst_ref=pair_in.at[ill_me], send_sem=pair_send.at[flip - 1], recv_sem=pair_recv.at[flip - 1],
            device_id=there, device_id_type=MESH_ID,
        )

    def start_far(i, make):
        make(liq_n - 1, i).start()

    def start_close(i, make):
        for step in range(liq_n - 2, 0, -1):
            make(step, i).start()

        @pl.when(ill_me != i)
        def _():
            make(0, i).start()

    for flip in range(1, ill_n):
        side_copy(flip).start()

    for load in loads[7:]:
        load.wait()
    for d, a in kinds:
        for q in range(liq_n):
            span = rows_at(d, a, q)
            late_out[d * liq_n + q, a] = lottery_ref[span, :] - SLOPE_GAIN * steady_ref[span, :]
            late_out[d * liq_n + q, ill_rows + a] = population_ref[span, :]
            late_out[d * liq_n + q, 2 * ill_rows + a] = target_ref[span, :].astype(f32)
    start_far(0, near_copy)
    start_far(0, goal_copy)
    start_close(0, near_copy)
    start_close(0, goal_copy)
    for i in range(1, ill_n):
        start_far(i, near_copy)
    start_far(0, late_copy)
    for i in range(1, ill_n):
        start_close(i, near_copy)
    start_close(0, late_copy)
    for i in range(1, ill_n):
        start_far(i, goal_copy)
        start_far(i, late_copy)
        start_close(i, goal_copy)
        start_close(i, late_copy)
    for flip in range(1, ill_n):
        pair_copy(flip).start()

    own_out = ill_me * liq_n + liq_me
    own_in = liq_me * ill_n + ill_me
    for k in range(per_dest):
        near_in[own_in, k] = near_out[own_out, k]
        late_in[own_in, k] = late_out[own_out, k]
    for k in range(ill_rows + 1):
        side_in[ill_me, k] = side_out[ill_me, k]
    for q in range(liq_n):
        for k in range(2 * ill_rows):
            pair_in[ill_me, q, k] = near_out[ill_me * liq_n + q, ill_rows + k]

    @pl.when(dur_me == dur_n - 1)
    def _():
        for a in range(ill_rows):
            mass_in[group + a] = jnp.zeros((incomes, liq_rows), f32)

    stay = [keep_ref[d] for d in range(durables)]
    first_d = as_float(dur_me == 0)
    stay[0] = first_d + (1.0 - first_d) * stay[0]

    def received(ref, kind, h, ag):
        return ref[h * ill_n + ag // ill_rows, kind * ill_rows + ag % ill_rows]

    def interpolate(blocks, index, weight):
        index = index.astype(jnp.int32)
        low_block, low_lane = split_by(index, liq_rows)
        high_block, high_lane = split_by(index + 1, liq_rows)
        low = high = None
        for h, block in enumerate(blocks):
            low_h = jnp.take_along_axis(block, low_lane, axis=1, mode="promise_in_bounds")
            high_h = jnp.take_along_axis(block, high_lane, axis=1, mode="promise_in_bounds")
            low = low_h if h == 0 else jnp.where(low_block == h, low_h, low)
            high = high_h if h == 0 else jnp.where(high_block == h, high_h, high)
        return weight * low + (1.0 - weight) * high

    own_z = pl.ds(pl.multiple_of(liq_me * part, TILE), part)

    def pieces_of(me):
        pair = (me + 1) % ill_n
        first = (pair * ill_rows, min(ill_rows + 1, ill_all - pair * ill_rows))
        rest = [ag for ag in range(ill_all) if not first[0] <= ag < sum(first)]
        return [first, (rest[0], len(rest))]

    def value_copy(me, k, step):
        start, count = pieces_of(me)[k]
        span = pl.ds(start * liq_n, count * liq_n)
        return pltpu.make_async_remote_copy(
            src_ref=value_two.at[span], dst_ref=values_in.at[span, own_z], send_sem=value_send.at[0],
            recv_sem=value_recv.at[k], device_id={"liq": peer_of(liq_me, step, liq_n)}, device_id_type=MESH_ID,
        )

    def value_all(k, count):
        span = pl.ds(0, (liq_n - 1) * count)
        return pltpu.make_async_remote_copy(
            src_ref=values_in.at[span], dst_ref=values_in.at[span], send_sem=value_send.at[0],
            recv_sem=value_recv.at[k], device_id=at(1, 0), device_id_type=MESH_ID,
        )

    def on_each_core(part_of):
        for me in range(ill_n):

            @pl.when(ill_me == me)
            def _():
                part_of(me)

    with scope("near"):
        for flip in range(1, ill_n):
            side_copy(flip).wait_recv()
        near_all().wait_recv()

    with scope("policy"):
        for ag in range(ill_all):
            i, a = divmod(ag, ill_rows)
            own = jnp.broadcast_to(side_in[i, ill_rows, a : a + 1, :], (TILE, liq_rows))
            for h in range(liq_n):
                drifted = own * received(near_in, 0, h, ag) + (1.0 - own) * received(near_in, 0, h, min(ag + 1, ill_all - 1))
                pencil_one[ag * liq_n + h] = lax.rsqrt(drifted)

        def policy(me):
            pieces = pieces_of(me)

            def loaded(k):
                start, count = pieces[k]
                return [
                    (
                        ag,
                        [pencil_one[ag * liq_n + h] for h in range(liq_n)],
                        [(received(near_in, 1, h, ag), received(near_in, 2, h, ag)) for h in range(liq_n)],
                    )
                    for ag in range(start, start + count)
                ]

            ahead = loaded(0)
            for k in range(len(pieces)):
                for ag, blocks, states in ahead:
                    for h, (index, weight) in enumerate(states):
                        chosen = interpolate(blocks, index, weight)
                        found = GROSS_RATE / (chosen * chosen)
                        value_two[ag * liq_n + h] = found
                        values_in[ag * liq_n + h, own_z, :] = found
                        pencil_one[ill_all * liq_n + ag * liq_n + h] = chosen
                ahead = loaded(k + 1) if k + 1 < len(pieces) else []
                for step in far_first:
                    if k == 0 or step == liq_n - 1 or me > 0:
                        value_copy(me, k, step).start()

        on_each_core(policy)

    half = liq_rows // 2
    cuts = 2 * liq_n
    sub = iota((cuts, liq_rows), 0).astype(f32)
    lane_at = iota((TILE, liq_rows), 1)
    lane_row = iota((half, liq_rows), 0).astype(f32).astype(jnp.bfloat16)
    one = jnp.ones((half, liq_rows), jnp.bfloat16)
    nil = jnp.zeros((half, liq_rows), jnp.bfloat16)

    with scope("goal"):
        goal_all().wait_recv()
    with scope("hots"):
        cut_at = {}
        for ag in range(ill_all):
            places = []
            for h in range(liq_n):
                target = received(late_in, 2, h, ag)
                cut = jnp.zeros(target.shape, f32)
                for other in range(1, cuts):
                    cut = cut + jnp.where(target >= other * half, 1.0, 0.0)
                cut_at[ag, h] = cut
                places.append(target - half * cut)
            for s in range(part):
                for h in range(liq_n):
                    place = jnp.broadcast_to(places[h][s : s + 1, :], (2 * TILE, liq_rows)).astype(jnp.bfloat16)
                    place = jnp.concatenate([place] * (half // (2 * TILE)), axis=0)
                    hots[s * ill_all + ag, :, h * liq_rows : (h + 1) * liq_rows] = jnp.where(lane_row == place, one, nil)
    with scope("late"):
        late_all().wait_recv()
    with scope("scatter"):
        held = {}
        for ag in range(ill_all):
            for h in range(liq_n):
                chosen = pencil_one[ill_all * liq_n + ag * liq_n + h]
                share = jnp.clip(received(late_in, 0, h, ag) + SLOPE_GAIN * chosen, 0.0, 1.0)
                mass = received(late_in, 1, h, ag)
                held[ag, h] = (mass * share, mass * (1.0 - share), cut_at[ag, h])
        for s in range(part):
            totals, to_row = [], []
            for ag in range(ill_all):
                lefts = []
                for h in range(liq_n):
                    low_t, high_t, cut_t = (x[s : s + 1, :] for x in held[ag, h])
                    here = cut_t == sub
                    both = jnp.concatenate([jnp.where(here, low_t, 0.0), jnp.where(here, high_t, 0.0)], axis=0)
                    first = both.astype(jnp.bfloat16)
                    lefts.append(jnp.concatenate([first, (both - first.astype(f32)).astype(jnp.bfloat16)], axis=0))
                found = lax.dot_general(
                    jnp.concatenate(lefts, axis=1), hots[s * ill_all + ag], NT, preferred_element_type=f32
                )
                totals.append(found[: 2 * cuts] + found[2 * cuts :])
                to_row.append(jnp.broadcast_to(side_in[ag // ill_rows, ag % ill_rows, s : s + 1, :half], (2 * cuts, half)))
            for dest in range(ill_all):
                out = None
                for ag in range(ill_all):
                    here = jnp.where(to_row[ag] == dest, totals[ag], 0.0)
                    out = here if out is None else out + here
                placed[pl.ds(dest * 2 * cuts * part + s, 2 * cuts, stride=part), :half] = out

    with scope("massout"):
        def joined(dest, side, h):
            start = ((dest * 2 + side) * cuts + 2 * h) * part
            return jnp.concatenate(
                [placed[pl.ds(start, part), :half], placed[pl.ds(start + part, part), :half]], axis=1
            )

        for dest in range(ill_all):
            carried = None
            for h in range(liq_n):
                low = joined(dest, 0, h)
                moved = pltpu.roll(joined(dest, 1, h), 1, 1)
                total = low + jnp.where(lane_at > 0, moved, 0.0 if carried is None else carried)
                carried = moved
                mass_out[h * ill_all + dest] = total
                depart_out[h * ill_all + dest] = (1.0 - stay[0]) * total

    def mass_copy(step, flip):
        there = at(step, flip)
        return pltpu.make_async_remote_copy(
            src_ref=mass_out.at[pl.ds(there["liq"] * ill_all + there["ill"] * ill_rows, ill_rows)],
            dst_ref=mass_in.at[pl.ds(ill_me * ill_rows, ill_rows), own_z],
            send_sem=mass_send.at[0], recv_sem=mass_recv.at[0], device_id=there, device_id_type=MESH_ID,
        )

    def mass_all():
        span = pl.ds(0, len(peers) * ill_rows)
        return pltpu.make_async_remote_copy(
            src_ref=mass_out.at[span], dst_ref=mass_out.at[span], send_sem=mass_send.at[0],
            recv_sem=mass_recv.at[0], device_id=at(0, 1), device_id_type=MESH_ID,
        )

    def depart_all(count):
        span = pl.ds(0, count * ill_rows)
        return pltpu.make_async_remote_copy(
            src_ref=depart_out.at[span], dst_ref=depart_out.at[span], send_sem=depart_send.at[0],
            recv_sem=depart_recv.at[0], device_id=at(0, 1), device_id_type=MESH_ID,
        )

    def depart_copy(step, i):
        liq_there = peer_of(liq_me, step, liq_n)
        return pltpu.make_async_remote_copy(
            src_ref=depart_out.at[pl.ds(liq_there * ill_all + i * ill_rows, ill_rows)],
            dst_ref=mass_in.at[pl.ds(group, ill_rows), own_z],
            send_sem=depart_send.at[0], recv_sem=depart_recv.at[0],
            device_id={"dur": jnp.maximum(dur_me - 1, 0), "liq": liq_there, "ill": i}, device_id_type=MESH_ID,
        )

    departs = (dur_me > 0) & (ill_me == 0)

    @pl.when(departs)
    def _():
        pl.semaphore_wait(ready_sem, 1)
        for step in range(liq_n - 1, -1, -1):
            for i in range(ill_n):
                depart_copy(step, i).start()

    def send_rest(me):
        for step in range(liq_n - 2, 0, -1):
            value_copy(me, 1, step).start()

    pl.when(ill_me == 0)(functools.partial(send_rest, 0))

    for step, flip in peers:
        mass_copy(step, flip).start()
    for a in range(ill_rows):
        mass_in[ill_me * ill_rows + a, own_z, :] = mass_out[liq_me * ill_all + ill_me * ill_rows + a]

    def found_copy(flip):
        there = at(0, flip)
        return pltpu.make_async_remote_copy(
            src_ref=found_out.at[flip - 1], dst_ref=found_in.at[flip - 1],
            send_sem=found_send.at[flip - 1], recv_sem=found_recv.at[flip - 1], device_id=there, device_id_type=MESH_ID,
        )

    for flip in range(1, ill_n):
        side_copy(flip).wait_send()
        pair_copy(flip).wait_send()
        pair_copy(flip).wait_recv()
    near_all().wait_send()
    late_all().wait_send()
    goal_all().wait_send()
    def expect(ag):
        wide = jnp.concatenate([values_in[ag * liq_n + h] for h in range(liq_n)], axis=1)
        return times(left_two, wide)

    def consume(i, expected, store_tile):
        for a in range(ill_rows):
            own = jnp.broadcast_to(side_in[i, ill_rows, a : a + 1, :], (incomes, liq_rows))
            own = jnp.concatenate([own] * liq_n, axis=1)
            found = lax.rsqrt(own * expected[a] + (1.0 - own) * expected[a + 1])
            for h in range(liq_n):
                pencil_two[a * liq_n + h] = found[:, h * liq_rows : (h + 1) * liq_rows]
        for a in range(ill_rows):
            for q in range(liq_n):
                blocks = [pencil_two[a * liq_n + h, pl.ds(q * part, part), :] for h in range(liq_n)]
                store_tile(a, q, interpolate(blocks, pair_in[i, q, a], pair_in[i, q, ill_rows + a]))

    def store_found(a, q, found):
        found_out[0, q * ill_rows + a] = found

    def store_own(a, q, found):
        consumption_ref[rows_at(ill_me, a, q), :] = found

    def second(me):
        pair, is_last = (me + 1) % ill_n, me == ill_n - 1
        with scope("values"):
            value_all(0, pieces_of(me)[0][1]).wait_recv()
        with scope("second_a"):
            expected = [expect(pair * ill_rows + a) for a in range(ill_rows)]
            lowest = expected[0]
            above = pair * ill_rows + ill_rows
            expected.append(expected[-1] if above == ill_all else expect(above))
            consume(pair, expected, store_found)
            found_copy(1).start()
        with scope("values_b"):
            value_all(1, pieces_of(me)[1][1]).wait_recv()
        with scope("second_b"):
            expected = [expect(me * ill_rows + a) for a in range(ill_rows)]
            expected.append(expected[-1] if is_last else lowest)
            consume(me, expected, store_own)

    on_each_core(second)

    with scope("sends"):
        value_all(0, ill_all).wait_send()
        mass_all().wait_send()

        @pl.when(departs)
        def _():
            depart_all(liq_n * ill_n).wait_send()

    with scope("found"):
        for flip in range(1, ill_n):
            found_copy(flip).wait_send()
            found_copy(flip).wait_recv()
            for q in range(liq_n):
                for a in range(ill_rows):
                    consumption_ref[rows_at(peer_of(ill_me, flip, ill_n), a, q), :] = found_in[flip - 1, q * ill_rows + a]

    with scope("mass"):
        mass_all().wait_recv()

        @pl.when(dur_me < dur_n - 1)
        def _():
            depart_all(liq_n).wait_recv()

    with scope("next"):
        settled = []
        for d, a in kinds:
            after = mass_in[(d + 1) * ill_rows + a]
            if d + 1 < durables:
                after = (1.0 - stay[d + 1]) * after
            settled.append(stay[d] * mass_in[d * ill_rows + a] + after)
        high, low = halves_of(transition)
        found = lax.dot_general(
            jnp.concatenate([high, high, low], axis=0), stack_data(jnp.concatenate(settled, axis=1)),
            (((0,), (0,)), ((), ())), preferred_element_type=f32,
        )
        for k, (d, a) in enumerate(kinds):
            for q in range(liq_n):
                next_ref[rows_at(d, a, q), :] = found[q * part : (q + 1) * part, k * liq_rows : (k + 1) * liq_rows]


def store(consumption_ref, next_ref, consumption_hbm, next_hbm, sem):
    copies = [
        pltpu.make_async_copy(consumption_ref, consumption_hbm, sem.at[0]),
        pltpu.make_async_copy(next_ref, next_hbm, sem.at[1]),
    ]
    for copy in copies:
        copy.start()
    for copy in copies:
        copy.wait()


def window_scratch(dims):
    incomes, durables, ill_rows, liq_rows, liq_n, ill_n, dur_n = dims
    f32 = jnp.float32
    rows, plane_rows = incomes * durables * ill_rows, incomes * ill_rows
    block = (rows, liq_rows)
    dma = pltpu.SemaphoreType.DMA
    return [
        pltpu.VMEM(block, f32),
        pltpu.VMEM((incomes, incomes), f32),
        pltpu.VMEM((1, incomes), f32),
        pltpu.VMEM(block, jnp.int32),
        pltpu.VMEM(block, f32),
        pltpu.VMEM(block, f32),
        pltpu.VMEM(block, f32),
        pltpu.VMEM(block, jnp.int32),
        pltpu.VMEM(block, f32),
        pltpu.SMEM((ill_rows,), f32),
        pltpu.SMEM((durables,), f32),
        pltpu.SMEM((durables * ill_rows, incomes), jnp.int32),
        dma((12,)),
        pltpu.VMEM((rows, rows), f32),
        pltpu.VMEM((rows, rows), f32),
        pltpu.VMEM((rows, rows), f32),
        pltpu.VMEM((rows, rows), f32),
        pltpu.VMEM((rows, rows), f32),
        pltpu.VMEM((rows, plane_rows), f32),
        pltpu.VMEM((2,) + block, f32),
        pltpu.VMEM(block, f32),
        pltpu.VMEM((2 * liq_n,) + block, f32),
        pltpu.VMEM(block, f32),
        pltpu.VMEM(block, f32),
        pltpu.VMEM(block, jnp.int32),
        pltpu.VMEM(block, f32),
        pltpu.VMEM((2 * ill_n * liq_n * plane_rows, liq_rows), f32),
        pltpu.VMEM((ill_n * liq_n * rows, liq_rows), f32),
        pltpu.VMEM((durables * (ill_n - 1), liq_n * plane_rows, liq_rows), f32),
        pltpu.VMEM((durables * liq_n, plane_rows, liq_rows), f32),
        pltpu.VMEM((durables * (liq_n - 1), plane_rows, liq_rows), f32),
        pltpu.VMEM(block, f32),
        pltpu.VMEM((plane_rows, liq_rows), f32),
        pltpu.VMEM((plane_rows, liq_rows), f32),
        dma((2,)),
        dma((2,)),
        dma((4 * liq_n,)),
        dma((4 * liq_n,)),
        dma((durables * (ill_n - 1),)),
        dma((durables * (ill_n - 1),)),
        dma((durables * (liq_n - 1),)),
        dma((durables * (liq_n - 1),)),
        dma((1,)),
        dma((1,)),
    ]


def transposed_scratch(dims):
    incomes, durables, ill_rows, liq_rows, liq_n, ill_n, dur_n = dims
    f32 = jnp.float32
    block = (incomes * durables * ill_rows, liq_rows)
    dma = pltpu.SemaphoreType.DMA
    part = incomes // liq_n
    ill_all = ill_n * ill_rows
    tiles = lambda n: pltpu.VMEM((n, part, liq_rows), f32)
    slabs = lambda n: pltpu.VMEM((n, incomes, liq_rows), f32)
    bundles = pltpu.VMEM((durables * liq_n, 3 * ill_rows, part, liq_rows), f32)
    return [
        pltpu.VMEM(block, f32),
        pltpu.VMEM((incomes, incomes), f32),
        pltpu.VMEM((1, incomes), f32),
        pltpu.VMEM(block, jnp.int32),
        pltpu.VMEM(block, f32),
        pltpu.VMEM(block, f32),
        pltpu.VMEM(block, f32),
        pltpu.VMEM(block, jnp.int32),
        pltpu.VMEM(block, f32),
        pltpu.VMEM((durables * ill_rows, incomes), jnp.int32),
        pltpu.SMEM((ill_rows,), f32),
        pltpu.SMEM((durables,), f32),
        dma((12,)),
        bundles,
        bundles,
        bundles,
        bundles,
        pltpu.VMEM((durables, ill_rows + 1, TILE, liq_rows), f32),
        pltpu.VMEM((ill_n, ill_rows + 1, TILE, liq_rows), f32),
        pltpu.VMEM((ill_n, liq_n, 2 * ill_rows, part, liq_rows), f32),
        tiles(2 * ill_all * liq_n),
        tiles(ill_all * liq_n),
        slabs(ill_all * liq_n),
        slabs(ill_rows * liq_n),
        pltpu.VMEM((ill_n - 1, liq_n * ill_rows, part, liq_rows), f32),
        pltpu.VMEM((ill_n - 1, liq_n * ill_rows, part, liq_rows), f32),
        pltpu.VMEM((part * ill_all, liq_rows // 2, liq_n * liq_rows), jnp.bfloat16),
        pltpu.VMEM((4 * liq_n * ill_all * part, liq_rows), f32),
        tiles(liq_n * ill_all),
        tiles(liq_n * ill_all),
        slabs((durables + 1) * ill_rows),
    ] + [
        dma((n,)) for n in (1, 1, 1, 1, 1, 1, 1, 1, 1, 1, 1, 2, 1, 1, 1, 1, 1, 1)
    ] + [pltpu.SemaphoreType.REGULAR]


def body(
    marginal_value,
    transition,
    discount_shock,
    illiquid_drift,
    durable_keep,
    bracket_index,
    bracket_weight,
    steady_consumption,
    lottery_weight,
    liquid_target,
    illiquid_target,
    population,
):
    shape = marginal_value.shape
    incomes, durables, ill_rows, liq_rows = shape
    liq_n, ill_n, dur_n = (lax.axis_size(name) for name in ("liq", "ill", "dur"))
    rows = incomes * durables * ill_rows
    flat = lambda x: x.reshape(rows, liq_rows)
    anywhere = pl.BlockSpec(memory_space=pl.ANY)
    f32 = jnp.float32
    block = (rows, liq_rows)
    dma = pltpu.SemaphoreType.DMA
    vmem = pl.BlockSpec(memory_space=pltpu.VMEM)
    held = pltpu.VMEM(block, f32)
    result = jax.ShapeDtypeStruct(block, f32)
    dims = (incomes, durables, ill_rows, liq_rows, liq_n, ill_n, dur_n)
    transposed = (
        ill_n == 2 and durables == ill_n and liq_n * 2 == TILE and incomes == liq_n * TILE and ill_rows < TILE
    )
    if transposed:
        step_kernel, scratch, name = transposed_kernel, transposed_scratch(dims), "transposed_window"
    else:
        step_kernel, scratch, name = kernel, window_scratch(dims), "window"
    outs = pl.pallas_call(
        functools.partial(step_kernel, dims),
        out_shape=(held, held),
        in_specs=[anywhere] * 12,
        out_specs=(vmem, vmem),
        scratch_shapes=scratch,
        compiler_params=pltpu.CompilerParams(collective_id=0, has_side_effects=True),
        name=name,
    )(
        flat(marginal_value),
        transition,
        discount_shock.reshape(1, incomes),
        illiquid_drift,
        durable_keep,
        flat(bracket_index),
        flat(bracket_weight),
        flat(steady_consumption),
        flat(lottery_weight),
        flat(liquid_target),
        jnp.transpose(illiquid_target, (1, 2, 0)).reshape(durables * ill_rows, incomes),
        flat(population),
    )
    outs = pl.pallas_call(
        store,
        out_shape=(result, result),
        in_specs=[vmem, vmem],
        out_specs=(anywhere, anywhere),
        scratch_shapes=[dma((2,))],
        name="store",
    )(*(pltpu.with_memory_space_constraint(out, pltpu.VMEM) for out in outs))
    return tuple(out.reshape(shape) for out in outs)


def solution(mesh):
    in_specs = (
        P(None, "dur", "ill", "liq"),
        P(),
        P(),
        P("ill"),
        P("dur"),
        P(None, "dur", "ill", "liq"),
        P(None, "dur", "ill", "liq"),
        P(None, "dur", "ill", "liq"),
        P(None, "dur", "ill", "liq"),
        P(None, "dur", "ill", "liq"),
        P(None, "dur", "ill"),
        P(None, "dur", "ill", "liq"),
    )
    out_specs = (P(None, "dur", "ill", "liq"), P(None, "dur", "ill", "liq"))
    return jax.shard_map(body, mesh=mesh, in_specs=in_specs, out_specs=out_specs, check_vma=False)
```

```python
import contextlib
import functools

import jax
import jax.numpy as jnp
from jax import lax
from jax.experimental import pallas as pl
from jax.experimental.pallas import tpu as pltpu
from jax.sharding import PartitionSpec as P

DISCOUNT = 0.96
GROSS_RATE = 1.01
SLOPE_GAIN = 0.5
HIGHEST_PREC = lax.Precision.HIGHEST
MESH_ID = pl.DeviceIdType.MESH
NT = (((1,), (1,)), ((), ()))
TILE = 8


def scope(name):
    return contextlib.nullcontext()


def split_by(x, n):
    if n & (n - 1) == 0:
        return x >> (n.bit_length() - 1), x & (n - 1)
    return lax.div(x, jnp.int32(n)), lax.rem(x, jnp.int32(n))


def dot(a, b):
    return jnp.dot(a, b, precision=HIGHEST_PREC, preferred_element_type=jnp.float32)


def iota(shape, axis):
    return lax.broadcasted_iota(jnp.int32, shape, axis)


def as_float(flag):
    return jnp.where(flag, jnp.float32(1.0), jnp.float32(0.0))


def peer_of(me, step, n):
    if n & (n - 1):
        return lax.rem(me + step, n)
    out = me
    for bit in range(n.bit_length() - 1):
        if step >> bit & 1:
            out = out + (1 - 2 * lax.rem(lax.div(me, jnp.int32(1 << bit)), jnp.int32(2))) * (1 << bit)
    return out


def kernel(
    dims,
    value_hbm, transition_hbm, shock_hbm, drift_hbm, keep_hbm, index_hbm, weight_hbm,
    steady_hbm, lottery_hbm, target_hbm, ill_target_hbm, population_hbm,
    consumption_ref, next_ref,
    value_ref, transition_ref, shock_ref, index_ref, weight_ref, steady_ref, lottery_ref, target_ref,
    population_ref, drift_ref, keep_ref, ill_target_ref, load_sem,
    first_mat, first_up, second_mat, second_up, next_mat, next_in,
    near_value, value_two, pencil, mass_low, mass_high, target_hi, target_lo,
    placed_rows, terms, terms_in, owner_sum, owner_in, settled, depart, depart_in,
    value_send, value_recv, pencil_send, pencil_recv, terms_send, terms_recv,
    owner_send, owner_recv, depart_send, depart_recv,
):
    incomes, durables, ill_rows, liq_rows, liq_n, ill_n, dur_n = dims
    group = durables * ill_rows
    rows = incomes * group
    half_rows = rows // 2
    plane_rows = incomes * ill_rows
    liq_me, ill_me, dur_me = (lax.axis_index(name) for name in ("liq", "ill", "dur"))
    far_first = range(liq_n - 1, 0, -1)

    barrier = pltpu.get_barrier_semaphore()
    for step in far_first:
        pl.semaphore_signal(barrier, inc=1, device_id={"liq": peer_of(liq_me, step, liq_n)}, device_id_type=MESH_ID)
    for step in range(1, ill_n):
        pl.semaphore_signal(barrier, inc=1, device_id={"ill": peer_of(ill_me, step, ill_n)}, device_id_type=MESH_ID)

    @pl.when(dur_me > 0)
    def _():
        pl.semaphore_signal(barrier, inc=1, device_id={"dur": dur_me - 1}, device_id_type=MESH_ID)

    @pl.when(dur_me < dur_n - 1)
    def _():
        pl.semaphore_signal(barrier, inc=1, device_id={"dur": dur_me + 1}, device_id_type=MESH_ID)

    loads = [
        pltpu.make_async_copy(source, held, load_sem.at[slot])
        for slot, (source, held) in enumerate((
            (transition_hbm, transition_ref), (shock_hbm, shock_ref), (drift_hbm, drift_ref), (value_hbm, value_ref),
            (keep_hbm, keep_ref), (ill_target_hbm, ill_target_ref),
            (index_hbm, index_ref), (weight_hbm, weight_ref), (target_hbm, target_ref),
            (lottery_hbm, lottery_ref), (steady_hbm, steady_ref), (population_hbm, population_ref),
        ))
    ]
    for load in loads:
        load.start()
    for load in loads[:3]:
        load.wait()

    transition = transition_ref[...]
    row_z, row_rest = split_by(iota((rows, rows), 0), group)
    col_z, col_rest = split_by(iota((rows, rows), 1), group)
    row_d, row_a = split_by(row_rest, ill_rows)
    col_d, col_a = split_by(col_rest, ill_rows)
    spread = as_float(split_by(iota((rows, incomes), 0), group)[0] == iota((rows, incomes), 1))
    spread_t = as_float(iota((incomes, rows), 0) == split_by(iota((incomes, rows), 1), group)[0])
    drift = jnp.zeros((rows, rows), jnp.float32)
    for a in range(ill_rows):
        drift = jnp.where(row_a == a, drift_ref[a], drift)
    is_last = as_float(ill_me == ill_n - 1)
    same_d = row_d == col_d
    top_row = row_a == ill_rows - 1
    local = jnp.where(col_a == row_a, drift, 0.0)
    local = local + jnp.where(col_a == row_a + 1, 1.0 - drift, 0.0)
    local = local + jnp.where(top_row & (col_a == ill_rows - 1), is_last * (1.0 - drift), 0.0)
    local = jnp.where(same_d, local, 0.0)
    upper = jnp.where(same_d & top_row & (col_a == 0), (1.0 - is_last) * (1.0 - drift), 0.0)
    constant = jnp.float32(DISCOUNT * GROSS_RATE)
    eye = iota((incomes, incomes), 0) == iota((incomes, incomes), 1)
    scaled = dot(jnp.where(eye, constant * shock_ref[...], 0.0), transition)
    wide = dot(dot(spread, scaled), spread_t)
    first_mat[...] = wide * local
    first_up[...] = wide * upper

    dur_peers = jnp.minimum(dur_me, 1) + jnp.minimum(dur_n - 1 - dur_me, 1)
    pl.semaphore_wait(barrier, liq_n - 1 + ill_n - 1 + dur_peers)

    ill_below = lax.rem(ill_me + ill_n - 1, ill_n)

    def value_copy(k, source):
        return pltpu.make_async_remote_copy(
            src_ref=source, dst_ref=near_value.at[k], send_sem=value_send.at[k],
            recv_sem=value_recv.at[k], device_id={"ill": ill_below}, device_id_type=MESH_ID,
        )

    def pencil_copy(k, half, step):
        slot = (k * 2 + half) * liq_n + step
        part = pencil.at[k * liq_n + liq_me, pl.ds(half * half_rows, half_rows)]
        return pltpu.make_async_remote_copy(
            src_ref=part, dst_ref=part, send_sem=pencil_send.at[slot], recv_sem=pencil_recv.at[slot],
            device_id={"liq": peer_of(liq_me, step, liq_n)}, device_id_type=MESH_ID,
        )

    def pencil_relay(half):
        near, far = (1, 2) if half == 0 else (2, 1)
        slot = (2 + half) * liq_n
        part = pencil.at[liq_n + peer_of(liq_me, near, liq_n), pl.ds(half * half_rows, half_rows)]
        return pltpu.make_async_remote_copy(
            src_ref=part, dst_ref=part, send_sem=pencil_send.at[slot], recv_sem=pencil_recv.at[slot],
            device_id={"liq": peer_of(liq_me, far, liq_n)}, device_id_type=MESH_ID,
        )

    relayed = liq_n == 4
    if relayed:
        early, late = [(0, 1), (1, 2)], [(1, 1), (0, 2)]
    else:
        early, late = [(0, step) for step in far_first], [(1, step) for step in far_first]

    def terms_copy(d, step):
        peer = peer_of(ill_me, step, ill_n)
        slot = d * (ill_n - 1) + step - 1
        return pltpu.make_async_remote_copy(
            src_ref=terms.at[pl.ds((d * ill_n + peer) * (liq_n * plane_rows), liq_n * plane_rows)],
            dst_ref=terms_in.at[slot], send_sem=terms_send.at[slot], recv_sem=terms_recv.at[slot],
            device_id={"ill": peer}, device_id_type=MESH_ID,
        )

    def owner_copy(d, step):
        peer = peer_of(liq_me, step, liq_n)
        slot = d * (liq_n - 1) + step - 1
        return pltpu.make_async_remote_copy(
            src_ref=owner_sum.at[d * liq_n + peer], dst_ref=owner_in.at[slot],
            send_sem=owner_send.at[slot], recv_sem=owner_recv.at[slot],
            device_id={"liq": peer}, device_id_type=MESH_ID,
        )

    loads[3].wait()
    value_copy(0, value_ref).start()
    drifted = dot(first_mat[...], value_ref[...])
    value_copy(0, value_ref).wait_recv()
    drifted = drifted + dot(first_up[...], near_value[0])
    pencil[liq_me] = lax.rsqrt(drifted)
    for half in range(2):
        for step in far_first:
            pencil_copy(0, half, step).start()

    wide = constant * dot(dot(spread, transition), spread_t)
    second_mat[...] = wide * local
    second_up[...] = wide * upper

    for load in loads[4:]:
        load.wait()

    first_d = as_float(dur_me == 0)
    stay = [keep_ref[d] for d in range(durables)]
    stay[0] = first_d + (1.0 - first_d) * stay[0]
    back_d, back_rest = split_by(iota((rows, rows), 1), plane_rows)
    back_a = split_by(back_rest, ill_rows)[1]
    stays = jnp.zeros((rows, rows), jnp.float32)
    for d in range(durables):
        stays = jnp.where(back_d == d, stay[d], stays)
    mix = jnp.where(back_d == row_d, stays, 0.0) + jnp.where(back_d == row_d + 1, 1.0 - stays, 0.0)
    mix = jnp.where(back_a == row_a, mix, 0.0)
    back_z = split_by(split_by(iota((incomes, rows), 1), plane_rows)[1], ill_rows)[0]
    turned = lax.dot_general(spread, transition, NT, precision=HIGHEST_PREC, preferred_element_type=jnp.float32)
    wide = dot(turned, as_float(iota((incomes, rows), 0) == back_z))
    next_mat[...] = wide * mix
    in_z, in_a = split_by(iota((incomes, plane_rows), 1), ill_rows)
    wide = dot(turned, as_float(iota((incomes, plane_rows), 0) == in_z))
    in_row = split_by(iota((rows, plane_rows), 0), group)[1]
    in_row_d, in_row_a = split_by(in_row, ill_rows)
    in_col_a = split_by(iota((rows, plane_rows), 1), ill_rows)[1]
    next_in[...] = jnp.where((in_row_d == durables - 1) & (in_row_a == in_col_a), wide, 0.0)

    def block_of(position):
        block = jnp.zeros(position.shape, jnp.int32)
        for h in range(1, liq_n):
            block = block + jnp.where(position >= h * liq_rows, 1, 0)
        return block, position - block * liq_rows

    target_hi[...], lo = block_of(target_ref[...])
    target_lo[...] = lo.astype(jnp.float32)

    def interpolate(k, tile):
        span = pl.ds(tile * TILE, TILE)
        index = index_ref[span, :]
        low_block, low_lane = block_of(index)
        high_block, high_lane = block_of(index + 1)
        low = high = None
        for h in range(liq_n):
            block = pencil[k * liq_n + h, span, :]
            low_h = jnp.take_along_axis(block, low_lane, axis=1, mode="promise_in_bounds")
            high_h = jnp.take_along_axis(block, high_lane, axis=1, mode="promise_in_bounds")
            low = low_h if h == 0 else jnp.where(low_block == h, low_h, low)
            high = high_h if h == 0 else jnp.where(high_block == h, high_h, high)
        weight = weight_ref[span, :]
        return weight * low + (1.0 - weight) * high

    tiles = rows // TILE
    halves = (range(tiles // 2), range(tiles // 2, tiles))

    def first_policy(half):
        for step in far_first:
            pencil_copy(0, half, step).wait_recv()
        for tile in halves[half]:
            span = pl.ds(tile * TILE, TILE)
            chosen = interpolate(0, tile)
            value_two[span, :] = GROSS_RATE / (chosen * chosen)
            share = jnp.clip(lottery_ref[span, :] + SLOPE_GAIN * (chosen - steady_ref[span, :]), 0.0, 1.0)
            mass = population_ref[span, :]
            mass_low[span, :] = mass * share
            mass_high[span, :] = mass * (1.0 - share)

    lanes = 2 * liq_n
    sub = iota((lanes, liq_rows), 0)
    lane_at = iota((TILE, liq_rows), 1)
    sub_block = jnp.where(sub < liq_n, sub, sub - liq_n)
    lane_row = iota((liq_rows, liq_rows), 0).astype(jnp.float32).astype(jnp.bfloat16)
    one = jnp.ones((liq_rows, liq_rows), jnp.bfloat16)
    nil = jnp.zeros((liq_rows, liq_rows), jnp.bfloat16)
    per_tile = TILE // group

    def scatter_tile(d, tile):
        span = pl.ds(pl.multiple_of(tile * TILE, TILE), TILE)
        low_t, high_t, hi_t, lo_t = mass_low[span, :], mass_high[span, :], target_hi[span, :], target_lo[span, :]
        for zz in range(per_tile):
            z = tile * per_tile + zz
            totals = []
            for a in range(ill_rows):
                k = zz * group + d * ill_rows + a
                both = jnp.where(sub < liq_n, low_t[k : k + 1, :], high_t[k : k + 1, :])
                both = jnp.where(hi_t[k : k + 1, :] == sub_block, both, 0.0)
                rounded = both.astype(jnp.bfloat16).astype(jnp.float32)
                parts = jnp.concatenate([both, both - rounded], axis=0).astype(jnp.bfloat16)
                place = jnp.broadcast_to(lo_t[k : k + 1, :], (2 * TILE, liq_rows)).astype(jnp.bfloat16)
                place = jnp.concatenate([place] * (liq_rows // (2 * TILE)), axis=0)
                hot = jnp.where(lane_row == place, one, nil)
                placed = lax.dot_general(parts, hot, NT, preferred_element_type=jnp.float32)
                placed = placed[:lanes] + placed[lanes:]
                totals.append(placed)
            for dest in range(ill_n * ill_rows):
                out = None
                for a in range(ill_rows):
                    here = as_float(ill_target_ref[d * ill_rows + a, z] == dest) * totals[a]
                    out = here if out is None else out + here
                base = dest // ill_rows * lanes * plane_rows + z * ill_rows + dest % ill_rows
                placed_rows[pl.ds(base, lanes, stride=plane_rows), :] = out

    unroll = tiles // 2

    def scatter(d, half):
        def step(pair, carry):
            for turn in range(unroll):
                scatter_tile(d, halves[half].start + unroll * pair + turn)
            return carry

        lax.fori_loop(0, tiles // 2 // unroll, step, 0)

    def send_terms(d):
        for owner in range(ill_n):
            for piece in range(plane_rows // TILE):
                carried = None
                for h in range(liq_n):
                    low_at = (owner * lanes + h) * plane_rows + piece * TILE
                    low = placed_rows[pl.ds(low_at, TILE), :]
                    moved = pltpu.roll(placed_rows[pl.ds(low_at + liq_n * plane_rows, TILE), :], 1, 1)
                    edge = jnp.where(lane_at > 0, moved, 0.0 if carried is None else carried)
                    carried = moved
                    out_at = ((d * ill_n + owner) * liq_n + h) * plane_rows + piece * TILE
                    terms[pl.ds(out_at, TILE), :] = low + edge
        for step in range(1, ill_n):
            terms_copy(d, step).start()

    def send_owners(d):
        for step in range(1, ill_n):
            terms_copy(d, step).wait_recv()
        for h in range(liq_n):
            start = pl.multiple_of(((d * ill_n + ill_me) * liq_n + h) * plane_rows, TILE)
            total = terms[pl.ds(start, plane_rows), :]
            for step in range(1, ill_n):
                total = total + terms_in[d * (ill_n - 1) + step - 1, pl.ds(h * plane_rows, plane_rows), :]
            owner_sum[d * liq_n + h] = total
        for step in far_first:
            owner_copy(d, step).start()

    def collect(d):
        for step in far_first:
            owner_copy(d, step).wait_recv()
        total = owner_sum[d * liq_n + liq_me]
        for step in range(1, liq_n):
            total = total + owner_in[d * (liq_n - 1) + step - 1]
        settled[pl.ds(d * plane_rows, plane_rows), :] = total
        return total

    def second_policy():
        if relayed:
            for half in range(2):
                pencil_relay(half).wait_recv()
        else:
            for half, step in early:
                pencil_copy(1, half, step).wait_recv()
        for half, step in late:
            pencil_copy(1, half, step).wait_recv()
        for tile in range(tiles):
            consumption_ref[pl.ds(tile * TILE, TILE), :] = interpolate(1, tile)

    first_policy(0)
    scatter(0, 0)
    first_policy(1)
    value_copy(1, value_two).start()
    scatter(0, 1)
    send_terms(0)
    value_copy(1, value_two).wait_recv()
    drifted = dot(second_mat[...], value_two[...]) + dot(second_up[...], near_value[1])
    pencil[liq_n + liq_me] = lax.rsqrt(drifted)
    for half, step in early:
        pencil_copy(1, half, step).start()
    for d in range(1, durables):
        scatter(d, 0)
        if d == 1:
            send_owners(0)
            for half, step in late:
                pencil_copy(1, half, step).start()
        scatter(d, 1)
        send_terms(d)
    for d in range(1, durables):
        send_owners(d)
    if relayed:
        for half, step in early:
            pencil_copy(1, half, step).wait_recv()
        for half in range(2):
            pencil_relay(half).start()

    depart_copy = pltpu.make_async_remote_copy(
        src_ref=depart, dst_ref=depart_in, send_sem=depart_send.at[0], recv_sem=depart_recv.at[0],
        device_id={"dur": jnp.maximum(dur_me - 1, 0)}, device_id_type=MESH_ID,
    )

    depart[...] = (1.0 - stay[0]) * collect(0)

    @pl.when(dur_me > 0)
    def _():
        depart_copy.start()

    for d in range(1, durables):
        collect(d)
    next_ref[...] = dot(next_mat[...], settled[...])
    second_policy()

    @pl.when(dur_me < dur_n - 1)
    def _():
        depart_copy.wait_recv()
        next_ref[...] += dot(next_in[...], depart_in[...])

    value_copy(0, value_ref).wait_send()
    value_copy(1, value_two).wait_send()
    for step in range(1, liq_n):
        for half in range(2):
            pencil_copy(0, half, step).wait_send()
        for d in range(durables):
            owner_copy(d, step).wait_send()
    for half, step in early + late:
        pencil_copy(1, half, step).wait_send()
    if relayed:
        for half in range(2):
            pencil_relay(half).wait_send()
    for step in range(1, ill_n):
        for d in range(durables):
            terms_copy(d, step).wait_send()

    @pl.when(dur_me > 0)
    def _():
        depart_copy.wait_send()


def halves_of(x):
    high = x.astype(jnp.bfloat16)
    return high, (x - high.astype(jnp.float32)).astype(jnp.bfloat16)


def stack_data(x):
    high, low = halves_of(x)
    return jnp.concatenate([high, low, high], axis=0)


def transposed_kernel(
    dims,
    value_hbm, transition_hbm, shock_hbm, drift_hbm, keep_hbm, index_hbm, weight_hbm,
    steady_hbm, lottery_hbm, target_hbm, ill_target_hbm, population_hbm,
    consumption_ref, next_ref,
    value_ref, transition_ref, shock_ref, index_ref, weight_ref, steady_ref, lottery_ref, target_ref,
    population_ref, ill_target_ref, drift_ref, keep_ref, load_sem,
    near_out, near_in, late_out, late_in, side_out, side_in, pair_in,
    pencil_one, value_two, values_in, pencil_two, found_out, found_in, hots, placed, mass_out, depart_out, mass_in,
    near_send, near_recv, late_send, late_recv, goal_recv, side_send, side_recv, pair_send, pair_recv,
    value_send, value_recv, found_send, found_recv, mass_send, mass_recv, depart_send, depart_recv, ready_sem,
):
    incomes, durables, ill_rows, liq_rows, liq_n, ill_n, dur_n = dims
    group = durables * ill_rows
    ill_all = ill_n * ill_rows
    part = incomes // liq_n
    per_dest = 3 * ill_rows
    constant = jnp.float32(DISCOUNT * GROSS_RATE)
    f32 = jnp.float32
    liq_me, ill_me, dur_me = (lax.axis_index(name) for name in ("liq", "ill", "dur"))
    far_first = range(liq_n - 1, 0, -1)
    peers = [(step, flip) for step in range(liq_n - 1, -1, -1) for flip in range(ill_n) if step or flip]

    def at(step, flip):
        return {"liq": peer_of(liq_me, step, liq_n), "ill": peer_of(ill_me, flip, ill_n)}

    barrier = pltpu.get_barrier_semaphore()
    for step, flip in peers:
        pl.semaphore_signal(barrier, inc=1, device_id=at(step, flip), device_id_type=MESH_ID)

    @pl.when(dur_me > 0)
    def _():
        pl.semaphore_signal(barrier, inc=1, device_id={"dur": dur_me - 1}, device_id_type=MESH_ID)

    @pl.when(dur_me < dur_n - 1)
    def _():
        pl.semaphore_signal(barrier, inc=1, device_id={"dur": dur_me + 1}, device_id_type=MESH_ID)

    loads = [
        pltpu.make_async_copy(source, held, load_sem.at[slot])
        for slot, source, held in (
            (0, transition_hbm, transition_ref), (1, shock_hbm, shock_ref), (2, value_hbm, value_ref),
            (3, index_hbm, index_ref), (3, weight_hbm, weight_ref), (4, drift_hbm, drift_ref),
            (5, ill_target_hbm, ill_target_ref), (6, target_hbm, target_ref), (6, lottery_hbm, lottery_ref),
            (6, steady_hbm, steady_ref), (6, population_hbm, population_ref), (7, keep_hbm, keep_ref),
        )
    ]
    for load in loads:
        load.start()

    def load_all(slot, count):
        span = pl.ds(0, count * group)
        pltpu.make_async_copy(values_in.at[span], values_in.at[span], load_sem.at[slot]).wait()

    def rows_at(d, a, z_part):
        return pl.ds(z_part * part * group + d * ill_rows + a, part, stride=group)

    def whole_rows(d, a):
        return pl.ds(d * ill_rows + a, incomes, stride=group)

    kinds = [(d, a) for d in range(durables) for a in range(ill_rows)]
    for load in loads[:2]:
        load.wait()
    transition = transition_ref[...]
    eye = iota((incomes, incomes), 0) == iota((incomes, incomes), 1)
    scaled = dot(jnp.where(eye, constant * shock_ref[...], 0.0), transition)

    def stack_left(x):
        high, low = halves_of(x)
        return jnp.concatenate([high, high, low], axis=1)

    def times(left, x):
        return jnp.dot(left, stack_data(x), preferred_element_type=f32)

    left_one = stack_left(scaled)
    left_two = stack_left(constant * transition)
    loads[2].wait()
    wide = jnp.concatenate([value_ref[whole_rows(d, a), :] for d, a in kinds], axis=1)
    wide = times(left_one, wide)
    load_all(3, 2)
    for k, (d, a) in enumerate(kinds):
        for q in range(liq_n):
            near_out[d * liq_n + q, a] = wide[q * part : (q + 1) * part, k * liq_rows : (k + 1) * liq_rows]
            near_out[d * liq_n + q, ill_rows + a] = index_ref[rows_at(d, a, q), :].astype(f32)
            near_out[d * liq_n + q, 2 * ill_rows + a] = weight_ref[rows_at(d, a, q), :]

    for load in loads[5:7]:
        load.wait()
    column = iota((part, incomes), 1)
    wanted = column == liq_me * part + iota((part, incomes), 0)
    picked = jnp.concatenate(
        [
            jnp.where(wanted, jnp.broadcast_to(ill_target_ref[k : k + 1, :], (part, incomes)), 0)
            for k in range(group)
        ],
        axis=0,
    )
    spread = jnp.dot(
        picked.astype(f32).astype(jnp.bfloat16), jnp.ones((incomes, liq_rows), jnp.bfloat16), preferred_element_type=f32
    )
    row = iota((TILE, liq_rows), 0)
    drifts = jnp.zeros((TILE, liq_rows), f32)
    for a in range(ill_rows):
        drifts = jnp.where(row == a, drift_ref[a], drifts)
    for k, (d, a) in enumerate(kinds):
        side_out[d, a] = spread[k * part : (k + 1) * part]
    for d in range(durables):
        side_out[d, ill_rows] = drifts

    with scope("bar"):
        dur_peers = jnp.minimum(dur_me, 1) + jnp.minimum(dur_n - 1 - dur_me, 1)
        pl.semaphore_wait(barrier, len(peers) + dur_peers)

    @pl.when((dur_me < dur_n - 1) & (ill_me == 0))
    def _():
        pl.semaphore_signal(ready_sem, inc=1, device_id={"dur": dur_me + 1}, device_id_type=MESH_ID)

    def bundle_copy(out_ref, in_ref, send, recv, first, count, step, i):
        liq_there, kept = peer_of(liq_me, step, liq_n), pl.ds(first, count)
        return pltpu.make_async_remote_copy(
            src_ref=out_ref.at[i * liq_n + liq_there, kept], dst_ref=in_ref.at[liq_me * ill_n + ill_me, kept],
            send_sem=send.at[0], recv_sem=recv.at[0], device_id={"liq": liq_there, "ill": i}, device_id_type=MESH_ID,
        )

    def bundle_all(out_ref, in_ref, send, recv, first, count):
        span, kept = pl.ds(0, len(peers)), pl.ds(first, count)
        return pltpu.make_async_remote_copy(
            src_ref=out_ref.at[span, kept], dst_ref=in_ref.at[span, kept], send_sem=send.at[0], recv_sem=recv.at[0],
            device_id=at(0, 1), device_id_type=MESH_ID,
        )

    def near_all():
        return bundle_all(near_out, near_in, near_send, near_recv, 0, per_dest)

    def late_all():
        return bundle_all(late_out, late_in, late_send, late_recv, 0, 2 * ill_rows)

    def goal_all():
        return bundle_all(late_out, late_in, late_send, goal_recv, 2 * ill_rows, ill_rows)

    def near_copy(step, i):
        return bundle_copy(near_out, near_in, near_send, near_recv, 0, per_dest, step, i)

    def late_copy(step, i):
        return bundle_copy(late_out, late_in, late_send, late_recv, 0, 2 * ill_rows, step, i)

    def goal_copy(step, i):
        return bundle_copy(late_out, late_in, late_send, goal_recv, 2 * ill_rows, ill_rows, step, i)

    def side_copy(flip):
        there = at(0, flip)
        return pltpu.make_async_remote_copy(
            src_ref=side_out.at[there["ill"]], dst_ref=side_in.at[ill_me],
            send_sem=side_send.at[flip - 1], recv_sem=side_recv.at[flip - 1], device_id=there, device_id_type=MESH_ID,
        )

    def pair_copy(flip):
        there = at(0, flip)
        return pltpu.make_async_remote_copy(
            src_ref=near_out.at[pl.ds(there["ill"] * liq_n, liq_n), pl.ds(ill_rows, 2 * ill_rows)],
            dst_ref=pair_in.at[ill_me], send_sem=pair_send.at[flip - 1], recv_sem=pair_recv.at[flip - 1],
            device_id=there, device_id_type=MESH_ID,
        )

    def start_far(i, make):
        make(liq_n - 1, i).start()

    def start_close(i, make):
        for step in range(liq_n - 2, 0, -1):
            make(step, i).start()

        @pl.when(ill_me != i)
        def _():
            make(0, i).start()

    for flip in range(1, ill_n):
        side_copy(flip).start()

    load_all(6, 4)
    loads[11].wait()
    for d, a in kinds:
        for q in range(liq_n):
            span = rows_at(d, a, q)
            late_out[d * liq_n + q, a] = lottery_ref[span, :] - SLOPE_GAIN * steady_ref[span, :]
            late_out[d * liq_n + q, ill_rows + a] = population_ref[span, :]
            late_out[d * liq_n + q, 2 * ill_rows + a] = target_ref[span, :].astype(f32)
    start_far(0, near_copy)
    start_far(0, goal_copy)
    start_close(0, near_copy)
    start_close(0, goal_copy)
    for i in range(1, ill_n):
        start_far(i, near_copy)
    start_far(0, late_copy)
    for i in range(1, ill_n):
        start_close(i, near_copy)
    start_close(0, late_copy)
    for i in range(1, ill_n):
        start_far(i, goal_copy)
        start_far(i, late_copy)
        start_close(i, goal_copy)
        start_close(i, late_copy)
    for flip in range(1, ill_n):
        pair_copy(flip).start()

    own_out = ill_me * liq_n + liq_me
    own_in = liq_me * ill_n + ill_me
    for k in range(per_dest):
        near_in[own_in, k] = near_out[own_out, k]
        late_in[own_in, k] = late_out[own_out, k]
    for k in range(ill_rows + 1):
        side_in[ill_me, k] = side_out[ill_me, k]
    for q in range(liq_n):
        for k in range(2 * ill_rows):
            pair_in[ill_me, q, k] = near_out[ill_me * liq_n + q, ill_rows + k]

    @pl.when(dur_me == dur_n - 1)
    def _():
        for a in range(ill_rows):
            mass_in[group + a] = jnp.zeros((incomes, liq_rows), f32)

    stay = [keep_ref[d] for d in range(durables)]
    first_d = as_float(dur_me == 0)
    stay[0] = first_d + (1.0 - first_d) * stay[0]

    def received(ref, kind, h, ag):
        return ref[h * ill_n + ag // ill_rows, kind * ill_rows + ag % ill_rows]

    def interpolate(blocks, index, weight):
        index = index.astype(jnp.int32)
        low_block, low_lane = split_by(index, liq_rows)
        high_block, high_lane = split_by(index + 1, liq_rows)
        low = high = None
        for h, block in enumerate(blocks):
            low_h = jnp.take_along_axis(block, low_lane, axis=1, mode="promise_in_bounds")
            high_h = jnp.take_along_axis(block, high_lane, axis=1, mode="promise_in_bounds")
            low = low_h if h == 0 else jnp.where(low_block == h, low_h, low)
            high = high_h if h == 0 else jnp.where(high_block == h, high_h, high)
        return weight * low + (1.0 - weight) * high

    own_z = pl.ds(pl.multiple_of(liq_me * part, TILE), part)

    def pieces_of(me):
        pair = (me + 1) % ill_n
        first = (pair * ill_rows, min(ill_rows + 1, ill_all - pair * ill_rows))
        rest = [ag for ag in range(ill_all) if not first[0] <= ag < sum(first)]
        return [first, (rest[0], len(rest))]

    def value_copy(me, k, step):
        start, count = pieces_of(me)[k]
        span = pl.ds(start * liq_n, count * liq_n)
        return pltpu.make_async_remote_copy(
            src_ref=value_two.at[span], dst_ref=values_in.at[span, own_z], send_sem=value_send.at[0],
            recv_sem=value_recv.at[k], device_id={"liq": peer_of(liq_me, step, liq_n)}, device_id_type=MESH_ID,
        )

    def value_all(k, count):
        span = pl.ds(0, (liq_n - 1) * count)
        return pltpu.make_async_remote_copy(
            src_ref=values_in.at[span], dst_ref=values_in.at[span], send_sem=value_send.at[0],
            recv_sem=value_recv.at[k], device_id=at(1, 0), device_id_type=MESH_ID,
        )

    def on_each_core(part_of):
        for me in range(ill_n):

            @pl.when(ill_me == me)
            def _():
                part_of(me)

    with scope("near"):
        for flip in range(1, ill_n):
            side_copy(flip).wait_recv()
        near_all().wait_recv()

    with scope("policy"):
        for ag in range(ill_all):
            i, a = divmod(ag, ill_rows)
            own = jnp.broadcast_to(side_in[i, ill_rows, a : a + 1, :], (TILE, liq_rows))
            for h in range(liq_n):
                drifted = own * received(near_in, 0, h, ag) + (1.0 - own) * received(near_in, 0, h, min(ag + 1, ill_all - 1))
                pencil_one[ag * liq_n + h] = lax.rsqrt(drifted)

        def policy(me):
            pieces = pieces_of(me)

            def loaded(k):
                start, count = pieces[k]
                return [
                    (
                        ag,
                        [pencil_one[ag * liq_n + h] for h in range(liq_n)],
                        [(received(near_in, 1, h, ag), received(near_in, 2, h, ag)) for h in range(liq_n)],
                    )
                    for ag in range(start, start + count)
                ]

            ahead = loaded(0)
            for k in range(len(pieces)):
                for ag, blocks, states in ahead:
                    for h, (index, weight) in enumerate(states):
                        chosen = interpolate(blocks, index, weight)
                        found = GROSS_RATE / (chosen * chosen)
                        value_two[ag * liq_n + h] = found
                        values_in[ag * liq_n + h, own_z, :] = found
                        pencil_one[ill_all * liq_n + ag * liq_n + h] = chosen
                ahead = loaded(k + 1) if k + 1 < len(pieces) else []
                for step in far_first:
                    if k == 0 or step == liq_n - 1 or me > 0:
                        value_copy(me, k, step).start()

        on_each_core(policy)

    half = liq_rows // 2
    cuts = 2 * liq_n
    sub = iota((cuts, liq_rows), 0).astype(f32)
    lane_at = iota((TILE, liq_rows), 1)
    lane_row = iota((half, liq_rows), 0).astype(f32).astype(jnp.bfloat16)
    one = jnp.ones((half, liq_rows), jnp.bfloat16)
    nil = jnp.zeros((half, liq_rows), jnp.bfloat16)

    with scope("goal"):
        goal_all().wait_recv()
    with scope("hots"):
        cut_at = {}
        for ag in range(ill_all):
            places = []
            for h in range(liq_n):
                target = received(late_in, 2, h, ag)
                cut = jnp.zeros(target.shape, f32)
                for other in range(1, cuts):
                    cut = cut + jnp.where(target >= other * half, 1.0, 0.0)
                cut_at[ag, h] = cut
                places.append(target - half * cut)
            for s in range(part):
                for h in range(liq_n):
                    place = jnp.broadcast_to(places[h][s : s + 1, :], (2 * TILE, liq_rows)).astype(jnp.bfloat16)
                    place = jnp.concatenate([place] * (half // (2 * TILE)), axis=0)
                    hots[s * ill_all + ag, :, h * liq_rows : (h + 1) * liq_rows] = jnp.where(lane_row == place, one, nil)
    with scope("late"):
        late_all().wait_recv()
    with scope("scatter"):
        held = {}
        for ag in range(ill_all):
            for h in range(liq_n):
                chosen = pencil_one[ill_all * liq_n + ag * liq_n + h]
                share = jnp.clip(received(late_in, 0, h, ag) + SLOPE_GAIN * chosen, 0.0, 1.0)
                mass = received(late_in, 1, h, ag)
                held[ag, h] = (mass * share, mass * (1.0 - share), cut_at[ag, h])
        for s in range(part):
            totals, to_row = [], []
            for ag in range(ill_all):
                lefts = []
                for h in range(liq_n):
                    low_t, high_t, cut_t = (x[s : s + 1, :] for x in held[ag, h])
                    here = cut_t == sub
                    both = jnp.concatenate([jnp.where(here, low_t, 0.0), jnp.where(here, high_t, 0.0)], axis=0)
                    first = both.astype(jnp.bfloat16)
                    lefts.append(jnp.concatenate([first, (both - first.astype(f32)).astype(jnp.bfloat16)], axis=0))
                found = lax.dot_general(
                    jnp.concatenate(lefts, axis=1), hots[s * ill_all + ag], NT, preferred_element_type=f32
                )
                totals.append(found[: 2 * cuts] + found[2 * cuts :])
                to_row.append(jnp.broadcast_to(side_in[ag // ill_rows, ag % ill_rows, s : s + 1, :half], (2 * cuts, half)))
            for dest in range(ill_all):
                out = None
                for ag in range(ill_all):
                    here = jnp.where(to_row[ag] == dest, totals[ag], 0.0)
                    out = here if out is None else out + here
                placed[pl.ds(dest * 2 * cuts * part + s, 2 * cuts, stride=part), :half] = out

    with scope("massout"):
        def joined(dest, side, h):
            start = ((dest * 2 + side) * cuts + 2 * h) * part
            return jnp.concatenate(
                [placed[pl.ds(start, part), :half], placed[pl.ds(start + part, part), :half]], axis=1
            )

        for dest in range(ill_all):
            carried = None
            for h in range(liq_n):
                low = joined(dest, 0, h)
                moved = pltpu.roll(joined(dest, 1, h), 1, 1)
                total = low + jnp.where(lane_at > 0, moved, 0.0 if carried is None else carried)
                carried = moved
                mass_out[h * ill_all + dest] = total
                depart_out[h * ill_all + dest] = (1.0 - stay[0]) * total

    def mass_copy(step, flip):
        there = at(step, flip)
        return pltpu.make_async_remote_copy(
            src_ref=mass_out.at[pl.ds(there["liq"] * ill_all + there["ill"] * ill_rows, ill_rows)],
            dst_ref=mass_in.at[pl.ds(ill_me * ill_rows, ill_rows), own_z],
            send_sem=mass_send.at[0], recv_sem=mass_recv.at[0], device_id=there, device_id_type=MESH_ID,
        )

    def mass_all():
        span = pl.ds(0, len(peers) * ill_rows)
        return pltpu.make_async_remote_copy(
            src_ref=mass_out.at[span], dst_ref=mass_out.at[span], send_sem=mass_send.at[0],
            recv_sem=mass_recv.at[0], device_id=at(0, 1), device_id_type=MESH_ID,
        )

    def depart_all(count):
        span = pl.ds(0, count * ill_rows)
        return pltpu.make_async_remote_copy(
            src_ref=depart_out.at[span], dst_ref=depart_out.at[span], send_sem=depart_send.at[0],
            recv_sem=depart_recv.at[0], device_id=at(0, 1), device_id_type=MESH_ID,
        )

    def depart_copy(step, i):
        liq_there = peer_of(liq_me, step, liq_n)
        return pltpu.make_async_remote_copy(
            src_ref=depart_out.at[pl.ds(liq_there * ill_all + i * ill_rows, ill_rows)],
            dst_ref=mass_in.at[pl.ds(group, ill_rows), own_z],
            send_sem=depart_send.at[0], recv_sem=depart_recv.at[0],
            device_id={"dur": jnp.maximum(dur_me - 1, 0), "liq": liq_there, "ill": i}, device_id_type=MESH_ID,
        )

    departs = (dur_me > 0) & (ill_me == 0)

    @pl.when(departs)
    def _():
        pl.semaphore_wait(ready_sem, 1)
        for step in range(liq_n - 1, -1, -1):
            for i in range(ill_n):
                depart_copy(step, i).start()

    def send_rest(me):
        for step in range(liq_n - 2, 0, -1):
            value_copy(me, 1, step).start()

    pl.when(ill_me == 0)(functools.partial(send_rest, 0))

    for step, flip in peers:
        mass_copy(step, flip).start()
    for a in range(ill_rows):
        mass_in[ill_me * ill_rows + a, own_z, :] = mass_out[liq_me * ill_all + ill_me * ill_rows + a]

    def found_copy(flip):
        there = at(0, flip)
        return pltpu.make_async_remote_copy(
            src_ref=found_out.at[flip - 1], dst_ref=found_in.at[flip - 1],
            send_sem=found_send.at[flip - 1], recv_sem=found_recv.at[flip - 1], device_id=there, device_id_type=MESH_ID,
        )

    for flip in range(1, ill_n):
        side_copy(flip).wait_send()
        pair_copy(flip).wait_send()
        pair_copy(flip).wait_recv()
    near_all().wait_send()
    bundle_all(late_out, late_in, late_send, late_recv, 0, per_dest).wait_send()
    def expect(ag):
        wide = jnp.concatenate([values_in[ag * liq_n + h] for h in range(liq_n)], axis=1)
        return times(left_two, wide)

    def consume(i, expected, store_tile):
        for a in range(ill_rows):
            own = jnp.broadcast_to(side_in[i, ill_rows, a : a + 1, :], (incomes, liq_rows))
            own = jnp.concatenate([own] * liq_n, axis=1)
            found = lax.rsqrt(own * expected[a] + (1.0 - own) * expected[a + 1])
            for h in range(liq_n):
                pencil_two[a * liq_n + h] = found[:, h * liq_rows : (h + 1) * liq_rows]
        for a in range(ill_rows):
            for q in range(liq_n):
                blocks = [pencil_two[a * liq_n + h, pl.ds(q * part, part), :] for h in range(liq_n)]
                store_tile(a, q, interpolate(blocks, pair_in[i, q, a], pair_in[i, q, ill_rows + a]))

    def store_found(a, q, found):
        found_out[0, q * ill_rows + a] = found

    def store_own(a, q, found):
        consumption_ref[rows_at(ill_me, a, q), :] = found

    def second(me):
        pair, is_last = (me + 1) % ill_n, me == ill_n - 1
        with scope("values"):
            value_all(0, pieces_of(me)[0][1]).wait_recv()
        with scope("second_a"):
            expected = [expect(pair * ill_rows + a) for a in range(ill_rows)]
            lowest = expected[0]
            above = pair * ill_rows + ill_rows
            expected.append(expected[-1] if above == ill_all else expect(above))
            consume(pair, expected, store_found)
            found_copy(1).start()
        with scope("values_b"):
            value_all(1, pieces_of(me)[1][1]).wait_recv()
        with scope("second_b"):
            expected = [expect(me * ill_rows + a) for a in range(ill_rows)]
            expected.append(expected[-1] if is_last else lowest)
            consume(me, expected, store_own)

    on_each_core(second)

    with scope("sends"):
        value_all(0, ill_all).wait_send()
        mass_all().wait_send()

        @pl.when(departs)
        def _():
            depart_all(liq_n * ill_n).wait_send()

    with scope("found"):
        for flip in range(1, ill_n):
            found_copy(flip).wait_send()
            found_copy(flip).wait_recv()
            for q in range(liq_n):
                for a in range(ill_rows):
                    consumption_ref[rows_at(peer_of(ill_me, flip, ill_n), a, q), :] = found_in[flip - 1, q * ill_rows + a]

    with scope("mass"):
        mass_all().wait_recv()

        @pl.when(dur_me < dur_n - 1)
        def _():
            depart_all(liq_n).wait_recv()

    with scope("next"):
        settled = []
        for d, a in kinds:
            after = mass_in[(d + 1) * ill_rows + a]
            if d + 1 < durables:
                after = (1.0 - stay[d + 1]) * after
            settled.append(stay[d] * mass_in[d * ill_rows + a] + after)
        high, low = halves_of(transition)
        found = lax.dot_general(
            jnp.concatenate([high, high, low], axis=0), stack_data(jnp.concatenate(settled, axis=1)),
            (((0,), (0,)), ((), ())), preferred_element_type=f32,
        )
        for k, (d, a) in enumerate(kinds):
            for q in range(liq_n):
                next_ref[rows_at(d, a, q), :] = found[q * part : (q + 1) * part, k * liq_rows : (k + 1) * liq_rows]


def store(consumption_ref, next_ref, consumption_hbm, next_hbm, sem):
    copies = [
        pltpu.make_async_copy(consumption_ref, consumption_hbm, sem.at[0]),
        pltpu.make_async_copy(next_ref, next_hbm, sem.at[1]),
    ]
    for copy in copies:
        copy.start()
    for copy in copies:
        copy.wait()


def window_scratch(dims):
    incomes, durables, ill_rows, liq_rows, liq_n, ill_n, dur_n = dims
    f32 = jnp.float32
    rows, plane_rows = incomes * durables * ill_rows, incomes * ill_rows
    block = (rows, liq_rows)
    dma = pltpu.SemaphoreType.DMA
    return [
        pltpu.VMEM(block, f32),
        pltpu.VMEM((incomes, incomes), f32),
        pltpu.VMEM((1, incomes), f32),
        pltpu.VMEM(block, jnp.int32),
        pltpu.VMEM(block, f32),
        pltpu.VMEM(block, f32),
        pltpu.VMEM(block, f32),
        pltpu.VMEM(block, jnp.int32),
        pltpu.VMEM(block, f32),
        pltpu.SMEM((ill_rows,), f32),
        pltpu.SMEM((durables,), f32),
        pltpu.SMEM((durables * ill_rows, incomes), jnp.int32),
        dma((12,)),
        pltpu.VMEM((rows, rows), f32),
        pltpu.VMEM((rows, rows), f32),
        pltpu.VMEM((rows, rows), f32),
        pltpu.VMEM((rows, rows), f32),
        pltpu.VMEM((rows, rows), f32),
        pltpu.VMEM((rows, plane_rows), f32),
        pltpu.VMEM((2,) + block, f32),
        pltpu.VMEM(block, f32),
        pltpu.VMEM((2 * liq_n,) + block, f32),
        pltpu.VMEM(block, f32),
        pltpu.VMEM(block, f32),
        pltpu.VMEM(block, jnp.int32),
        pltpu.VMEM(block, f32),
        pltpu.VMEM((2 * ill_n * liq_n * plane_rows, liq_rows), f32),
        pltpu.VMEM((ill_n * liq_n * rows, liq_rows), f32),
        pltpu.VMEM((durables * (ill_n - 1), liq_n * plane_rows, liq_rows), f32),
        pltpu.VMEM((durables * liq_n, plane_rows, liq_rows), f32),
        pltpu.VMEM((durables * (liq_n - 1), plane_rows, liq_rows), f32),
        pltpu.VMEM(block, f32),
        pltpu.VMEM((plane_rows, liq_rows), f32),
        pltpu.VMEM((plane_rows, liq_rows), f32),
        dma((2,)),
        dma((2,)),
        dma((4 * liq_n,)),
        dma((4 * liq_n,)),
        dma((durables * (ill_n - 1),)),
        dma((durables * (ill_n - 1),)),
        dma((durables * (liq_n - 1),)),
        dma((durables * (liq_n - 1),)),
        dma((1,)),
        dma((1,)),
    ]


def transposed_scratch(dims):
    incomes, durables, ill_rows, liq_rows, liq_n, ill_n, dur_n = dims
    f32 = jnp.float32
    block = (incomes * durables * ill_rows, liq_rows)
    dma = pltpu.SemaphoreType.DMA
    part = incomes // liq_n
    ill_all = ill_n * ill_rows
    tiles = lambda n: pltpu.VMEM((n, part, liq_rows), f32)
    slabs = lambda n: pltpu.VMEM((n, incomes, liq_rows), f32)
    bundles = pltpu.VMEM((durables * liq_n, 3 * ill_rows, part, liq_rows), f32)
    return [
        pltpu.VMEM(block, f32),
        pltpu.VMEM((incomes, incomes), f32),
        pltpu.VMEM((1, incomes), f32),
        pltpu.VMEM(block, jnp.int32),
        pltpu.VMEM(block, f32),
        pltpu.VMEM(block, f32),
        pltpu.VMEM(block, f32),
        pltpu.VMEM(block, jnp.int32),
        pltpu.VMEM(block, f32),
        pltpu.VMEM((durables * ill_rows, incomes), jnp.int32),
        pltpu.SMEM((ill_rows,), f32),
        pltpu.SMEM((durables,), f32),
        dma((8,)),
        bundles,
        bundles,
        bundles,
        bundles,
        pltpu.VMEM((durables, ill_rows + 1, TILE, liq_rows), f32),
        pltpu.VMEM((ill_n, ill_rows + 1, TILE, liq_rows), f32),
        pltpu.VMEM((ill_n, liq_n, 2 * ill_rows, part, liq_rows), f32),
        tiles(2 * ill_all * liq_n),
        tiles(ill_all * liq_n),
        slabs(ill_all * liq_n),
        slabs(ill_rows * liq_n),
        pltpu.VMEM((ill_n - 1, liq_n * ill_rows, part, liq_rows), f32),
        pltpu.VMEM((ill_n - 1, liq_n * ill_rows, part, liq_rows), f32),
        pltpu.VMEM((part * ill_all, liq_rows // 2, liq_n * liq_rows), jnp.bfloat16),
        pltpu.VMEM((4 * liq_n * ill_all * part, liq_rows), f32),
        tiles(liq_n * ill_all),
        tiles(liq_n * ill_all),
        slabs((durables + 1) * ill_rows),
    ] + [
        dma((n,)) for n in (1, 1, 1, 1, 1, 1, 1, 1, 1, 1, 2, 1, 1, 1, 1, 1, 1)
    ] + [pltpu.SemaphoreType.REGULAR]


def body(
    marginal_value,
    transition,
    discount_shock,
    illiquid_drift,
    durable_keep,
    bracket_index,
    bracket_weight,
    steady_consumption,
    lottery_weight,
    liquid_target,
    illiquid_target,
    population,
):
    shape = marginal_value.shape
    incomes, durables, ill_rows, liq_rows = shape
    liq_n, ill_n, dur_n = (lax.axis_size(name) for name in ("liq", "ill", "dur"))
    rows = incomes * durables * ill_rows
    flat = lambda x: x.reshape(rows, liq_rows)
    anywhere = pl.BlockSpec(memory_space=pl.ANY)
    f32 = jnp.float32
    block = (rows, liq_rows)
    dma = pltpu.SemaphoreType.DMA
    vmem = pl.BlockSpec(memory_space=pltpu.VMEM)
    held = pltpu.VMEM(block, f32)
    result = jax.ShapeDtypeStruct(block, f32)
    dims = (incomes, durables, ill_rows, liq_rows, liq_n, ill_n, dur_n)
    transposed = (
        ill_n == 2 and durables == ill_n and liq_n * 2 == TILE and incomes == liq_n * TILE and ill_rows < TILE
    )
    if transposed:
        step_kernel, scratch, name = transposed_kernel, transposed_scratch(dims), "transposed_window"
    else:
        step_kernel, scratch, name = kernel, window_scratch(dims), "window"
    outs = pl.pallas_call(
        functools.partial(step_kernel, dims),
        out_shape=(held, held),
        in_specs=[anywhere] * 12,
        out_specs=(vmem, vmem),
        scratch_shapes=scratch,
        compiler_params=pltpu.CompilerParams(collective_id=0, has_side_effects=True),
        name=name,
    )(
        flat(marginal_value),
        transition,
        discount_shock.reshape(1, incomes),
        illiquid_drift,
        durable_keep,
        flat(bracket_index),
        flat(bracket_weight),
        flat(steady_consumption),
        flat(lottery_weight),
        flat(liquid_target),
        jnp.transpose(illiquid_target, (1, 2, 0)).reshape(durables * ill_rows, incomes),
        flat(population),
    )
    outs = pl.pallas_call(
        store,
        out_shape=(result, result),
        in_specs=[vmem, vmem],
        out_specs=(anywhere, anywhere),
        scratch_shapes=[dma((2,))],
        name="store",
    )(*(pltpu.with_memory_space_constraint(out, pltpu.VMEM) for out in outs))
    return tuple(out.reshape(shape) for out in outs)


def solution(mesh):
    in_specs = (
        P(None, "dur", "ill", "liq"),
        P(),
        P(),
        P("ill"),
        P("dur"),
        P(None, "dur", "ill", "liq"),
        P(None, "dur", "ill", "liq"),
        P(None, "dur", "ill", "liq"),
        P(None, "dur", "ill", "liq"),
        P(None, "dur", "ill", "liq"),
        P(None, "dur", "ill"),
        P(None, "dur", "ill", "liq"),
    )
    out_specs = (P(None, "dur", "ill", "liq"), P(None, "dur", "ill", "liq"))
    return jax.shard_map(body, mesh=mesh, in_specs=in_specs, out_specs=out_specs, check_vma=False)
```

```python
import contextlib
import functools

import jax
import jax.numpy as jnp
from jax import lax
from jax.experimental import pallas as pl
from jax.experimental.pallas import tpu as pltpu
from jax.sharding import PartitionSpec as P

DISCOUNT = 0.96
GROSS_RATE = 1.01
SLOPE_GAIN = 0.5
HIGHEST_PREC = lax.Precision.HIGHEST
MESH_ID = pl.DeviceIdType.MESH
NT = (((1,), (1,)), ((), ()))
TILE = 8


def scope(name):
    return contextlib.nullcontext()


def split_by(x, n):
    if n & (n - 1) == 0:
        return x >> (n.bit_length() - 1), x & (n - 1)
    return lax.div(x, jnp.int32(n)), lax.rem(x, jnp.int32(n))


def dot(a, b):
    return jnp.dot(a, b, precision=HIGHEST_PREC, preferred_element_type=jnp.float32)


def iota(shape, axis):
    return lax.broadcasted_iota(jnp.int32, shape, axis)


def as_float(flag):
    return jnp.where(flag, jnp.float32(1.0), jnp.float32(0.0))


def peer_of(me, step, n):
    if n & (n - 1):
        return lax.rem(me + step, n)
    out = me
    for bit in range(n.bit_length() - 1):
        if step >> bit & 1:
            out = out + (1 - 2 * lax.rem(lax.div(me, jnp.int32(1 << bit)), jnp.int32(2))) * (1 << bit)
    return out


def kernel(
    dims,
    value_hbm, transition_hbm, shock_hbm, drift_hbm, keep_hbm, index_hbm, weight_hbm,
    steady_hbm, lottery_hbm, target_hbm, ill_target_hbm, population_hbm,
    consumption_ref, next_ref,
    value_ref, transition_ref, shock_ref, index_ref, weight_ref, steady_ref, lottery_ref, target_ref,
    population_ref, drift_ref, keep_ref, ill_target_ref, load_sem,
    first_mat, first_up, second_mat, second_up, next_mat, next_in,
    near_value, value_two, pencil, mass_low, mass_high, target_hi, target_lo,
    placed_rows, terms, terms_in, owner_sum, owner_in, settled, depart, depart_in,
    value_send, value_recv, pencil_send, pencil_recv, terms_send, terms_recv,
    owner_send, owner_recv, depart_send, depart_recv,
):
    incomes, durables, ill_rows, liq_rows, liq_n, ill_n, dur_n = dims
    group = durables * ill_rows
    rows = incomes * group
    half_rows = rows // 2
    plane_rows = incomes * ill_rows
    liq_me, ill_me, dur_me = (lax.axis_index(name) for name in ("liq", "ill", "dur"))
    far_first = range(liq_n - 1, 0, -1)

    barrier = pltpu.get_barrier_semaphore()
    for step in far_first:
        pl.semaphore_signal(barrier, inc=1, device_id={"liq": peer_of(liq_me, step, liq_n)}, device_id_type=MESH_ID)
    for step in range(1, ill_n):
        pl.semaphore_signal(barrier, inc=1, device_id={"ill": peer_of(ill_me, step, ill_n)}, device_id_type=MESH_ID)

    @pl.when(dur_me > 0)
    def _():
        pl.semaphore_signal(barrier, inc=1, device_id={"dur": dur_me - 1}, device_id_type=MESH_ID)

    @pl.when(dur_me < dur_n - 1)
    def _():
        pl.semaphore_signal(barrier, inc=1, device_id={"dur": dur_me + 1}, device_id_type=MESH_ID)

    loads = [
        pltpu.make_async_copy(source, held, load_sem.at[slot])
        for slot, (source, held) in enumerate((
            (transition_hbm, transition_ref), (shock_hbm, shock_ref), (drift_hbm, drift_ref), (value_hbm, value_ref),
            (keep_hbm, keep_ref), (ill_target_hbm, ill_target_ref),
            (index_hbm, index_ref), (weight_hbm, weight_ref), (target_hbm, target_ref),
            (lottery_hbm, lottery_ref), (steady_hbm, steady_ref), (population_hbm, population_ref),
        ))
    ]
    for load in loads:
        load.start()
    for load in loads[:3]:
        load.wait()

    transition = transition_ref[...]
    row_z, row_rest = split_by(iota((rows, rows), 0), group)
    col_z, col_rest = split_by(iota((rows, rows), 1), group)
    row_d, row_a = split_by(row_rest, ill_rows)
    col_d, col_a = split_by(col_rest, ill_rows)
    spread = as_float(split_by(iota((rows, incomes), 0), group)[0] == iota((rows, incomes), 1))
    spread_t = as_float(iota((incomes, rows), 0) == split_by(iota((incomes, rows), 1), group)[0])
    drift = jnp.zeros((rows, rows), jnp.float32)
    for a in range(ill_rows):
        drift = jnp.where(row_a == a, drift_ref[a], drift)
    is_last = as_float(ill_me == ill_n - 1)
    same_d = row_d == col_d
    top_row = row_a == ill_rows - 1
    local = jnp.where(col_a == row_a, drift, 0.0)
    local = local + jnp.where(col_a == row_a + 1, 1.0 - drift, 0.0)
    local = local + jnp.where(top_row & (col_a == ill_rows - 1), is_last * (1.0 - drift), 0.0)
    local = jnp.where(same_d, local, 0.0)
    upper = jnp.where(same_d & top_row & (col_a == 0), (1.0 - is_last) * (1.0 - drift), 0.0)
    constant = jnp.float32(DISCOUNT * GROSS_RATE)
    eye = iota((incomes, incomes), 0) == iota((incomes, incomes), 1)
    scaled = dot(jnp.where(eye, constant * shock_ref[...], 0.0), transition)
    wide = dot(dot(spread, scaled), spread_t)
    first_mat[...] = wide * local
    first_up[...] = wide * upper

    dur_peers = jnp.minimum(dur_me, 1) + jnp.minimum(dur_n - 1 - dur_me, 1)
    pl.semaphore_wait(barrier, liq_n - 1 + ill_n - 1 + dur_peers)

    ill_below = lax.rem(ill_me + ill_n - 1, ill_n)

    def value_copy(k, source):
        return pltpu.make_async_remote_copy(
            src_ref=source, dst_ref=near_value.at[k], send_sem=value_send.at[k],
            recv_sem=value_recv.at[k], device_id={"ill": ill_below}, device_id_type=MESH_ID,
        )

    def pencil_copy(k, half, step):
        slot = (k * 2 + half) * liq_n + step
        part = pencil.at[k * liq_n + liq_me, pl.ds(half * half_rows, half_rows)]
        return pltpu.make_async_remote_copy(
            src_ref=part, dst_ref=part, send_sem=pencil_send.at[slot], recv_sem=pencil_recv.at[slot],
            device_id={"liq": peer_of(liq_me, step, liq_n)}, device_id_type=MESH_ID,
        )

    def pencil_relay(half):
        near, far = (1, 2) if half == 0 else (2, 1)
        slot = (2 + half) * liq_n
        part = pencil.at[liq_n + peer_of(liq_me, near, liq_n), pl.ds(half * half_rows, half_rows)]
        return pltpu.make_async_remote_copy(
            src_ref=part, dst_ref=part, send_sem=pencil_send.at[slot], recv_sem=pencil_recv.at[slot],
            device_id={"liq": peer_of(liq_me, far, liq_n)}, device_id_type=MESH_ID,
        )

    relayed = liq_n == 4
    if relayed:
        early, late = [(0, 1), (1, 2)], [(1, 1), (0, 2)]
    else:
        early, late = [(0, step) for step in far_first], [(1, step) for step in far_first]

    def terms_copy(d, step):
        peer = peer_of(ill_me, step, ill_n)
        slot = d * (ill_n - 1) + step - 1
        return pltpu.make_async_remote_copy(
            src_ref=terms.at[pl.ds((d * ill_n + peer) * (liq_n * plane_rows), liq_n * plane_rows)],
            dst_ref=terms_in.at[slot], send_sem=terms_send.at[slot], recv_sem=terms_recv.at[slot],
            device_id={"ill": peer}, device_id_type=MESH_ID,
        )

    def owner_copy(d, step):
        peer = peer_of(liq_me, step, liq_n)
        slot = d * (liq_n - 1) + step - 1
        return pltpu.make_async_remote_copy(
            src_ref=owner_sum.at[d * liq_n + peer], dst_ref=owner_in.at[slot],
            send_sem=owner_send.at[slot], recv_sem=owner_recv.at[slot],
            device_id={"liq": peer}, device_id_type=MESH_ID,
        )

    loads[3].wait()
    value_copy(0, value_ref).start()
    drifted = dot(first_mat[...], value_ref[...])
    value_copy(0, value_ref).wait_recv()
    drifted = drifted + dot(first_up[...], near_value[0])
    pencil[liq_me] = lax.rsqrt(drifted)
    for half in range(2):
        for step in far_first:
            pencil_copy(0, half, step).start()

    wide = constant * dot(dot(spread, transition), spread_t)
    second_mat[...] = wide * local
    second_up[...] = wide * upper

    for load in loads[4:]:
        load.wait()

    first_d = as_float(dur_me == 0)
    stay = [keep_ref[d] for d in range(durables)]
    stay[0] = first_d + (1.0 - first_d) * stay[0]
    back_d, back_rest = split_by(iota((rows, rows), 1), plane_rows)
    back_a = split_by(back_rest, ill_rows)[1]
    stays = jnp.zeros((rows, rows), jnp.float32)
    for d in range(durables):
        stays = jnp.where(back_d == d, stay[d], stays)
    mix = jnp.where(back_d == row_d, stays, 0.0) + jnp.where(back_d == row_d + 1, 1.0 - stays, 0.0)
    mix = jnp.where(back_a == row_a, mix, 0.0)
    back_z = split_by(split_by(iota((incomes, rows), 1), plane_rows)[1], ill_rows)[0]
    turned = lax.dot_general(spread, transition, NT, precision=HIGHEST_PREC, preferred_element_type=jnp.float32)
    wide = dot(turned, as_float(iota((incomes, rows), 0) == back_z))
    next_mat[...] = wide * mix
    in_z, in_a = split_by(iota((incomes, plane_rows), 1), ill_rows)
    wide = dot(turned, as_float(iota((incomes, plane_rows), 0) == in_z))
    in_row = split_by(iota((rows, plane_rows), 0), group)[1]
    in_row_d, in_row_a = split_by(in_row, ill_rows)
    in_col_a = split_by(iota((rows, plane_rows), 1), ill_rows)[1]
    next_in[...] = jnp.where((in_row_d == durables - 1) & (in_row_a == in_col_a), wide, 0.0)

    def block_of(position):
        block = jnp.zeros(position.shape, jnp.int32)
        for h in range(1, liq_n):
            block = block + jnp.where(position >= h * liq_rows, 1, 0)
        return block, position - block * liq_rows

    target_hi[...], lo = block_of(target_ref[...])
    target_lo[...] = lo.astype(jnp.float32)

    def interpolate(k, tile):
        span = pl.ds(tile * TILE, TILE)
        index = index_ref[span, :]
        low_block, low_lane = block_of(index)
        high_block, high_lane = block_of(index + 1)
        low = high = None
        for h in range(liq_n):
            block = pencil[k * liq_n + h, span, :]
            low_h = jnp.take_along_axis(block, low_lane, axis=1, mode="promise_in_bounds")
            high_h = jnp.take_along_axis(block, high_lane, axis=1, mode="promise_in_bounds")
            low = low_h if h == 0 else jnp.where(low_block == h, low_h, low)
            high = high_h if h == 0 else jnp.where(high_block == h, high_h, high)
        weight = weight_ref[span, :]
        return weight * low + (1.0 - weight) * high

    tiles = rows // TILE
    halves = (range(tiles // 2), range(tiles // 2, tiles))

    def first_policy(half):
        for step in far_first:
            pencil_copy(0, half, step).wait_recv()
        for tile in halves[half]:
            span = pl.ds(tile * TILE, TILE)
            chosen = interpolate(0, tile)
            value_two[span, :] = GROSS_RATE / (chosen * chosen)
            share = jnp.clip(lottery_ref[span, :] + SLOPE_GAIN * (chosen - steady_ref[span, :]), 0.0, 1.0)
            mass = population_ref[span, :]
            mass_low[span, :] = mass * share
            mass_high[span, :] = mass * (1.0 - share)

    lanes = 2 * liq_n
    sub = iota((lanes, liq_rows), 0)
    lane_at = iota((TILE, liq_rows), 1)
    sub_block = jnp.where(sub < liq_n, sub, sub - liq_n)
    lane_row = iota((liq_rows, liq_rows), 0).astype(jnp.float32).astype(jnp.bfloat16)
    one = jnp.ones((liq_rows, liq_rows), jnp.bfloat16)
    nil = jnp.zeros((liq_rows, liq_rows), jnp.bfloat16)
    per_tile = TILE // group

    def scatter_tile(d, tile):
        span = pl.ds(pl.multiple_of(tile * TILE, TILE), TILE)
        low_t, high_t, hi_t, lo_t = mass_low[span, :], mass_high[span, :], target_hi[span, :], target_lo[span, :]
        for zz in range(per_tile):
            z = tile * per_tile + zz
            totals = []
            for a in range(ill_rows):
                k = zz * group + d * ill_rows + a
                both = jnp.where(sub < liq_n, low_t[k : k + 1, :], high_t[k : k + 1, :])
                both = jnp.where(hi_t[k : k + 1, :] == sub_block, both, 0.0)
                rounded = both.astype(jnp.bfloat16).astype(jnp.float32)
                parts = jnp.concatenate([both, both - rounded], axis=0).astype(jnp.bfloat16)
                place = jnp.broadcast_to(lo_t[k : k + 1, :], (2 * TILE, liq_rows)).astype(jnp.bfloat16)
                place = jnp.concatenate([place] * (liq_rows // (2 * TILE)), axis=0)
                hot = jnp.where(lane_row == place, one, nil)
                placed = lax.dot_general(parts, hot, NT, preferred_element_type=jnp.float32)
                placed = placed[:lanes] + placed[lanes:]
                totals.append(placed)
            for dest in range(ill_n * ill_rows):
                out = None
                for a in range(ill_rows):
                    here = as_float(ill_target_ref[d * ill_rows + a, z] == dest) * totals[a]
                    out = here if out is None else out + here
                base = dest // ill_rows * lanes * plane_rows + z * ill_rows + dest % ill_rows
                placed_rows[pl.ds(base, lanes, stride=plane_rows), :] = out

    unroll = tiles // 2

    def scatter(d, half):
        def step(pair, carry):
            for turn in range(unroll):
                scatter_tile(d, halves[half].start + unroll * pair + turn)
            return carry

        lax.fori_loop(0, tiles // 2 // unroll, step, 0)

    def send_terms(d):
        for owner in range(ill_n):
            for piece in range(plane_rows // TILE):
                carried = None
                for h in range(liq_n):
                    low_at = (owner * lanes + h) * plane_rows + piece * TILE
                    low = placed_rows[pl.ds(low_at, TILE), :]
                    moved = pltpu.roll(placed_rows[pl.ds(low_at + liq_n * plane_rows, TILE), :], 1, 1)
                    edge = jnp.where(lane_at > 0, moved, 0.0 if carried is None else carried)
                    carried = moved
                    out_at = ((d * ill_n + owner) * liq_n + h) * plane_rows + piece * TILE
                    terms[pl.ds(out_at, TILE), :] = low + edge
        for step in range(1, ill_n):
            terms_copy(d, step).start()

    def send_owners(d):
        for step in range(1, ill_n):
            terms_copy(d, step).wait_recv()
        for h in range(liq_n):
            start = pl.multiple_of(((d * ill_n + ill_me) * liq_n + h) * plane_rows, TILE)
            total = terms[pl.ds(start, plane_rows), :]
            for step in range(1, ill_n):
                total = total + terms_in[d * (ill_n - 1) + step - 1, pl.ds(h * plane_rows, plane_rows), :]
            owner_sum[d * liq_n + h] = total
        for step in far_first:
            owner_copy(d, step).start()

    def collect(d):
        for step in far_first:
            owner_copy(d, step).wait_recv()
        total = owner_sum[d * liq_n + liq_me]
        for step in range(1, liq_n):
            total = total + owner_in[d * (liq_n - 1) + step - 1]
        settled[pl.ds(d * plane_rows, plane_rows), :] = total
        return total

    def second_policy():
        if relayed:
            for half in range(2):
                pencil_relay(half).wait_recv()
        else:
            for half, step in early:
                pencil_copy(1, half, step).wait_recv()
        for half, step in late:
            pencil_copy(1, half, step).wait_recv()
        for tile in range(tiles):
            consumption_ref[pl.ds(tile * TILE, TILE), :] = interpolate(1, tile)

    first_policy(0)
    scatter(0, 0)
    first_policy(1)
    value_copy(1, value_two).start()
    scatter(0, 1)
    send_terms(0)
    value_copy(1, value_two).wait_recv()
    drifted = dot(second_mat[...], value_two[...]) + dot(second_up[...], near_value[1])
    pencil[liq_n + liq_me] = lax.rsqrt(drifted)
    for half, step in early:
        pencil_copy(1, half, step).start()
    for d in range(1, durables):
        scatter(d, 0)
        if d == 1:
            send_owners(0)
            for half, step in late:
                pencil_copy(1, half, step).start()
        scatter(d, 1)
        send_terms(d)
    for d in range(1, durables):
        send_owners(d)
    if relayed:
        for half, step in early:
            pencil_copy(1, half, step).wait_recv()
        for half in range(2):
            pencil_relay(half).start()

    depart_copy = pltpu.make_async_remote_copy(
        src_ref=depart, dst_ref=depart_in, send_sem=depart_send.at[0], recv_sem=depart_recv.at[0],
        device_id={"dur": jnp.maximum(dur_me - 1, 0)}, device_id_type=MESH_ID,
    )

    depart[...] = (1.0 - stay[0]) * collect(0)

    @pl.when(dur_me > 0)
    def _():
        depart_copy.start()

    for d in range(1, durables):
        collect(d)
    next_ref[...] = dot(next_mat[...], settled[...])
    second_policy()

    @pl.when(dur_me < dur_n - 1)
    def _():
        depart_copy.wait_recv()
        next_ref[...] += dot(next_in[...], depart_in[...])

    value_copy(0, value_ref).wait_send()
    value_copy(1, value_two).wait_send()
    for step in range(1, liq_n):
        for half in range(2):
            pencil_copy(0, half, step).wait_send()
        for d in range(durables):
            owner_copy(d, step).wait_send()
    for half, step in early + late:
        pencil_copy(1, half, step).wait_send()
    if relayed:
        for half in range(2):
            pencil_relay(half).wait_send()
    for step in range(1, ill_n):
        for d in range(durables):
            terms_copy(d, step).wait_send()

    @pl.when(dur_me > 0)
    def _():
        depart_copy.wait_send()


def halves_of(x):
    high = x.astype(jnp.bfloat16)
    return high, (x - high.astype(jnp.float32)).astype(jnp.bfloat16)


def stack_data(x):
    high, low = halves_of(x)
    return jnp.concatenate([high, low, high], axis=0)


def transposed_kernel(
    dims,
    value_hbm, transition_hbm, shock_hbm, drift_hbm, keep_hbm, index_hbm, weight_hbm,
    steady_hbm, lottery_hbm, target_hbm, ill_target_hbm, population_hbm,
    consumption_ref, next_ref,
    value_ref, transition_ref, shock_ref, index_ref, weight_ref, steady_ref, lottery_ref, target_ref,
    population_ref, ill_target_ref, drift_ref, keep_ref, load_sem,
    near_out, near_in, late_out, late_in, side_out, side_in, pair_in,
    pencil_one, value_two, values_in, pencil_two, found_out, found_in, hots, placed, mass_out, depart_out, mass_in,
    near_send, near_recv, late_send, late_recv, goal_recv, side_send, side_recv, pair_send, pair_recv,
    value_send, value_recv, found_send, found_recv, mass_send, mass_recv, depart_send, depart_recv, ready_sem,
):
    incomes, durables, ill_rows, liq_rows, liq_n, ill_n, dur_n = dims
    group = durables * ill_rows
    ill_all = ill_n * ill_rows
    part = incomes // liq_n
    per_dest = 3 * ill_rows
    constant = jnp.float32(DISCOUNT * GROSS_RATE)
    f32 = jnp.float32
    liq_me, ill_me, dur_me = (lax.axis_index(name) for name in ("liq", "ill", "dur"))
    far_first = range(liq_n - 1, 0, -1)
    peers = [(step, flip) for step in range(liq_n - 1, -1, -1) for flip in range(ill_n) if step or flip]

    def at(step, flip):
        return {"liq": peer_of(liq_me, step, liq_n), "ill": peer_of(ill_me, flip, ill_n)}

    barrier = pltpu.get_barrier_semaphore()
    for step, flip in peers:
        pl.semaphore_signal(barrier, inc=1, device_id=at(step, flip), device_id_type=MESH_ID)

    @pl.when(dur_me > 0)
    def _():
        pl.semaphore_signal(barrier, inc=1, device_id={"dur": dur_me - 1}, device_id_type=MESH_ID)

    @pl.when(dur_me < dur_n - 1)
    def _():
        pl.semaphore_signal(barrier, inc=1, device_id={"dur": dur_me + 1}, device_id_type=MESH_ID)

    loads = [
        pltpu.make_async_copy(source, held, load_sem.at[slot])
        for slot, source, held in (
            (0, transition_hbm, transition_ref), (1, shock_hbm, shock_ref), (2, value_hbm, value_ref),
            (3, index_hbm, index_ref), (3, weight_hbm, weight_ref), (4, drift_hbm, drift_ref),
            (5, ill_target_hbm, ill_target_ref), (6, target_hbm, target_ref), (6, lottery_hbm, lottery_ref),
            (6, steady_hbm, steady_ref), (6, population_hbm, population_ref), (7, keep_hbm, keep_ref),
        )
    ]
    for load in loads:
        load.start()

    def load_all(slot, count):
        span = pl.ds(0, count * group)
        pltpu.make_async_copy(values_in.at[span], values_in.at[span], load_sem.at[slot]).wait()

    def rows_at(d, a, z_part):
        return pl.ds(z_part * part * group + d * ill_rows + a, part, stride=group)

    def whole_rows(d, a):
        return pl.ds(d * ill_rows + a, incomes, stride=group)

    kinds = [(d, a) for d in range(durables) for a in range(ill_rows)]
    for load in loads[:2]:
        load.wait()
    transition = transition_ref[...]
    eye = iota((incomes, incomes), 0) == iota((incomes, incomes), 1)
    scaled = dot(jnp.where(eye, constant * shock_ref[...], 0.0), transition)

    def stack_left(x):
        high, low = halves_of(x)
        return jnp.concatenate([high, high, low], axis=1)

    def times(left, x):
        return jnp.dot(left, stack_data(x), preferred_element_type=f32)

    left_one = stack_left(scaled)
    left_two = stack_left(constant * transition)
    loads[2].wait()
    wide = jnp.concatenate([value_ref[whole_rows(d, a), :] for d, a in kinds], axis=1)
    wide = times(left_one, wide)
    load_all(3, 2)
    for k, (d, a) in enumerate(kinds):
        for q in range(liq_n):
            near_out[d * liq_n + q, a] = wide[q * part : (q + 1) * part, k * liq_rows : (k + 1) * liq_rows]
            near_out[d * liq_n + q, ill_rows + a] = index_ref[rows_at(d, a, q), :].astype(f32)
            near_out[d * liq_n + q, 2 * ill_rows + a] = weight_ref[rows_at(d, a, q), :]

    for load in loads[5:7]:
        load.wait()
    column = iota((part, incomes), 1)
    wanted = column == liq_me * part + iota((part, incomes), 0)
    picked = jnp.concatenate(
        [
            jnp.where(wanted, jnp.broadcast_to(ill_target_ref[k : k + 1, :], (part, incomes)), 0)
            for k in range(group)
        ],
        axis=0,
    )
    spread = jnp.dot(
        picked.astype(f32).astype(jnp.bfloat16), jnp.ones((incomes, liq_rows), jnp.bfloat16), preferred_element_type=f32
    )
    row = iota((TILE, liq_rows), 0)
    drifts = jnp.zeros((TILE, liq_rows), f32)
    for a in range(ill_rows):
        drifts = jnp.where(row == a, drift_ref[a], drifts)
    for k, (d, a) in enumerate(kinds):
        side_out[d, a] = spread[k * part : (k + 1) * part]
    for d in range(durables):
        side_out[d, ill_rows] = drifts

    load_all(6, 4)
    loads[11].wait()
    for d, a in kinds:
        for q in range(liq_n):
            span = rows_at(d, a, q)
            late_out[d * liq_n + q, a] = lottery_ref[span, :] - SLOPE_GAIN * steady_ref[span, :]
            late_out[d * liq_n + q, ill_rows + a] = population_ref[span, :]
            late_out[d * liq_n + q, 2 * ill_rows + a] = target_ref[span, :].astype(f32)
    with scope("bar"):
        dur_peers = jnp.minimum(dur_me, 1) + jnp.minimum(dur_n - 1 - dur_me, 1)
        pl.semaphore_wait(barrier, len(peers) + dur_peers)

    @pl.when((dur_me < dur_n - 1) & (ill_me == 0))
    def _():
        pl.semaphore_signal(ready_sem, inc=1, device_id={"dur": dur_me + 1}, device_id_type=MESH_ID)

    def bundle_copy(out_ref, in_ref, send, recv, first, count, step, i):
        liq_there, kept = peer_of(liq_me, step, liq_n), pl.ds(first, count)
        return pltpu.make_async_remote_copy(
            src_ref=out_ref.at[i * liq_n + liq_there, kept], dst_ref=in_ref.at[liq_me * ill_n + ill_me, kept],
            send_sem=send.at[0], recv_sem=recv.at[0], device_id={"liq": liq_there, "ill": i}, device_id_type=MESH_ID,
        )

    def bundle_all(out_ref, in_ref, send, recv, first, count):
        span, kept = pl.ds(0, len(peers)), pl.ds(first, count)
        return pltpu.make_async_remote_copy(
            src_ref=out_ref.at[span, kept], dst_ref=in_ref.at[span, kept], send_sem=send.at[0], recv_sem=recv.at[0],
            device_id=at(0, 1), device_id_type=MESH_ID,
        )

    def near_all():
        return bundle_all(near_out, near_in, near_send, near_recv, 0, per_dest)

    def late_all():
        return bundle_all(late_out, late_in, late_send, late_recv, 0, 2 * ill_rows)

    def goal_all():
        return bundle_all(late_out, late_in, late_send, goal_recv, 2 * ill_rows, ill_rows)

    def near_copy(step, i):
        return bundle_copy(near_out, near_in, near_send, near_recv, 0, per_dest, step, i)

    def late_copy(step, i):
        return bundle_copy(late_out, late_in, late_send, late_recv, 0, 2 * ill_rows, step, i)

    def goal_copy(step, i):
        return bundle_copy(late_out, late_in, late_send, goal_recv, 2 * ill_rows, ill_rows, step, i)

    def side_copy(flip):
        there = at(0, flip)
        return pltpu.make_async_remote_copy(
            src_ref=side_out.at[there["ill"]], dst_ref=side_in.at[ill_me],
            send_sem=side_send.at[flip - 1], recv_sem=side_recv.at[flip - 1], device_id=there, device_id_type=MESH_ID,
        )

    def pair_copy(flip):
        there = at(0, flip)
        return pltpu.make_async_remote_copy(
            src_ref=near_out.at[pl.ds(there["ill"] * liq_n, liq_n), pl.ds(ill_rows, 2 * ill_rows)],
            dst_ref=pair_in.at[ill_me], send_sem=pair_send.at[flip - 1], recv_sem=pair_recv.at[flip - 1],
            device_id=there, device_id_type=MESH_ID,
        )

    def start_far(i, make):
        make(liq_n - 1, i).start()

    def start_close(i, make):
        for step in range(liq_n - 2, 0, -1):
            make(step, i).start()

        @pl.when(ill_me != i)
        def _():
            make(0, i).start()

    for flip in range(1, ill_n):
        side_copy(flip).start()

    start_far(0, near_copy)
    start_far(0, goal_copy)
    start_close(0, near_copy)
    start_close(0, goal_copy)
    for i in range(1, ill_n):
        start_far(i, near_copy)
    start_far(0, late_copy)
    for i in range(1, ill_n):
        start_close(i, near_copy)
    start_close(0, late_copy)
    for i in range(1, ill_n):
        start_far(i, goal_copy)
        start_far(i, late_copy)
        start_close(i, goal_copy)
        start_close(i, late_copy)
    for flip in range(1, ill_n):
        pair_copy(flip).start()

    own_out = ill_me * liq_n + liq_me
    own_in = liq_me * ill_n + ill_me
    for k in range(per_dest):
        near_in[own_in, k] = near_out[own_out, k]
        late_in[own_in, k] = late_out[own_out, k]
    for k in range(ill_rows + 1):
        side_in[ill_me, k] = side_out[ill_me, k]
    for q in range(liq_n):
        for k in range(2 * ill_rows):
            pair_in[ill_me, q, k] = near_out[ill_me * liq_n + q, ill_rows + k]

    @pl.when(dur_me == dur_n - 1)
    def _():
        for a in range(ill_rows):
            mass_in[group + a] = jnp.zeros((incomes, liq_rows), f32)

    stay = [keep_ref[d] for d in range(durables)]
    first_d = as_float(dur_me == 0)
    stay[0] = first_d + (1.0 - first_d) * stay[0]

    def received(ref, kind, h, ag):
        return ref[h * ill_n + ag // ill_rows, kind * ill_rows + ag % ill_rows]

    def interpolate(blocks, index, weight):
        index = index.astype(jnp.int32)
        low_block, low_lane = split_by(index, liq_rows)
        high_block, high_lane = split_by(index + 1, liq_rows)
        low = high = None
        for h, block in enumerate(blocks):
            low_h = jnp.take_along_axis(block, low_lane, axis=1, mode="promise_in_bounds")
            high_h = jnp.take_along_axis(block, high_lane, axis=1, mode="promise_in_bounds")
            low = low_h if h == 0 else jnp.where(low_block == h, low_h, low)
            high = high_h if h == 0 else jnp.where(high_block == h, high_h, high)
        return weight * low + (1.0 - weight) * high

    own_z = pl.ds(pl.multiple_of(liq_me * part, TILE), part)

    def pieces_of(me):
        pair = (me + 1) % ill_n
        first = (pair * ill_rows, min(ill_rows + 1, ill_all - pair * ill_rows))
        rest = [ag for ag in range(ill_all) if not first[0] <= ag < sum(first)]
        return [first, (rest[0], len(rest))]

    def value_copy(me, k, step):
        start, count = pieces_of(me)[k]
        span = pl.ds(start * liq_n, count * liq_n)
        return pltpu.make_async_remote_copy(
            src_ref=value_two.at[span], dst_ref=values_in.at[span, own_z], send_sem=value_send.at[0],
            recv_sem=value_recv.at[k], device_id={"liq": peer_of(liq_me, step, liq_n)}, device_id_type=MESH_ID,
        )

    def value_all(k, count):
        span = pl.ds(0, (liq_n - 1) * count)
        return pltpu.make_async_remote_copy(
            src_ref=values_in.at[span], dst_ref=values_in.at[span], send_sem=value_send.at[0],
            recv_sem=value_recv.at[k], device_id=at(1, 0), device_id_type=MESH_ID,
        )

    def on_each_core(part_of):
        for me in range(ill_n):

            @pl.when(ill_me == me)
            def _():
                part_of(me)

    with scope("near"):
        for flip in range(1, ill_n):
            side_copy(flip).wait_recv()
        near_all().wait_recv()

    with scope("policy"):
        for ag in range(ill_all):
            i, a = divmod(ag, ill_rows)
            own = jnp.broadcast_to(side_in[i, ill_rows, a : a + 1, :], (TILE, liq_rows))
            for h in range(liq_n):
                drifted = own * received(near_in, 0, h, ag) + (1.0 - own) * received(near_in, 0, h, min(ag + 1, ill_all - 1))
                pencil_one[ag * liq_n + h] = lax.rsqrt(drifted)

        def policy(me):
            pieces = pieces_of(me)

            def loaded(k):
                start, count = pieces[k]
                return [
                    (
                        ag,
                        [pencil_one[ag * liq_n + h] for h in range(liq_n)],
                        [(received(near_in, 1, h, ag), received(near_in, 2, h, ag)) for h in range(liq_n)],
                    )
                    for ag in range(start, start + count)
                ]

            ahead = loaded(0)
            for k in range(len(pieces)):
                for ag, blocks, states in ahead:
                    for h, (index, weight) in enumerate(states):
                        chosen = interpolate(blocks, index, weight)
                        found = GROSS_RATE / (chosen * chosen)
                        value_two[ag * liq_n + h] = found
                        values_in[ag * liq_n + h, own_z, :] = found
                        pencil_one[ill_all * liq_n + ag * liq_n + h] = chosen
                ahead = loaded(k + 1) if k + 1 < len(pieces) else []
                for step in far_first:
                    if k == 0 or step == liq_n - 1 or me > 0:
                        value_copy(me, k, step).start()

        on_each_core(policy)

    half = liq_rows // 2
    cuts = 2 * liq_n
    sub = iota((cuts, liq_rows), 0).astype(f32)
    lane_at = iota((TILE, liq_rows), 1)
    lane_row = iota((half, liq_rows), 0).astype(f32).astype(jnp.bfloat16)
    one = jnp.ones((half, liq_rows), jnp.bfloat16)
    nil = jnp.zeros((half, liq_rows), jnp.bfloat16)

    with scope("goal"):
        goal_all().wait_recv()
    with scope("hots"):
        cut_at = {}
        for ag in range(ill_all):
            places = []
            for h in range(liq_n):
                target = received(late_in, 2, h, ag)
                cut = jnp.zeros(target.shape, f32)
                for other in range(1, cuts):
                    cut = cut + jnp.where(target >= other * half, 1.0, 0.0)
                cut_at[ag, h] = cut
                places.append(target - half * cut)
            for s in range(part):
                for h in range(liq_n):
                    place = jnp.broadcast_to(places[h][s : s + 1, :], (2 * TILE, liq_rows)).astype(jnp.bfloat16)
                    place = jnp.concatenate([place] * (half // (2 * TILE)), axis=0)
                    hots[s * ill_all + ag, :, h * liq_rows : (h + 1) * liq_rows] = jnp.where(lane_row == place, one, nil)
    with scope("late"):
        late_all().wait_recv()
    with scope("scatter"):
        held = {}
        for ag in range(ill_all):
            for h in range(liq_n):
                chosen = pencil_one[ill_all * liq_n + ag * liq_n + h]
                share = jnp.clip(received(late_in, 0, h, ag) + SLOPE_GAIN * chosen, 0.0, 1.0)
                mass = received(late_in, 1, h, ag)
                held[ag, h] = (mass * share, mass * (1.0 - share), cut_at[ag, h])
        for s in range(part):
            totals, to_row = [], []
            for ag in range(ill_all):
                lefts = []
                for h in range(liq_n):
                    low_t, high_t, cut_t = (x[s : s + 1, :] for x in held[ag, h])
                    here = cut_t == sub
                    both = jnp.concatenate([jnp.where(here, low_t, 0.0), jnp.where(here, high_t, 0.0)], axis=0)
                    first = both.astype(jnp.bfloat16)
                    lefts.append(jnp.concatenate([first, (both - first.astype(f32)).astype(jnp.bfloat16)], axis=0))
                found = lax.dot_general(
                    jnp.concatenate(lefts, axis=1), hots[s * ill_all + ag], NT, preferred_element_type=f32
                )
                totals.append(found[: 2 * cuts] + found[2 * cuts :])
                to_row.append(jnp.broadcast_to(side_in[ag // ill_rows, ag % ill_rows, s : s + 1, :half], (2 * cuts, half)))
            for dest in range(ill_all):
                out = None
                for ag in range(ill_all):
                    here = jnp.where(to_row[ag] == dest, totals[ag], 0.0)
                    out = here if out is None else out + here
                placed[pl.ds(dest * 2 * cuts * part + s, 2 * cuts, stride=part), :half] = out

    with scope("massout"):
        def joined(dest, side, h):
            start = ((dest * 2 + side) * cuts + 2 * h) * part
            return jnp.concatenate(
                [placed[pl.ds(start, part), :half], placed[pl.ds(start + part, part), :half]], axis=1
            )

        for dest in range(ill_all):
            carried = None
            for h in range(liq_n):
                low = joined(dest, 0, h)
                moved = pltpu.roll(joined(dest, 1, h), 1, 1)
                total = low + jnp.where(lane_at > 0, moved, 0.0 if carried is None else carried)
                carried = moved
                mass_out[h * ill_all + dest] = total
                depart_out[h * ill_all + dest] = (1.0 - stay[0]) * total

    def mass_copy(step, flip):
        there = at(step, flip)
        return pltpu.make_async_remote_copy(
            src_ref=mass_out.at[pl.ds(there["liq"] * ill_all + there["ill"] * ill_rows, ill_rows)],
            dst_ref=mass_in.at[pl.ds(ill_me * ill_rows, ill_rows), own_z],
            send_sem=mass_send.at[0], recv_sem=mass_recv.at[0], device_id=there, device_id_type=MESH_ID,
        )

    def mass_all():
        span = pl.ds(0, len(peers) * ill_rows)
        return pltpu.make_async_remote_copy(
            src_ref=mass_out.at[span], dst_ref=mass_out.at[span], send_sem=mass_send.at[0],
            recv_sem=mass_recv.at[0], device_id=at(0, 1), device_id_type=MESH_ID,
        )

    def depart_all(count):
        span = pl.ds(0, count * ill_rows)
        return pltpu.make_async_remote_copy(
            src_ref=depart_out.at[span], dst_ref=depart_out.at[span], send_sem=depart_send.at[0],
            recv_sem=depart_recv.at[0], device_id=at(0, 1), device_id_type=MESH_ID,
        )

    def depart_copy(step, i):
        liq_there = peer_of(liq_me, step, liq_n)
        return pltpu.make_async_remote_copy(
            src_ref=depart_out.at[pl.ds(liq_there * ill_all + i * ill_rows, ill_rows)],
            dst_ref=mass_in.at[pl.ds(group, ill_rows), own_z],
            send_sem=depart_send.at[0], recv_sem=depart_recv.at[0],
            device_id={"dur": jnp.maximum(dur_me - 1, 0), "liq": liq_there, "ill": i}, device_id_type=MESH_ID,
        )

    departs = (dur_me > 0) & (ill_me == 0)

    @pl.when(departs)
    def _():
        pl.semaphore_wait(ready_sem, 1)
        for step in range(liq_n - 1, -1, -1):
            for i in range(ill_n):
                depart_copy(step, i).start()

    def send_rest(me):
        for step in range(liq_n - 2, 0, -1):
            value_copy(me, 1, step).start()

    pl.when(ill_me == 0)(functools.partial(send_rest, 0))

    for step, flip in peers:
        mass_copy(step, flip).start()
    for a in range(ill_rows):
        mass_in[ill_me * ill_rows + a, own_z, :] = mass_out[liq_me * ill_all + ill_me * ill_rows + a]

    def found_copy(flip):
        there = at(0, flip)
        return pltpu.make_async_remote_copy(
            src_ref=found_out.at[flip - 1], dst_ref=found_in.at[flip - 1],
            send_sem=found_send.at[flip - 1], recv_sem=found_recv.at[flip - 1], device_id=there, device_id_type=MESH_ID,
        )

    for flip in range(1, ill_n):
        side_copy(flip).wait_send()
        pair_copy(flip).wait_send()
        pair_copy(flip).wait_recv()
    near_all().wait_send()
    bundle_all(late_out, late_in, late_send, late_recv, 0, per_dest).wait_send()
    def expect(ag):
        wide = jnp.concatenate([values_in[ag * liq_n + h] for h in range(liq_n)], axis=1)
        return times(left_two, wide)

    def consume(i, expected, store_tile):
        for a in range(ill_rows):
            own = jnp.broadcast_to(side_in[i, ill_rows, a : a + 1, :], (incomes, liq_rows))
            own = jnp.concatenate([own] * liq_n, axis=1)
            found = lax.rsqrt(own * expected[a] + (1.0 - own) * expected[a + 1])
            for h in range(liq_n):
                pencil_two[a * liq_n + h] = found[:, h * liq_rows : (h + 1) * liq_rows]
        for a in range(ill_rows):
            for q in range(liq_n):
                blocks = [pencil_two[a * liq_n + h, pl.ds(q * part, part), :] for h in range(liq_n)]
                store_tile(a, q, interpolate(blocks, pair_in[i, q, a], pair_in[i, q, ill_rows + a]))

    def store_found(a, q, found):
        found_out[0, q * ill_rows + a] = found

    def store_own(a, q, found):
        consumption_ref[rows_at(ill_me, a, q), :] = found

    def second(me):
        pair, is_last = (me + 1) % ill_n, me == ill_n - 1
        with scope("values"):
            value_all(0, pieces_of(me)[0][1]).wait_recv()
        with scope("second_a"):
            expected = [expect(pair * ill_rows + a) for a in range(ill_rows)]
            lowest = expected[0]
            above = pair * ill_rows + ill_rows
            expected.append(expected[-1] if above == ill_all else expect(above))
            consume(pair, expected, store_found)
            found_copy(1).start()
        with scope("values_b"):
            value_all(1, pieces_of(me)[1][1]).wait_recv()
        with scope("second_b"):
            expected = [expect(me * ill_rows + a) for a in range(ill_rows)]
            expected.append(expected[-1] if is_last else lowest)
            consume(me, expected, store_own)

    on_each_core(second)

    with scope("sends"):
        value_all(0, ill_all).wait_send()
        mass_all().wait_send()

        @pl.when(departs)
        def _():
            depart_all(liq_n * ill_n).wait_send()

    with scope("found"):
        for flip in range(1, ill_n):
            found_copy(flip).wait_send()
            found_copy(flip).wait_recv()
            for q in range(liq_n):
                for a in range(ill_rows):
                    consumption_ref[rows_at(peer_of(ill_me, flip, ill_n), a, q), :] = found_in[flip - 1, q * ill_rows + a]

    with scope("mass"):
        mass_all().wait_recv()

        @pl.when(dur_me < dur_n - 1)
        def _():
            depart_all(liq_n).wait_recv()

    with scope("next"):
        settled = []
        for d, a in kinds:
            after = mass_in[(d + 1) * ill_rows + a]
            if d + 1 < durables:
                after = (1.0 - stay[d + 1]) * after
            settled.append(stay[d] * mass_in[d * ill_rows + a] + after)
        high, low = halves_of(transition)
        found = lax.dot_general(
            jnp.concatenate([high, high, low], axis=0), stack_data(jnp.concatenate(settled, axis=1)),
            (((0,), (0,)), ((), ())), preferred_element_type=f32,
        )
        for k, (d, a) in enumerate(kinds):
            for q in range(liq_n):
                next_ref[rows_at(d, a, q), :] = found[q * part : (q + 1) * part, k * liq_rows : (k + 1) * liq_rows]


def store(consumption_ref, next_ref, consumption_hbm, next_hbm, sem):
    copies = [
        pltpu.make_async_copy(consumption_ref, consumption_hbm, sem.at[0]),
        pltpu.make_async_copy(next_ref, next_hbm, sem.at[1]),
    ]
    for copy in copies:
        copy.start()
    for copy in copies:
        copy.wait()


def window_scratch(dims):
    incomes, durables, ill_rows, liq_rows, liq_n, ill_n, dur_n = dims
    f32 = jnp.float32
    rows, plane_rows = incomes * durables * ill_rows, incomes * ill_rows
    block = (rows, liq_rows)
    dma = pltpu.SemaphoreType.DMA
    return [
        pltpu.VMEM(block, f32),
        pltpu.VMEM((incomes, incomes), f32),
        pltpu.VMEM((1, incomes), f32),
        pltpu.VMEM(block, jnp.int32),
        pltpu.VMEM(block, f32),
        pltpu.VMEM(block, f32),
        pltpu.VMEM(block, f32),
        pltpu.VMEM(block, jnp.int32),
        pltpu.VMEM(block, f32),
        pltpu.SMEM((ill_rows,), f32),
        pltpu.SMEM((durables,), f32),
        pltpu.SMEM((durables * ill_rows, incomes), jnp.int32),
        dma((12,)),
        pltpu.VMEM((rows, rows), f32),
        pltpu.VMEM((rows, rows), f32),
        pltpu.VMEM((rows, rows), f32),
        pltpu.VMEM((rows, rows), f32),
        pltpu.VMEM((rows, rows), f32),
        pltpu.VMEM((rows, plane_rows), f32),
        pltpu.VMEM((2,) + block, f32),
        pltpu.VMEM(block, f32),
        pltpu.VMEM((2 * liq_n,) + block, f32),
        pltpu.VMEM(block, f32),
        pltpu.VMEM(block, f32),
        pltpu.VMEM(block, jnp.int32),
        pltpu.VMEM(block, f32),
        pltpu.VMEM((2 * ill_n * liq_n * plane_rows, liq_rows), f32),
        pltpu.VMEM((ill_n * liq_n * rows, liq_rows), f32),
        pltpu.VMEM((durables * (ill_n - 1), liq_n * plane_rows, liq_rows), f32),
        pltpu.VMEM((durables * liq_n, plane_rows, liq_rows), f32),
        pltpu.VMEM((durables * (liq_n - 1), plane_rows, liq_rows), f32),
        pltpu.VMEM(block, f32),
        pltpu.VMEM((plane_rows, liq_rows), f32),
        pltpu.VMEM((plane_rows, liq_rows), f32),
        dma((2,)),
        dma((2,)),
        dma((4 * liq_n,)),
        dma((4 * liq_n,)),
        dma((durables * (ill_n - 1),)),
        dma((durables * (ill_n - 1),)),
        dma((durables * (liq_n - 1),)),
        dma((durables * (liq_n - 1),)),
        dma((1,)),
        dma((1,)),
    ]


def transposed_scratch(dims):
    incomes, durables, ill_rows, liq_rows, liq_n, ill_n, dur_n = dims
    f32 = jnp.float32
    block = (incomes * durables * ill_rows, liq_rows)
    dma = pltpu.SemaphoreType.DMA
    part = incomes // liq_n
    ill_all = ill_n * ill_rows
    tiles = lambda n: pltpu.VMEM((n, part, liq_rows), f32)
    slabs = lambda n: pltpu.VMEM((n, incomes, liq_rows), f32)
    bundles = pltpu.VMEM((durables * liq_n, 3 * ill_rows, part, liq_rows), f32)
    return [
        pltpu.VMEM(block, f32),
        pltpu.VMEM((incomes, incomes), f32),
        pltpu.VMEM((1, incomes), f32),
        pltpu.VMEM(block, jnp.int32),
        pltpu.VMEM(block, f32),
        pltpu.VMEM(block, f32),
        pltpu.VMEM(block, f32),
        pltpu.VMEM(block, jnp.int32),
        pltpu.VMEM(block, f32),
        pltpu.VMEM((durables * ill_rows, incomes), jnp.int32),
        pltpu.SMEM((ill_rows,), f32),
        pltpu.SMEM((durables,), f32),
        dma((8,)),
        bundles,
        bundles,
        bundles,
        bundles,
        pltpu.VMEM((durables, ill_rows + 1, TILE, liq_rows), f32),
        pltpu.VMEM((ill_n, ill_rows + 1, TILE, liq_rows), f32),
        pltpu.VMEM((ill_n, liq_n, 2 * ill_rows, part, liq_rows), f32),
        tiles(2 * ill_all * liq_n),
        tiles(ill_all * liq_n),
        slabs(ill_all * liq_n),
        slabs(ill_rows * liq_n),
        pltpu.VMEM((ill_n - 1, liq_n * ill_rows, part, liq_rows), f32),
        pltpu.VMEM((ill_n - 1, liq_n * ill_rows, part, liq_rows), f32),
        pltpu.VMEM((part * ill_all, liq_rows // 2, liq_n * liq_rows), jnp.bfloat16),
        pltpu.VMEM((4 * liq_n * ill_all * part, liq_rows), f32),
        tiles(liq_n * ill_all),
        tiles(liq_n * ill_all),
        slabs((durables + 1) * ill_rows),
    ] + [
        dma((n,)) for n in (1, 1, 1, 1, 1, 1, 1, 1, 1, 1, 2, 1, 1, 1, 1, 1, 1)
    ] + [pltpu.SemaphoreType.REGULAR]


def body(
    marginal_value,
    transition,
    discount_shock,
    illiquid_drift,
    durable_keep,
    bracket_index,
    bracket_weight,
    steady_consumption,
    lottery_weight,
    liquid_target,
    illiquid_target,
    population,
):
    shape = marginal_value.shape
    incomes, durables, ill_rows, liq_rows = shape
    liq_n, ill_n, dur_n = (lax.axis_size(name) for name in ("liq", "ill", "dur"))
    rows = incomes * durables * ill_rows
    flat = lambda x: x.reshape(rows, liq_rows)
    anywhere = pl.BlockSpec(memory_space=pl.ANY)
    f32 = jnp.float32
    block = (rows, liq_rows)
    dma = pltpu.SemaphoreType.DMA
    vmem = pl.BlockSpec(memory_space=pltpu.VMEM)
    held = pltpu.VMEM(block, f32)
    result = jax.ShapeDtypeStruct(block, f32)
    dims = (incomes, durables, ill_rows, liq_rows, liq_n, ill_n, dur_n)
    transposed = (
        ill_n == 2 and durables == ill_n and liq_n * 2 == TILE and incomes == liq_n * TILE and ill_rows < TILE
    )
    if transposed:
        step_kernel, scratch, name = transposed_kernel, transposed_scratch(dims), "transposed_window"
    else:
        step_kernel, scratch, name = kernel, window_scratch(dims), "window"
    outs = pl.pallas_call(
        functools.partial(step_kernel, dims),
        out_shape=(held, held),
        in_specs=[anywhere] * 12,
        out_specs=(vmem, vmem),
        scratch_shapes=scratch,
        compiler_params=pltpu.CompilerParams(collective_id=0, has_side_effects=True),
        name=name,
    )(
        flat(marginal_value),
        transition,
        discount_shock.reshape(1, incomes),
        illiquid_drift,
        durable_keep,
        flat(bracket_index),
        flat(bracket_weight),
        flat(steady_consumption),
        flat(lottery_weight),
        flat(liquid_target),
        jnp.transpose(illiquid_target, (1, 2, 0)).reshape(durables * ill_rows, incomes),
        flat(population),
    )
    outs = pl.pallas_call(
        store,
        out_shape=(result, result),
        in_specs=[vmem, vmem],
        out_specs=(anywhere, anywhere),
        scratch_shapes=[dma((2,))],
        name="store",
    )(*(pltpu.with_memory_space_constraint(out, pltpu.VMEM) for out in outs))
    return tuple(out.reshape(shape) for out in outs)


def solution(mesh):
    in_specs = (
        P(None, "dur", "ill", "liq"),
        P(),
        P(),
        P("ill"),
        P("dur"),
        P(None, "dur", "ill", "liq"),
        P(None, "dur", "ill", "liq"),
        P(None, "dur", "ill", "liq"),
        P(None, "dur", "ill", "liq"),
        P(None, "dur", "ill", "liq"),
        P(None, "dur", "ill"),
        P(None, "dur", "ill", "liq"),
    )
    out_specs = (P(None, "dur", "ill", "liq"), P(None, "dur", "ill", "liq"))
    return jax.shard_map(body, mesh=mesh, in_specs=in_specs, out_specs=out_specs, check_vma=False)
```
